32 devices in a mesh: grp: 2 (over x), seq: 16 (over z, y, core).
Axes of the slice: x: 2, y: 2, z: 4, core: 2. Of those that a mesh axis runs over, the one named last changes fastest.
Arguments:
- hidden_in: bfloat16 [8192, 768], P(('grp', 'seq')), parts along dimension 0, may hold values from -6 to 6
- w_in: bfloat16 [768, 1024], replicated, may hold values from -0.21875 to 0.21875
- w_dt: bfloat16 [768, 12], replicated, may hold values from -0.21875 to 0.21875
- dt_bias: float32 [12], replicated, may hold values from -7 to -2
- a_log: float32 [12], replicated, may hold values from -4 to 3
- conv_w: float32 [4, 1024], replicated, may hold values from -3 to 3
- d_skip: float32 [12], replicated, may hold values from 0.5 to 1.5
- norm_gain: float32 [768], replicated, may hold values from 0.5 to 1.5
- w_out: bfloat16 [768, 768], replicated, may hold values from -0.21875 to 0.21875
- w_cls: bfloat16 [768, 16], replicated, may hold values from -0.21875 to 0.21875
- teacher_rows: bfloat16 [4096, 4096], P(('grp', 'seq')), parts along dimension 0, may hold values from -1800 to 1800
- w_teacher: bfloat16 [4096, 16], replicated, may hold values from -0.09375 to 0.09375
- row_dest: int32 [4096, 1], P(('grp', 'seq')), parts along dimension 0, may hold values from 0 to 15; in each aligned block of 128 rows (0 to 127, 128 to 255, ...) at most 16 rows name the same one
- row_start: int32 [4096], P(('grp', 'seq')), parts along dimension 0, may hold values from 0 to 224
- row_len: int32 [4096], P(('grp', 'seq')), parts along dimension 0, may hold values from 1 to 32
Outputs:
- grad_hidden: bfloat16 [8192, 768], P(('grp', 'seq')), parts along dimension 0
- grad_w_in: float32 [1536, 1024], P(('grp', 'seq')), parts along dimension 0
- grad_w_out: float32 [1536, 768], P(('grp', 'seq')), parts along dimension 0
- grad_conv: float32 [8, 1024], P('grp'), parts along dimension 0
- grad_w_dt: float32 [1536, 12], P('grp'), parts along dimension 0
- grad_heads: float32 [6, 12], P('grp'), parts along dimension 0
- grad_norm_gain: float32 [1536], P('grp'), parts along dimension 0
- grad_w_cls: float32 [1536, 16], P('grp'), parts along dimension 0
- loss: float32 [2], P('grp'), parts along dimension 0
The draws below stay inside these ranges and needn't reach their ends.
There are 2 independent parts, one for each index of `grp`. The reference program is written for one: setup_inputs(seed, part) draws one part's arguments, and reference() takes and returns one part's arrays. A program takes and returns all parts, laid end to end along the dimension named above; an argument that names none is the same for every part. Nothing has to cross between parts.
Inputs may be any that keep to these rules, and one draw needn't show every extreme that they name: `row_dest`: within the rows of one device (aligned blocks of 128 rows), no destination is named by more than 16 rows, a bound that some block reaches.
All inputs are finite; a program needn't handle non-finite values.
Results may differ from the reference program's by a relative error of at most 0.014.
Values may be sent and summed in bfloat16 or wider, within the bound.
No kernel may reach another device: no remote copies, remote signals or barrier semaphores. Data moves between devices by JAX's collectives and lax.ppermute only.
A program may use at most 128 MiB of HBM per device.

```python
import math
import jax
import jax.numpy as jnp
import numpy as np
from jax import lax

D = 768
HEADS = 12
HDIM = 64
STATE = 128
KCONV = 4
TEACH = 4096
LABELS = 16
BLOCK = 64
MSG_MAX = 32
TOK_DEV = 256
ROWS_DEV = 128
INNER = 768
CONVW = 1024
SEQ = 4096
ROWS_TOTAL = 2048
CAP = 16
N_SEQ = 16


def draw_teacher_rows(key, part):
    first_key = jax.random.fold_in(key, 0)
    base = jnp.clip(jax.random.normal(first_key, (ROWS_TOTAL, TEACH), jnp.float32), -6.0, 6.0)
    return base.astype(jnp.bfloat16)


def with_ends(values, stream_key, least, top_value):
    longest = values.shape.index(max(values.shape))
    spots = []
    for shift in (0, 1):
        where = [jax.random.randint(jax.random.fold_in(stream_key, axis), (), 0, length) for axis, length in enumerate(values.shape)]
        where[longest] = (where[longest] + shift) % values.shape[longest]
        spots.append(tuple(where))
    return values.at[spots[0]].set(least).at[spots[1]].set(top_value)


def steps_of(own_key, extent, shards, smallest, largest):
    level, own = 1.0, jax.random.fold_in(own_key, 6)
    for dim, blocks in shards:
        steps = jnp.exp(jax.random.uniform(jax.random.fold_in(own, dim), (blocks,), jnp.float32, smallest / len(shards), largest / len(shards)))
        level = level * jnp.repeat(steps, extent[dim] // blocks).reshape([-1 if axis == dim else 1 for axis in range(len(extent))])
    return level


def deal_out(stream_key, own, number, rows, number_of, top, most, lean):
    sequence = jax.random.permutation(stream_key, number_of)
    packed, usual = shares(number_of, rows * top, most, lean, True), shares(number_of, rows * top, most, lean, False)
    places = jnp.arange(number_of)

    def named(tallies, rotation):
        used = int((tallies > 0).sum())
        fixed = max(1, used // 4)
        moved = fixed + (places - fixed + rotation * (used - fixed)) % max(1, number_of - fixed)
        return jnp.zeros((number_of,), jnp.int32).at[sequence[jnp.where(places < fixed, places, moved)]].set(jnp.asarray(tallies, jnp.int32))

    tallies = jnp.where(number % 4 == 0, named(packed, number // 4), named(usual, number - number // 4 - 1))
    mixed = jax.random.permutation(jax.random.fold_in(own, 3), number_of)
    donor, receiver = mixed[0:number_of // 2 * 2:2], mixed[1:number_of // 2 * 2:2]
    room = jnp.minimum(tallies[donor] - 1, most - tallies[receiver]) // 2
    room = jnp.where((donor == sequence[0]) | (receiver == sequence[0]) | (tallies[receiver] == 0), 0, jnp.maximum(room, 0))
    moved = jax.random.randint(jax.random.fold_in(own, 4), (number_of // 2,), 0, 1 << 20) % (room + 1)
    tallies = tallies.at[donor].add(-moved).at[receiver].add(moved)
    members = jnp.searchsorted(jnp.cumsum(tallies), jnp.arange(rows * top), side="right").astype(jnp.int32)
    table = members.reshape(top, rows).T
    table = table[jax.random.permutation(jax.random.fold_in(own, 1), rows)]
    rotation = jax.random.randint(jax.random.fold_in(own, 2), (rows, 1), 0, top)
    return jnp.take_along_axis(table, (jnp.arange(top)[None, :] + rotation) % top, axis=1)


def shares(count, total, reach, lean, full):
    weights = [(1 << 20) // math.isqrt(standing ** lean) + 1 for standing in range(1, count + 1)]
    largest = reach if full else min(reach, max(-(-total // count), total * weights[0] // sum(weights)))
    least = 1 if total - largest >= count - 1 else 0
    given, spare = [largest] + [least] * (count - 1), total - largest - least * (count - 1)
    while spare > 0:
        free = [i for i in range(1, count) if given[i] < largest] or [i for i in range(1, count) if given[i] < reach]
        whole, remaining = sum([weights[i] for i in free]), spare
        for i in free:
            more = min(reach - given[i], max(1, remaining * weights[i] // whole), spare)
            given[i] = given[i] + more
            spare = spare - more
    return np.array(given)


def centred(stream_key, shape, deviation, bound, cuts=(), kind=jnp.bfloat16):
    values = jax.random.normal(stream_key, shape, jnp.float32) * deviation
    if len(cuts) > 0:
        values = steps_of(stream_key, shape, cuts, -0.22, 0.18) * values
    return jnp.clip(values, min=-bound, max=bound).astype(kind)


def setup_inputs(seed: int = 0, part: int = 0) -> dict:
    streams_of = jax.random.split(jax.random.key(seed), 16)
    own_keys = jax.random.split(jax.random.fold_in(streams_of[15], part), 16)
    hidden_in = centred(own_keys[0], (SEQ, D), 1.0, 6.0, ((0, 16),))
    w_in = centred(streams_of[1], (D, CONVW), D ** -0.5, 0.21875)
    w_dt = centred(streams_of[2], (D, HEADS), D ** -0.5, 0.21875)
    dt_bias = jnp.clip(jax.random.uniform(streams_of[3], (HEADS,), jnp.float32, -7.0, -2.0), -7.0, -2.0)
    a_log = jnp.clip(jax.random.uniform(streams_of[4], (HEADS,), jnp.float32, -4.0, 3.0), -4.0, 3.0)
    conv_w = centred(streams_of[5], (KCONV, CONVW), KCONV ** -0.5, 3.0, (), jnp.float32)
    d_skip = jnp.clip(jax.random.uniform(streams_of[6], (HEADS,), jnp.float32, 0.5, 1.5), 0.5, 1.5)
    norm_gain = jnp.clip(1.0 + 0.1 * jax.random.normal(streams_of[7], (INNER,), jnp.float32), 0.5, 1.5)
    w_out = centred(streams_of[8], (INNER, D), INNER ** -0.5, 0.21875)
    w_cls = centred(streams_of[9], (D, LABELS), D ** -0.5, 0.21875)
    teacher_rows = draw_teacher_rows(jax.random.fold_in(jax.random.fold_in(streams_of[15], part), 71), part)
    w_teacher = centred(streams_of[11], (TEACH, LABELS), TEACH ** -0.5, 0.09375)
    row_dest_keys = jax.random.split(jax.random.fold_in(own_keys[12], 1), ROWS_TOTAL // ROWS_DEV)
    row_dest_turns = jax.random.permutation(jax.random.fold_in(own_keys[12], 3), ROWS_TOTAL // ROWS_DEV)
    row_dest = jax.vmap(lambda own, number: deal_out(jax.random.fold_in(own_keys[12], 2), own, number, ROWS_DEV, N_SEQ, 1, CAP, 2))(row_dest_keys, row_dest_turns).reshape((ROWS_TOTAL, 1))
    row_start = with_ends(jax.random.randint(own_keys[13], (ROWS_TOTAL,), 0, TOK_DEV - MSG_MAX + 1), jax.random.fold_in(own_keys[13], 1), 0, TOK_DEV - MSG_MAX).astype(jnp.int32)
    row_len = with_ends(jax.random.randint(own_keys[14], (ROWS_TOTAL,), 1, MSG_MAX + 1), jax.random.fold_in(own_keys[14], 1), 1, MSG_MAX).astype(jnp.int32)
    return {"hidden_in": hidden_in, "w_in": w_in, "w_dt": w_dt, "dt_bias": dt_bias, "a_log": a_log, "conv_w": conv_w, "d_skip": d_skip, "norm_gain": norm_gain, "w_out": w_out, "w_cls": w_cls, "teacher_rows": teacher_rows, "w_teacher": w_teacher, "row_dest": row_dest, "row_start": row_start, "row_len": row_len}


PRECISE = lax.Precision.HIGHEST
EPSILON = 1e-05
CONTRACT_ROWS = (((0,), (0,)), ((), ()))

def block_step(carry_state, pieces):
    values, in_map, out_map, step_size, log_decay = pieces
    running = jnp.cumsum(log_decay, axis=0)
    block_width = log_decay.shape[0]
    causal = jnp.arange(block_width)[:, None] >= jnp.arange(block_width)[None, :]
    spread = running.T[:, :, None] - running.T[:, None, :]
    decay_mix = jnp.exp(jnp.where(causal[None, :, :], spread, -jnp.inf))
    scores = jnp.dot(out_map, in_map.T, precision=PRECISE)
    weighted = values * step_size[:, :, None]
    within = jnp.einsum('hts,shp->thp', decay_mix * scores[None, :, :], weighted, precision=PRECISE)
    carried = jnp.einsum('tn,hnp->thp', out_map, carry_state, precision=PRECISE) * jnp.exp(running)[:, :, None]
    tail_decay = jnp.exp(running[-1][None, :] - running)
    fresh_state = jnp.einsum('sn,shp->hnp', in_map, weighted * tail_decay[:, :, None], precision=PRECISE)
    carry_state = carry_state * jnp.exp(running[-1])[:, None, None] + fresh_state
    return (carry_state, within + carried)

def unpack(mixed_f, raw_step, dt_bias, a_log):
    inner_width = HEADS * HDIM
    values = mixed_f[:, :inner_width].reshape(mixed_f.shape[0], HEADS, HDIM)
    in_map = mixed_f[:, inner_width:inner_width + STATE]
    out_map = mixed_f[:, inner_width + STATE:]
    step_size = jax.nn.softplus(raw_step + dt_bias)
    log_decay = -step_size * jnp.exp(a_log)
    return (values, in_map, out_map, step_size, log_decay)

def full_branch(mixed_f, raw_step, dt_bias, a_log, d_skip, norm_gain, start_state):
    values, in_map, out_map, step_size, log_decay = unpack(mixed_f, raw_step, dt_bias, a_log)
    block_count = values.shape[0] // BLOCK
    pieces = tuple((piece.reshape((block_count, BLOCK) + piece.shape[1:]) for piece in (values, in_map, out_map, step_size, log_decay)))
    _, outputs = lax.scan(block_step, start_state, pieces)
    scanned = outputs.reshape(values.shape) + d_skip[None, :, None] * values
    flat = scanned.reshape(values.shape[0], HEADS * HDIM)
    mean_square = lax.optimization_barrier(jnp.mean(flat * flat, axis=1, keepdims=True))
    return flat * lax.rsqrt(mean_square + EPSILON) * norm_gain

def reference(hidden_in, w_in, w_dt, dt_bias, a_log, conv_w, d_skip, norm_gain, w_out, w_cls, teacher_rows, w_teacher, row_dest, row_start, row_len):
    taps = conv_w.shape[0]
    flipped = hidden_in[::-1]
    length = flipped.shape[0]
    raw = jnp.dot(flipped, w_in, preferred_element_type=jnp.float32).astype(jnp.bfloat16)
    raw_step = jnp.dot(flipped, w_dt, preferred_element_type=jnp.float32)
    padded = jnp.concatenate([jnp.zeros((taps - 1, raw.shape[1]), raw.dtype), raw], axis=0)
    conv_sum = jnp.zeros(raw.shape, jnp.float32)
    for tap_index in range(taps):
        conv_sum = conv_sum + conv_w[tap_index] * padded[taps - 1 - tap_index:taps - 1 - tap_index + length]
    mixed = jax.nn.silu(conv_sum).astype(jnp.bfloat16)
    zero_state = jnp.zeros((HEADS, STATE, HDIM), jnp.float32)
    normed_f, pull_full = jax.vjp(full_branch, mixed.astype(jnp.float32), raw_step, dt_bias, a_log, d_skip, norm_gain, zero_state)
    normed = normed_f.astype(jnp.bfloat16)
    branch = jnp.dot(normed, w_out, preferred_element_type=jnp.float32).astype(jnp.bfloat16)
    student_logp = jax.nn.log_softmax(jnp.dot(branch, w_cls, preferred_element_type=jnp.float32), axis=-1)
    teacher_logp = jax.nn.log_softmax(jnp.dot(teacher_rows, w_teacher, preferred_element_type=jnp.float32), axis=-1)
    teacher_prob = jnp.exp(teacher_logp)
    target_dev = row_dest[:, 0]
    span_end = row_start + row_len
    positions = jnp.arange(TOK_DEV, dtype=jnp.int32)

    def one_device(device):
        covered = ((target_dev[:, None] == device) & (positions[None, :] >= row_start[:, None]) & (positions[None, :] < span_end[:, None])).astype(jnp.float32)
        return (lax.dot_general(covered, teacher_prob, CONTRACT_ROWS, precision=PRECISE), lax.optimization_barrier(jnp.sum(covered, axis=0)))
    targets, counts = lax.map(one_device, jnp.arange(N_SEQ, dtype=jnp.int32))
    target = targets.reshape(length, LABELS)[::-1]
    cover_count = counts.reshape(length)[::-1]
    own_term = jnp.sum(row_len.astype(jnp.float32) * lax.optimization_barrier(jnp.sum(teacher_prob * teacher_logp, axis=1)))
    total = own_term - jnp.sum(target * student_logp)
    back_logits = cover_count[:, None] * jnp.exp(student_logp) - target
    grad_w_cls = lax.dot_general(branch.astype(jnp.float32), back_logits, CONTRACT_ROWS, precision=PRECISE)
    back_branch = jnp.dot(back_logits, w_cls.astype(jnp.float32).T, precision=PRECISE).astype(jnp.bfloat16)
    grad_w_out = lax.dot_general(normed, back_branch, CONTRACT_ROWS, preferred_element_type=jnp.float32)
    back_normed = jnp.dot(back_branch, w_out.T, preferred_element_type=jnp.float32)
    back_mixed, back_step, back_bias, back_alog, back_skip, grad_norm_gain, _ = pull_full(back_normed)
    sigmoid_part = jax.nn.sigmoid(conv_sum)
    back_conv = back_mixed * sigmoid_part * (1.0 + conv_sum * (1.0 - sigmoid_part))
    extended = jnp.concatenate([back_conv, jnp.zeros((taps - 1, back_conv.shape[1]), jnp.float32)], axis=0)
    back_raw_f = jnp.zeros(back_conv.shape, jnp.float32)
    conv_rows = []
    for tap_index in range(taps):
        back_raw_f = back_raw_f + conv_w[tap_index] * extended[tap_index:tap_index + length]
        conv_rows.append(lax.optimization_barrier(jnp.sum(back_conv * padded[taps - 1 - tap_index:taps - 1 - tap_index + length], axis=0)))
    back_raw = back_raw_f.astype(jnp.bfloat16)
    back_step_b = back_step.astype(jnp.bfloat16)
    grad_conv = jnp.stack(conv_rows)
    grad_w_in = lax.dot_general(flipped, back_raw, CONTRACT_ROWS, preferred_element_type=jnp.float32)
    grad_w_dt = lax.dot_general(flipped, back_step_b, CONTRACT_ROWS, preferred_element_type=jnp.float32)
    grad_flip = jnp.dot(back_raw, w_in.T, preferred_element_type=jnp.float32) + jnp.dot(back_step_b, w_dt.T, preferred_element_type=jnp.float32)
    grad_hidden = grad_flip.astype(jnp.bfloat16)[::-1]
    grad_heads = jnp.stack([back_bias, back_alog, back_skip])
    loss = (total / (ROWS_DEV * N_SEQ)).reshape(1)
    return (grad_hidden, grad_w_in, grad_w_out, grad_conv, grad_w_dt, grad_heads, grad_norm_gain, grad_w_cls, loss)
```

```python
import functools

import jax
import jax.numpy as jnp
from jax import lax
from jax.experimental import pallas as pl
from jax.experimental.pallas import tpu as pltpu
from jax.sharding import PartitionSpec as P

HEADS = 12
HDIM = 64
STATE = 128
LABELS = 16
LANES = 128
HALO = 8
META = 8
EPSILON = 1e-05
FAR = -1e30

F32 = jnp.float32
BF16 = jnp.bfloat16


def partner(x, axis, apart):
    return lax.ppermute(x, axis, [(i, i ^ 1 << apart) for i in range(lax.axis_size(axis))])


def passed_along(x, axis, by):
    length = lax.axis_size(axis)
    pairs = [(i, i + by) for i in range(length) if 0 <= i + by < length]
    return lax.ppermute(x, axis, pairs)


def dot(a, b, left=1, right=0):
    return lax.dot_general(a, b, (((left,), (right,)), ((), ())), preferred_element_type=F32)


def pieces(x, count):
    parts = []
    for _ in range(count):
        part = x.astype(BF16)
        parts.append(part)
        x = x - part.astype(F32)
    return parts


def finer(a, x, count, left=1, right=0):
    return sum(dot(a, part, left, right) for part in pieces(x, count))


def iota(shape, axis):
    return lax.broadcasted_iota(jnp.int32, shape, axis)


def spread_heads(x):
    rows = x.shape[0]
    first = iota((rows, LANES), 1) < HDIM
    return jnp.concatenate(
        [
            jnp.where(
                first,
                jnp.broadcast_to(x[:, 2 * pair : 2 * pair + 1], (rows, LANES)),
                jnp.broadcast_to(x[:, 2 * pair + 1 : 2 * pair + 2], (rows, LANES)),
            )
            for pair in range(HEADS // 2)
        ],
        axis=1,
    )


def head_sums(x):
    width = x.shape[1]
    member = (iota((width, LANES), 0) // HDIM == iota((width, LANES), 1)).astype(BF16)
    return sum(dot(part, member) for part in pieces(x, 2))


def call(body, outs, *args, scratch=(), scalars=0):
    in_specs = [
        pl.BlockSpec(memory_space=pltpu.SMEM if i < scalars else pltpu.VMEM)
        for i in range(len(args))
    ]
    return pl.pallas_call(
        body,
        out_shape=[jax.ShapeDtypeStruct(shape, dtype) for shape, dtype in outs],
        in_specs=in_specs,
        out_specs=[pl.BlockSpec(memory_space=pltpu.VMEM)] * len(outs),
        scratch_shapes=list(scratch),
        compiler_params=pltpu.CompilerParams(vmem_limit_bytes=40 * 1024 * 1024),
    )(*args)


def teacher_kernel(rows, weights, meta, packed, own):
    logits = dot(rows[...], weights[...])
    top = jnp.max(logits, axis=1, keepdims=True)
    shifted = logits - top
    logp = shifted - jnp.log(jnp.sum(jnp.exp(shifted), axis=1, keepdims=True))
    count = logits.shape[0]
    same = (iota((count, count), 0) == iota((count, count), 1)).astype(BF16)
    logp_t = sum(dot(part, same, 0, 0) for part in pieces(logp, 3))
    prob_t = jnp.exp(logp_t)
    packed[0:LABELS, :] = prob_t
    packed[LABELS:, :] = meta[...]
    own[...] = jnp.sum(prob_t * logp_t, axis=0, keepdims=True) * meta[2:3, :]


def target_kernel(place, packed, target):
    length = target.shape[0]
    height = LABELS + META
    count = packed.shape[1]
    me = place[0].astype(F32)
    position = iota((length, count), 0).astype(F32)
    total = jnp.zeros((length, LANES), F32)
    fill = jnp.zeros((LANES - 2 * LABELS, count), F32)
    ones = jnp.ones((LABELS, count), F32)
    for source in range(packed.shape[0] // height):
        base = source * height
        prob = packed[base : base + LABELS, :]
        meta = packed[base + LABELS : base + height, :]
        start = jnp.where(meta[0:1, :] == me, meta[1:2, :], FAR)
        stop = start + meta[2:3, :]
        covered = ((position >= start) & (position < stop)).astype(F32).astype(BF16)
        total = total + finer(covered, jnp.concatenate([prob, ones, fill], axis=0), 2, 1, 1)
    target[...] = total


def front_kernel(
    hidden, edge, w_in, w_dt, heads, conv_w, message, mixed_o, conv_o, raw_o, step_o, run_o, run_t
):
    length = hidden.shape[0]
    taps = conv_w.shape[0]
    weights = w_in[...]
    raw_o[0:length, :] = dot(hidden[...], weights).astype(BF16).astype(F32)
    raw_o[length:, :] = dot(edge[...], weights).astype(BF16).astype(F32)
    before = dot(hidden[...], w_dt[...]) + heads[0:1, :]
    step = jnp.maximum(before, 0.0) + jnp.log1p(jnp.exp(-jnp.abs(before)))
    step = jnp.where(iota((length, LANES), 1) < HEADS, step, 0.0)
    log_decay = -step * jnp.exp(heads[1:2, :])
    later = (iota((length, length), 1) >= iota((length, length), 0)).astype(BF16)
    run = finer(later, log_decay, 3)
    step_o[:, 0:LANES] = step
    step_o[:, LANES:] = before
    run_o[...] = run
    run_t[...] = run.T
    conv = conv_w[0:1, :] * raw_o[0:length, :]
    for tap in range(1, taps):
        conv = conv + conv_w[tap : tap + 1, :] * raw_o[pl.ds(tap, length), :]
    conv_o[...] = conv
    mixed = (conv / (1.0 + jnp.exp(-conv))).astype(BF16)
    mixed_o[...] = mixed
    width = HEADS * HDIM
    total = run[0:1, :]
    weighted = mixed[:, :width].astype(F32) * spread_heads(step * jnp.exp(total - run))
    state = dot(mixed[:, width : width + STATE], weighted.astype(BF16), 0, 0)
    message[:, :width] = state.astype(BF16)
    high, middle, low = (part.astype(F32) for part in pieces(total, 3))
    tags = high + pltpu.roll(middle, 16, 1) + pltpu.roll(low, 32, 1)
    message[:, width:] = jnp.broadcast_to(tags, (STATE, LANES)).astype(BF16)


def decay_blocks(run, run_t, head, half):
    top = run[0:half, head : head + 1] - run_t[head : head + 1, :]
    low = run[half:, head : head + 1] - run_t[head : head + 1, half:]
    top_seen = iota(top.shape, 1) >= iota(top.shape, 0)
    low_seen = iota(low.shape, 1) >= iota(low.shape, 0)
    return jnp.exp(jnp.where(top_seen, top, FAR)), jnp.exp(jnp.where(low_seen, low, FAR))


def local_kernel(mixed, step, run, run_t, local):
    length = mixed.shape[0]
    half = length // 2
    width = HEADS * HDIM
    in_map = mixed[:, width : width + STATE]
    out_map = mixed[:, width + STATE :]
    top_scores = dot(out_map[0:half], in_map, 1, 1)
    low_scores = dot(out_map[half:], in_map[half:], 1, 1)
    weighted = (mixed[:, :width].astype(F32) * spread_heads(step[:, 0:LANES])).astype(BF16)
    first = iota((half, LANES), 1) < HDIM
    for pair in range(HEADS // 2):
        lanes = slice(pair * LANES, (pair + 1) * LANES)
        own = weighted[:, lanes]
        tops, lows = [], []
        for head in (2 * pair, 2 * pair + 1):
            top, low = decay_blocks(run, run_t, head, half)
            tops.append(dot((top * top_scores).astype(BF16), own))
            lows.append(dot((low * low_scores).astype(BF16), own[half:]))
        local[0:half, lanes] = jnp.where(first, tops[0], tops[1])
        local[half:, lanes] = jnp.where(first, lows[0], lows[1])


def states_kernel(arrived, onward, decay):
    count = arrived.shape[0]
    width = HEADS * HDIM
    rows = arrived.shape[1]
    keep = iota((rows, LANES), 1) < HEADS
    state = jnp.zeros((rows, width), F32)
    for source in range(count - 1, -1, -1):
        onward[source] = state.astype(BF16)
        tags = arrived[source, :, width:].astype(F32)
        total = tags + pltpu.roll(tags, LANES - 16, 1) + pltpu.roll(tags, LANES - 32, 1)
        factor = spread_heads(jnp.exp(jnp.where(keep, total, 0.0)))
        decay[source] = factor
        state = arrived[source, :, :width].astype(F32) + factor * state


def state_grads_kernel(arrived, decay, onward):
    count = arrived.shape[0]
    state = jnp.zeros(arrived.shape[1:], F32)
    for source in range(count):
        onward[source] = state.astype(BF16)
        state = arrived[source].astype(F32) + decay[source] * state


def middle_kernel(
    local, mixed, run, state, wide, w_out, w_cls, target,
    back_state, grad_scanned, scaled_o, normed_o, branch_o, back_branch_o, logits_o, run_grad, small,
):
    length = mixed.shape[0]
    width = HEADS * HDIM
    values = mixed[:, :width].astype(F32)
    out_map = mixed[:, width + STATE :]
    reach = spread_heads(jnp.exp(run[...]))
    carried = dot(out_map, state[...]) * reach
    gain = wide[0:1, :]
    skip = wide[1:2, :]
    scanned = local[...] + carried + skip * values
    scale = lax.rsqrt(jnp.mean(scanned * scanned, axis=1, keepdims=True) + EPSILON)
    plain = scanned * scale
    normed = (plain * gain).astype(BF16)
    normed_o[...] = normed
    branch = dot(normed, w_out[...]).astype(BF16)
    branch_o[...] = branch
    label = iota((length, LANES), 1) < LABELS
    logits = jnp.where(label, dot(branch, w_cls[...]), FAR)
    shifted = logits - jnp.max(logits, axis=1, keepdims=True)
    raised = jnp.exp(shifted)
    whole = jnp.sum(raised, axis=1, keepdims=True)
    logp = shifted - jnp.log(whole)
    wanted = target[...]
    cover = wanted[:, LABELS : LABELS + 1]
    back_logits = jnp.where(label, cover * (raised / whole) - wanted, 0.0)
    logits_o[...] = back_logits
    lost = jnp.sum(jnp.where(label, wanted * logp, 0.0), axis=0, keepdims=True)
    back_branch = sum(dot(part, w_cls[...], 1, 1) for part in pieces(back_logits, 2)).astype(BF16)
    back_branch_o[...] = back_branch
    back_normed = dot(back_branch, w_out[...], 1, 1)
    back_plain = back_normed * gain
    along = jnp.mean(back_plain * plain, axis=1, keepdims=True)
    back = scale * (back_plain - plain * along)
    grad_scanned[...] = back
    scaled = (back * reach).astype(BF16)
    scaled_o[...] = scaled
    back_state[...] = dot(out_map, scaled, 0, 0).astype(BF16)
    run_grad[...] = head_sums(back * carried)
    small[0:1, :] = jnp.sum(back_normed * plain, axis=0, keepdims=True)
    small[1:2, :] = jnp.sum(back * values, axis=0, keepdims=True)
    small[2:3, :] = jnp.zeros((1, width), F32)
    small[2:3, 0:LANES] = lost
    small[3:, :] = jnp.zeros((5, width), F32)


def halves(full, keep, send, odd, blocks):
    size = full.shape[0] // blocks
    for side in (0, 1):

        @pl.when(odd == side)
        def _():
            for block in range(blocks // 2):
                at = slice(block * size, (block + 1) * size)
                mine = (2 * block + side) * size
                other = (2 * block + 1 - side) * size
                keep[at, :] = full[mine : mine + size, :]
                send[at, :] = full[other : other + size, :].astype(BF16)


def outward_kernel(blocks, place, normed, back_branch, branch, back_logits, keep, send, cls, full):
    full[...] = dot(normed[...], back_branch[...], 0, 0)
    halves(full, keep, send, place[0] % 2, blocks)
    parts = pieces(back_logits[...], 2)
    cls[...] = sum(dot(part, branch[...], 0, 0) for part in parts)[0:LABELS]


def local_back_kernel(
    mixed, step, run, run_t, grad_scanned, scaled, state, carried_grad, weighted_grad, maps, run_grad
):
    length = mixed.shape[0]
    half = length // 2
    width = HEADS * HDIM
    in_map = mixed[:, width : width + STATE]
    out_map = mixed[:, width + STATE :]
    top_scores = dot(out_map[0:half], in_map, 1, 1)
    low_scores = dot(out_map[half:], in_map[half:], 1, 1)
    weighted = (mixed[:, :width].astype(F32) * spread_heads(step[:, 0:LANES])).astype(BF16)
    lane = iota((length, LANES), 1)
    back_top = jnp.zeros((half, length), F32)
    back_low = jnp.zeros((half, half), F32)
    rows_top = jnp.zeros((half, LANES), F32)
    rows_low = jnp.zeros((half, LANES), F32)
    columns = jnp.zeros((length, LANES), F32)
    columns_low = jnp.zeros((half, LANES), F32)
    for pair in range(HEADS // 2):
        lanes = slice(pair * LANES, (pair + 1) * LANES)
        own = weighted[:, lanes]
        back_f = grad_scanned[:, lanes]
        back = back_f.astype(BF16)
        tops, lows = [], []
        for side in (0, 1):
            head = 2 * pair + side
            top, low = decay_blocks(run, run_t, head, half)
            mine = jnp.where((lane >= HDIM) == (side == 1), back_f, 0.0).astype(BF16)
            mix_top = (top * top_scores).astype(BF16)
            mix_low = (low * low_scores).astype(BF16)
            tops.append(dot(mix_top, back[0:half], 0, 0))
            lows.append(dot(mix_low, back[half:], 0, 0))
            grad_top = top * dot(mine[0:half], own, 1, 1)
            grad_low = low * dot(mine[half:], own[half:], 1, 1)
            back_top = back_top + grad_top
            back_low = back_low + grad_low
            part_top = (grad_top * top_scores).astype(BF16)
            part_low = (grad_low * low_scores).astype(BF16)
            marker = (lane == head).astype(F32).astype(BF16)
            rows_top = rows_top + dot(part_top, marker)
            rows_low = rows_low + dot(part_low, marker[half:])
            columns = columns + dot(part_top, marker[0:half], 0, 0)
            columns_low = columns_low + dot(part_low, marker[half:], 0, 0)
        weighted_grad[0:half, lanes] = jnp.where(lane[0:half] < HDIM, tops[0][0:half], tops[1][0:half])
        weighted_grad[half:, lanes] = jnp.where(
            lane[half:] < HDIM, tops[0][half:] + lows[0], tops[1][half:] + lows[1]
        )
    back_top = back_top.astype(BF16)
    back_low = back_low.astype(BF16)
    from_state = dot(scaled[...], state[...], 1, 1)
    maps[0:half, STATE:] = dot(back_top, in_map) + from_state[0:half]
    maps[half:, STATE:] = dot(back_low, in_map[half:]) + from_state[half:]
    in_grad = dot(back_top, out_map[0:half], 0, 0)
    maps[0:half, 0:STATE] = in_grad[0:half]
    maps[half:, 0:STATE] = in_grad[half:] + dot(back_low, out_map[half:], 0, 0)
    run_grad[0:half, :] = carried_grad[0:half, :] + rows_top - columns[0:half]
    run_grad[half:, :] = carried_grad[half:, :] + rows_low - columns[half:] - columns_low


def last_kernel(
    blocks, place, hidden, edge, mixed, conv, raw, step, run, state, state_grad, weighted_grad, maps,
    run_grad, grad_scanned, heads, wide, conv_w, small, cls, own,
    keep, send, rim, back_raw_o, step_grad_o, conv_sums, sums, full, padded,
):
    length = mixed.shape[0]
    taps = conv_w.shape[0]
    width = HEADS * HDIM
    values = mixed[:, :width].astype(F32)
    in_map = mixed[:, width : width + STATE]
    total = run[0:1, :]
    tail = spread_heads(jnp.exp(total - run[...]))
    steps = spread_heads(step[:, 0:LANES])
    incoming = state_grad[...]
    reached = dot(in_map, incoming) * tail
    weighted = values * steps
    ended = head_sums(reached * weighted)
    in_grad = maps[:, 0:STATE] + dot((weighted * tail).astype(BF16), incoming, 1, 1)
    weighted_all = weighted_grad[...] + reached
    product = jnp.sum(incoming.astype(F32) * state[...].astype(F32), axis=0, keepdims=True)
    total_grad = jnp.exp(total) * head_sums(jnp.broadcast_to(product, (8, width)))[0:1]
    row, column = iota((length, length), 0), iota((length, length), 1)
    decay_grad = (
        finer((column <= row).astype(BF16), run_grad[...], 3)
        + finer((column > row).astype(BF16), ended, 3)
        + total_grad
    )
    rate = jnp.exp(heads[1:2, :])
    step_grad = head_sums(weighted_all * values) - rate * decay_grad
    before = step[:, LANES:]
    step_grad = jnp.where(
        iota((length, LANES), 1) < HEADS, step_grad / (1.0 + jnp.exp(-before)), 0.0
    )
    step_grad_b = step_grad.astype(BF16)
    step_grad_o[...] = step_grad_b
    values_grad = weighted_all * steps + wide[1:2, :] * grad_scanned[...]
    padded[0:HALO, :] = jnp.zeros((HALO, padded.shape[1]), F32)
    padded[HALO + length :, :] = jnp.zeros((HALO, padded.shape[1]), F32)

    def through(mixed_grad, lanes):
        inner = conv[:, lanes]
        gate = 1.0 / (1.0 + jnp.exp(-inner))
        padded[HALO : HALO + length, lanes] = mixed_grad * gate * (1.0 + inner * (1.0 - gate))

    through(values_grad, slice(0, width))
    through(in_grad, slice(width, width + STATE))
    through(maps[:, STATE:], slice(width + STATE, width + 2 * STATE))
    back_conv = padded[HALO : HALO + length, :]
    rim[...] = padded[length : length + HALO, :]
    back_raw = jnp.zeros((length + HALO, padded.shape[1]), F32)
    for tap in range(taps):
        conv_sums[tap : tap + 1, :] = jnp.sum(
            back_conv * raw[pl.ds(tap, length), :], axis=0, keepdims=True
        )
        back_raw = back_raw + conv_w[tap : tap + 1, :] * padded[pl.ds(HALO - tap, length + HALO), :]
    back_raw_o[...] = back_raw[0:length]
    full[...] = dot(hidden[...], back_raw[0:length].astype(BF16), 0, 0) + dot(
        edge[...], back_raw[length:].astype(BF16), 0, 0
    )
    halves(full, keep, send, place[0] % 2, blocks)
    dt_grad = dot(step_grad_b, hidden[...], 0, 0)
    sums[0:LABELS, :] = dt_grad[0:LABELS]
    sums[LABELS : 2 * LABELS, :] = cls[...]
    base = 2 * LABELS
    sums[base:, :] = jnp.zeros((8, width), F32)
    sums[base : base + 1, :] = small[0:1, :]
    sums[base + 1 : base + 2, 0:LANES] = jnp.sum(step_grad, axis=0, keepdims=True)
    log_decay = -step[:, 0:LANES] * rate
    sums[base + 2 : base + 3, 0:LANES] = jnp.sum(decay_grad * log_decay, axis=0, keepdims=True)
    sums[base + 3 : base + 4, 0:LANES] = head_sums(jnp.broadcast_to(small[1:2, :], (8, width)))[0:1]
    sums[base + 4 : base + 5, 0:LANES] = own[...] - small[2:3, 0:LANES]


def hidden_kernel(back_raw, rim, step_grad, w_in, w_dt, conv_w, out, joined, edge):
    taps = conv_w.shape[0]
    joined[...] = back_raw[...]
    edge[0:HALO, :] = rim[...]
    edge[HALO:, :] = jnp.zeros((HALO, edge.shape[1]), F32)
    head = joined[0:HALO, :]
    for tap in range(taps):
        head = head + conv_w[tap : tap + 1, :] * edge[pl.ds(HALO - tap, HALO), :]
    joined[0:HALO, :] = head
    out[...] = (
        dot(joined[...].astype(BF16), w_in[...], 1, 1) + dot(step_grad[...], w_dt[...], 1, 1)
    ).astype(BF16)


def swapped(x, axis="seq"):
    return lax.all_to_all(x, axis, split_axis=0, concat_axis=0, tiled=True)


def scattered(keep, send, devices):
    both = keep + partner(send, "seq", 0).astype(F32)
    groups = [[i for i in range(devices) if i % 2 == side] for side in (0, 1)]
    parts = lax.all_to_all(
        both.astype(BF16), "seq", split_axis=0, concat_axis=0, axis_index_groups=groups, tiled=True
    )
    size = keep.shape[0] // (devices // 2)
    return jnp.sum(parts.reshape(devices // 2, size, keep.shape[1]).astype(F32), axis=0)


def per_device(
    hidden_in, w_in, w_dt, dt_bias, a_log, conv_w, d_skip, norm_gain, w_out, w_cls,
    teacher_rows, w_teacher, row_dest, row_start, row_len,
):
    devices = lax.axis_size("seq")
    length = hidden_in.shape[0]
    width = HEADS * HDIM
    channels = w_in.shape[1]
    slice_rows = STATE // devices
    row_count = teacher_rows.shape[0]
    place = lax.axis_index("seq").astype(jnp.int32).reshape(1)

    edge = passed_along(hidden_in[:HALO], "seq", -1)
    meta = jnp.concatenate(
        [
            row_dest.reshape(1, row_count),
            row_start.reshape(1, row_count),
            row_len.reshape(1, row_count),
            jnp.zeros((META - 3, row_count), jnp.int32),
        ],
        axis=0,
    ).astype(F32)
    packed, own = call(
        teacher_kernel,
        [((LABELS + META, row_count), F32), ((1, row_count), F32)],
        teacher_rows, w_teacher, meta,
    )
    everyone = lax.all_gather(packed, "seq", axis=0, tiled=True)

    w_dt_wide = jnp.pad(w_dt, ((0, 0), (0, LANES - HEADS)))
    w_cls_wide = jnp.pad(w_cls, ((0, 0), (0, LANES - LABELS)))
    heads = jnp.pad(jnp.stack([dt_bias, a_log]), ((0, 6), (0, LANES - HEADS)))
    wide = jnp.pad(jnp.stack([norm_gain, jnp.repeat(d_skip, HDIM)]), ((0, 6), (0, 0)))

    message, mixed, conv, raw, step, run, run_t = call(
        front_kernel,
        [
            ((STATE, width + LANES), BF16),
            ((length, channels), BF16),
            ((length, channels), F32),
            ((length + HALO, channels), F32),
            ((length, 2 * LANES), F32),
            ((length, LANES), F32),
            ((LANES, length), F32),
        ],
        hidden_in, edge, w_in, w_dt_wide, heads, conv_w,
    )
    arrived = swapped(message).reshape(devices, slice_rows, width + LANES)
    (local,) = call(local_kernel, [((length, width), F32)], mixed, step, run, run_t)
    onward, decay = call(
        states_kernel,
        [((devices, slice_rows, width), BF16), ((devices, slice_rows, width), F32)],
        arrived,
    )
    state = swapped(onward.reshape(STATE, width))
    (target,) = call(target_kernel, [((length, LANES), F32)], place, everyone, scalars=1)

    (
        back_state, grad_scanned, scaled, normed, branch, back_branch, back_logits, carried_grad, small,
    ) = call(
        middle_kernel,
        [
            ((STATE, width), BF16),
            ((length, width), F32),
            ((length, width), BF16),
            ((length, width), BF16),
            ((length, width), BF16),
            ((length, width), BF16),
            ((length, LANES), F32),
            ((length, LANES), F32),
            ((8, width), F32),
        ],
        local, mixed, run, state, wide, w_out, w_cls_wide, target,
    )
    back_arrived = swapped(back_state).reshape(devices, slice_rows, width)
    keep_out, send_out, cls = call(
        functools.partial(outward_kernel, devices),
        [((width // 2, width), F32), ((width // 2, width), BF16), ((LABELS, width), F32)],
        place, normed, back_branch, branch, back_logits,
        scratch=[pltpu.VMEM((width, width), F32)], scalars=1,
    )
    weighted_grad, maps, run_grad = call(
        local_back_kernel,
        [((length, width), F32), ((length, 2 * STATE), F32), ((length, LANES), F32)],
        mixed, step, run, run_t, grad_scanned, scaled, state, carried_grad,
    )
    (back_onward,) = call(
        state_grads_kernel, [((devices, slice_rows, width), BF16)], back_arrived, decay
    )
    state_grad = swapped(back_onward.reshape(STATE, width))
    grad_w_out = scattered(keep_out, send_out, devices)

    keep_in, send_in, rim, back_raw, step_grad, conv_sums, sums = call(
        functools.partial(last_kernel, devices),
        [
            ((width // 2, channels), F32),
            ((width // 2, channels), BF16),
            ((HALO, channels), F32),
            ((length, channels), F32),
            ((length, LANES), BF16),
            (conv_w.shape, F32),
            ((2 * LABELS + 8, width), F32),
        ],
        place, hidden_in, edge, mixed, conv, raw, step, run, state, state_grad, weighted_grad, maps,
        run_grad, grad_scanned, heads, wide, conv_w, small, cls, own,
        scratch=[pltpu.VMEM((width, channels), F32), pltpu.VMEM((length + 2 * HALO, channels), F32)],
        scalars=1,
    )
    grad_w_in = scattered(keep_in, send_in, devices)
    (grad_hidden,) = call(
        hidden_kernel,
        [((length, w_in.shape[0]), BF16)],
        back_raw, passed_along(rim, "seq", 1), step_grad, w_in, w_dt_wide, conv_w,
        scratch=[pltpu.VMEM((length, channels), F32), pltpu.VMEM((2 * HALO, channels), F32)],
    )
    flat = jnp.concatenate([sums.reshape(-1, LANES), conv_sums.reshape(-1, LANES)], axis=0)
    for bit in range(devices.bit_length() - 1):
        flat = flat + partner(flat, "seq", bit)
    split = sums.size // LANES
    sums = flat[:split].reshape(sums.shape)
    base = 2 * LABELS
    loss = jnp.sum(sums[base + 4, 0:LANES]).reshape(1) / (row_count * devices)
    return (
        grad_hidden,
        grad_w_in,
        grad_w_out,
        flat[split:].reshape(conv_w.shape),
        sums[0:HEADS].T,
        sums[base + 1 : base + 4, 0:HEADS],
        sums[base],
        sums[LABELS : 2 * LABELS].T,
        loss,
    )


def solution(mesh):
    rows = P(("grp", "seq"), None)
    placed = (rows,) + (P(),) * 9 + (rows, P(), rows, P(("grp", "seq")), P(("grp", "seq")))
    part = P("grp", None)
    return jax.shard_map(
        per_device,
        mesh=mesh,
        in_specs=placed,
        out_specs=(rows, rows, rows, part, part, part, P("grp"), part, P("grp")),
        check_vma=False,
    )
```

```python
import functools

import jax
import jax.numpy as jnp
from jax import lax
from jax.experimental import pallas as pl
from jax.experimental.pallas import tpu as pltpu
from jax.sharding import PartitionSpec as P

HEADS = 12
HDIM = 64
STATE = 128
LABELS = 16
LANES = 128
HALO = 8
TAGS = 48
FACTS = 40
EPSILON = 1e-05
FAR = -1e30

F32 = jnp.float32
BF16 = jnp.bfloat16


def partner(x, axis, apart):
    return lax.ppermute(x, axis, [(i, i ^ 1 << apart) for i in range(lax.axis_size(axis))])


def passed_along(x, axis, by):
    length = lax.axis_size(axis)
    pairs = [(i, i + by) for i in range(length) if 0 <= i + by < length]
    return lax.ppermute(x, axis, pairs)


def dot(a, b, left=1, right=0):
    return lax.dot_general(a, b, (((left,), (right,)), ((), ())), preferred_element_type=F32)


def pieces(x, count):
    parts = []
    for _ in range(count):
        part = x.astype(BF16)
        parts.append(part)
        x = x - part.astype(F32)
    return parts


def finer(a, x, count, left=1, right=0):
    return sum(dot(a, part, left, right) for part in pieces(x, count))


def iota(shape, axis):
    return lax.broadcasted_iota(jnp.int32, shape, axis)


def spread_heads(x):
    rows = x.shape[0]
    first = iota((rows, LANES), 1) < HDIM
    return jnp.concatenate(
        [
            jnp.where(
                first,
                jnp.broadcast_to(x[:, 2 * pair : 2 * pair + 1], (rows, LANES)),
                jnp.broadcast_to(x[:, 2 * pair + 1 : 2 * pair + 2], (rows, LANES)),
            )
            for pair in range(HEADS // 2)
        ],
        axis=1,
    )


def head_sums(x):
    width = x.shape[1]
    member = (iota((width, LANES), 0) // HDIM == iota((width, LANES), 1)).astype(BF16)
    return sum(dot(part, member) for part in pieces(x, 2))


class Fetched:
    def __init__(self, ref, copy):
        self.ref, self.copy, self.shape = ref, copy, ref.shape

    def ready(self):
        if self.copy is not None:
            self.copy.wait()
            self.copy = None
        return self.ref

    def __getitem__(self, at):
        return self.ready()[at]


class Result:
    def __init__(self, ref, copy):
        self.ref, self.copy, self.shape, self.sent = ref, copy, ref.shape, False

    def __getitem__(self, at):
        return self.ref[at]

    def __setitem__(self, at, value):
        self.ref[at] = value

    def send(self):
        self.copy.start()
        self.sent = True


class Kept:
    def __init__(self, ref):
        self.ref, self.shape = ref, ref.shape

    def __getitem__(self, at):
        return self.ref[at]

    def __setitem__(self, at, value):
        self.ref[at] = value

    def send(self):
        pass


def call(body, outs, *args, scratch=(), scalars=0, fetch=(), leave=(), after=(), wait=()):
    waits = len(after) + len(wait)
    fetch = sorted(fetch)

    def kernel(*refs):
        refs = list(refs)

        def take(count):
            taken = refs[:count]
            del refs[:count]
            return taken

        inputs = take(len(args))
        take(waits)
        results = take(len(outs))
        places, outputs, extra = take(len(fetch)), take(len(leave)), take(len(scratch))
        arrivals, departures = refs
        for i, (at, place) in enumerate(zip(fetch, places)):
            copy = pltpu.make_async_copy(inputs[at], place, arrivals.at[i])
            copy.start()
            inputs[at] = Fetched(place, copy)
        written = []
        for i, result in enumerate(results):
            if i in leave:
                at = leave.index(i)
                copy = pltpu.make_async_copy(outputs[at], result, departures.at[at])
                written.append(Result(outputs[at], copy))
            else:
                written.append(Kept(result))
        body(*inputs, *written, *extra)
        for at in fetch:
            inputs[at].ready()
        gone = [result for result in written if isinstance(result, Result)]
        for result in gone:
            if not result.sent:
                result.send()
        for result in gone:
            result.copy.wait()

    far, close = pltpu.HBM, pltpu.VMEM
    specs, given = [], []
    for i, arg in enumerate(args):
        if i < scalars:
            specs.append(pl.BlockSpec(memory_space=pltpu.SMEM))
            given.append(arg)
        else:
            space = far if i in fetch else close
            specs.append(pl.BlockSpec(memory_space=space))
            given.append(pltpu.with_memory_space_constraint(arg, space))
    for space, arrays in ((close, after), (far, wait)):
        for arg in arrays:
            specs.append(pl.BlockSpec(memory_space=space))
            given.append(pltpu.with_memory_space_constraint(arg, space))
    return pl.pallas_call(
        kernel,
        out_shape=[(far if i in leave else close)(*out) for i, out in enumerate(outs)],
        in_specs=specs,
        out_specs=[pl.BlockSpec(memory_space=far if i in leave else close) for i in range(len(outs))],
        scratch_shapes=[
            *(pltpu.VMEM(args[i].shape, args[i].dtype) for i in fetch),
            *(pltpu.VMEM(*outs[i]) for i in leave),
            *scratch,
            pltpu.SemaphoreType.DMA((max(len(fetch), 1),)),
            pltpu.SemaphoreType.DMA((max(len(leave), 1),)),
        ],
        compiler_params=pltpu.CompilerParams(vmem_limit_bytes=24 * 1024 * 1024),
    )(*given)


def widened(x):
    place = (iota((HEADS, LANES), 0) == iota((HEADS, LANES), 1)).astype(BF16)
    return sum(dot(part, place) for part in pieces(x, 3))


def teacher_kernel(slice_rows, rows, weights, dest, start, size, extra, own):
    count = rows.shape[0]
    row, lane = iota((count, count), 0), iota((count, count), 1)
    named = dest[...].astype(F32)
    facts = jnp.where(
        row == 0, named, jnp.where(row == 1, start[...].astype(F32), size[...].astype(F32))
    ).T
    spans = facts[:, 2:3]
    slot = jnp.sum(
        jnp.where((facts[:, 0:1] == named) & (row < lane), 1.0, 0.0), axis=0, keepdims=True
    ).astype(jnp.int32)
    logits = dot(rows[...], weights[...], 1, 1)
    top = jnp.max(logits, axis=1, keepdims=True)
    shifted = logits - top
    logp = shifted - jnp.log(jnp.sum(jnp.exp(shifted), axis=1, keepdims=True))
    prob = jnp.exp(logp)
    label, spot = iota((LABELS, LANES), 0), iota((LABELS, LANES), 1)
    total = jnp.zeros((STATE, LANES), F32)
    for group in range(2):
        base = TAGS + group * FACTS
        inside = sum(
            dot(part, (spot == label + base + i * LABELS).astype(BF16))
            for i, part in enumerate(pieces(prob, 2))
        )
        spare = base + 2 * LABELS
        inside = jnp.where(lane == spare, facts[:, 1:2], inside)
        inside = jnp.where(lane == spare + 1, spans, inside)
        inside = jnp.where(lane == spare + 2, 1.0, inside)
        where_to = dest[...] * slice_rows + slot - group * slice_rows
        fits = (slot >= group * slice_rows) & (slot < (group + 1) * slice_rows)
        chosen = (iota((STATE, count), 0) == jnp.where(fits, where_to, -1)).astype(F32)
        total = total + dot(chosen.astype(BF16), inside.astype(BF16))
    extra[...] = total.astype(BF16)
    gained = jnp.sum(prob * logp, axis=1, keepdims=True) * spans
    own[...] = jnp.where(lane[0:1] == 0, jnp.sum(gained, axis=0, keepdims=True), 0.0)


def target_kernel(arrived, target):
    length = target.shape[0]
    width = HEADS * HDIM
    count, rows = arrived.shape[0], arrived.shape[1]
    facts = arrived[:, :, width:].astype(F32).reshape(count * rows, LANES).astype(BF16)
    facts_f = facts.astype(F32)
    position = iota((count * rows, length), 1).astype(F32)
    total = jnp.zeros((length, LANES), F32)
    for group in range(2):
        base = TAGS + group * FACTS
        spare = base + 2 * LABELS
        start = facts_f[:, spare : spare + 1]
        stop = start + facts_f[:, spare + 1 : spare + 2]
        covered = jnp.where((position >= start) & (position < stop), 1.0, 0.0).astype(BF16)
        sums = dot(covered, facts, 0, 0)
        lane = iota(sums.shape, 1)
        high = pltpu.roll(sums, LANES - base, 1)
        low = pltpu.roll(sums, LANES - base - LABELS, 1)
        cover = pltpu.roll(sums, (LABELS - spare - 2) % LANES, 1)
        total = total + jnp.where(lane < LABELS, high + low, jnp.where(lane == LABELS, cover, 0.0))
    target[...] = total


def convolved(raw, conv_w, length):
    conv = conv_w[0:1, :] * raw[0:length, :]
    for tap in range(1, conv_w.shape[0]):
        conv = conv + conv_w[tap : tap + 1, :] * raw[pl.ds(tap, length), :]
    return conv


def front_kernel(
    edge, hidden, w_dt, dt_bias, a_log, w_in, conv_w, extra,
    message, mixed_o, raw_o, step_o, run_o, run_t, raw,
):
    length = hidden.shape[0]
    wide = (iota((LANES, HEADS), 0) == iota((LANES, HEADS), 1)).astype(BF16)
    w_dt_wide = dot(wide, w_dt[...]).astype(BF16)
    before = dot(hidden[...], w_dt_wide, 1, 1) + widened(dt_bias[...])
    step = jnp.maximum(before, 0.0) + jnp.log1p(jnp.exp(-jnp.abs(before)))
    step = jnp.where(iota((length, LANES), 1) < HEADS, step, 0.0)
    log_decay = -step * jnp.exp(widened(a_log[...]))
    later = (iota((length, length), 1) >= iota((length, length), 0)).astype(BF16)
    run = finer(later, log_decay, 3)
    step_o[:, 0:LANES] = step
    step_o[:, LANES:] = before
    run_o[...] = run
    run_t[...] = run.T
    for result in (step_o, run_o, run_t):
        result.send()
    weights = w_in[...]
    raw_o[0:length, :] = dot(hidden[...], weights).astype(BF16)
    raw_o[length:, :] = dot(edge[...], weights).astype(BF16)
    raw_o.send()
    raw[...] = raw_o[...].astype(F32)
    conv = convolved(raw, conv_w, length)
    mixed = (conv / (1.0 + jnp.exp(-conv))).astype(BF16)
    mixed_o[...] = mixed
    mixed_o.send()
    width = HEADS * HDIM
    total = run[0:1, :]
    weighted = mixed[:, :width].astype(F32) * spread_heads(step * jnp.exp(total - run))
    state = dot(mixed[:, width : width + STATE], weighted.astype(BF16), 0, 0)
    message[:, :width] = state.astype(BF16)
    high, middle, low = (part.astype(F32) for part in pieces(total, 3))
    tags = high + pltpu.roll(middle, 16, 1) + pltpu.roll(low, 32, 1)
    message[:, width:] = (extra[...].astype(F32) + tags).astype(BF16)


def decay_blocks(run, run_t, head, half):
    top = run[0:half, head : head + 1] - run_t[head : head + 1, :]
    low = run[half:, head : head + 1] - run_t[head : head + 1, half:]
    top_seen = iota(top.shape, 1) >= iota(top.shape, 0)
    low_seen = iota(low.shape, 1) >= iota(low.shape, 0)
    return jnp.exp(jnp.where(top_seen, top, FAR)), jnp.exp(jnp.where(low_seen, low, FAR))


def local_kernel(mixed, step, run, run_t, local):
    length = mixed.shape[0]
    half = length // 2
    width = HEADS * HDIM
    in_map = mixed[:, width : width + STATE]
    out_map = mixed[:, width + STATE :]
    top_scores = dot(out_map[0:half], in_map, 1, 1)
    low_scores = dot(out_map[half:], in_map[half:], 1, 1)
    weighted = (mixed[:, :width].astype(F32) * spread_heads(step[:, 0:LANES])).astype(BF16)
    first = iota((half, LANES), 1) < HDIM
    for pair in range(HEADS // 2):
        lanes = slice(pair * LANES, (pair + 1) * LANES)
        own = weighted[:, lanes]
        tops, lows = [], []
        for head in (2 * pair, 2 * pair + 1):
            top, low = decay_blocks(run, run_t, head, half)
            tops.append(dot((top * top_scores).astype(BF16), own))
            lows.append(dot((low * low_scores).astype(BF16), own[half:]))
        local[0:half, lanes] = jnp.where(first, tops[0], tops[1])
        local[half:, lanes] = jnp.where(first, lows[0], lows[1])


def states_kernel(arrived, onward, decay):
    count = arrived.shape[0]
    width = HEADS * HDIM
    rows = arrived.shape[1]
    keep = iota((rows, LANES), 1) < HEADS
    state = jnp.zeros((rows, width), F32)
    for source in range(count - 1, -1, -1):
        onward[source] = state.astype(BF16)
        tags = arrived[source, :, width:].astype(F32)
        total = tags + pltpu.roll(tags, LANES - 16, 1) + pltpu.roll(tags, LANES - 32, 1)
        factor = spread_heads(jnp.exp(jnp.where(keep, total, 0.0)))
        decay[source] = factor
        state = arrived[source, :, :width].astype(F32) + factor * state


def state_grads_kernel(arrived, decay, onward):
    count = arrived.shape[0]
    state = jnp.zeros(arrived.shape[1:], F32)
    for source in range(count):
        onward[source] = state.astype(BF16)
        state = arrived[source].astype(F32) + decay[source] * state


def middle_kernel(
    state, mixed, run, local, d_skip, gains, w_out, w_cls, target,
    back_state, grad_scanned, normed_o, branch_o, back_branch_o, logits_o, run_grad, small,
):
    length = mixed.shape[0]
    width = HEADS * HDIM
    values = mixed[:, :width].astype(F32)
    out_map = mixed[:, width + STATE :]
    reach = spread_heads(jnp.exp(run[...]))
    carried = dot(out_map, state[...]) * reach
    gain = gains[...].reshape(1, width)
    skip = spread_heads(d_skip[...])
    scanned = local[...] + carried + skip * values
    scale = lax.rsqrt(jnp.mean(scanned * scanned, axis=1, keepdims=True) + EPSILON)
    plain = scanned * scale
    normed = (plain * gain).astype(BF16)
    normed_o[...] = normed
    normed_o.send()
    branch = dot(normed, w_out[...]).astype(BF16)
    branch_o[...] = branch
    branch_o.send()
    label = iota((length, LANES), 1) < LABELS
    wide = (iota((LANES, LABELS), 0) == iota((LANES, LABELS), 1)).astype(BF16)
    weights = dot(wide, w_cls[...]).astype(BF16)
    logits = jnp.where(label, dot(branch, weights, 1, 1), FAR)
    shifted = logits - jnp.max(logits, axis=1, keepdims=True)
    raised = jnp.exp(shifted)
    whole = jnp.sum(raised, axis=1, keepdims=True)
    logp = shifted - jnp.log(whole)
    wanted = target[...]
    cover = wanted[:, LABELS : LABELS + 1]
    back_logits = jnp.where(label, cover * (raised / whole) - wanted, 0.0)
    logits_o[...] = back_logits
    logits_o.send()
    lost = jnp.sum(jnp.where(label, wanted * logp, 0.0), axis=0, keepdims=True)
    back_branch = sum(dot(part, weights) for part in pieces(back_logits, 2)).astype(BF16)
    back_branch_o[...] = back_branch
    back_branch_o.send()
    back_normed = dot(back_branch, w_out[...], 1, 1)
    back_plain = back_normed * gain
    along = jnp.mean(back_plain * plain, axis=1, keepdims=True)
    back = scale * (back_plain - plain * along)
    grad_scanned[...] = back
    grad_scanned.send()
    back_state[...] = dot(out_map, (back * reach).astype(BF16), 0, 0).astype(BF16)
    back_state.send()
    run_grad[...] = head_sums(back * carried)
    small[0:1, :] = jnp.sum(back_normed * plain, axis=0, keepdims=True)
    small[1:2, :] = jnp.sum(back * values, axis=0, keepdims=True)
    small[2:3, :] = jnp.zeros((1, width), F32)
    small[2:3, 0:LANES] = lost
    small[3:, :] = jnp.zeros((5, width), F32)


def halves(full, keep, send, odd, blocks):
    size = full.shape[0] // blocks
    for side in (0, 1):

        @pl.when(odd == side)
        def _():
            for block in range(blocks // 2):
                at = slice(block * size, (block + 1) * size)
                mine = (2 * block + side) * size
                other = (2 * block + 1 - side) * size
                keep[at, :] = full[mine : mine + size, :].astype(BF16)
                send[at, :] = full[other : other + size, :].astype(BF16)


def outward_kernel(blocks, place, normed, back_branch, branch, back_logits, keep, send, cls, full):
    full[...] = dot(normed[...], back_branch[...], 0, 0)
    halves(full, keep, send, place[0] % 2, blocks)
    keep.send()
    send.send()
    parts = pieces(back_logits[...], 2)
    cls[...] = sum(dot(part, branch[...], 0, 0) for part in parts)[0:LABELS]


def local_back_kernel(
    mixed, step, run, run_t, grad_scanned, d_skip, state, carried_grad,
    values_grad, maps, run_grad, step_grad, weighted_grad,
):
    length = mixed.shape[0]
    half = length // 2
    width = HEADS * HDIM
    in_map = mixed[:, width : width + STATE]
    out_map = mixed[:, width + STATE :]
    top_scores = dot(out_map[0:half], in_map, 1, 1)
    low_scores = dot(out_map[half:], in_map[half:], 1, 1)
    values = mixed[:, :width].astype(F32)
    steps = spread_heads(step[:, 0:LANES])
    weighted = (values * steps).astype(BF16)
    lane = iota((length, LANES), 1)
    back_top = jnp.zeros((half, length), F32)
    back_low = jnp.zeros((half, half), F32)
    rows_top = jnp.zeros((half, LANES), F32)
    rows_low = jnp.zeros((half, LANES), F32)
    columns = jnp.zeros((length, LANES), F32)
    columns_low = jnp.zeros((half, LANES), F32)
    for pair in range(HEADS // 2):
        lanes = slice(pair * LANES, (pair + 1) * LANES)
        own = weighted[:, lanes]
        back_f = grad_scanned[:, lanes]
        back = back_f.astype(BF16)
        tops, lows = [], []
        for side in (0, 1):
            head = 2 * pair + side
            top, low = decay_blocks(run, run_t, head, half)
            mine = jnp.where((lane >= HDIM) == (side == 1), back_f, 0.0).astype(BF16)
            mix_top = (top * top_scores).astype(BF16)
            mix_low = (low * low_scores).astype(BF16)
            tops.append(dot(mix_top, back[0:half], 0, 0))
            lows.append(dot(mix_low, back[half:], 0, 0))
            grad_top = top * dot(mine[0:half], own, 1, 1)
            grad_low = low * dot(mine[half:], own[half:], 1, 1)
            back_top = back_top + grad_top
            back_low = back_low + grad_low
            part_top = (grad_top * top_scores).astype(BF16)
            part_low = (grad_low * low_scores).astype(BF16)
            marker = (lane == head).astype(F32).astype(BF16)
            rows_top = rows_top + dot(part_top, marker)
            rows_low = rows_low + dot(part_low, marker[half:])
            columns = columns + dot(part_top, marker[0:half], 0, 0)
            columns_low = columns_low + dot(part_low, marker[half:], 0, 0)
        weighted_grad[0:half, lanes] = jnp.where(lane[0:half] < HDIM, tops[0][0:half], tops[1][0:half])
        weighted_grad[half:, lanes] = jnp.where(
            lane[half:] < HDIM, tops[0][half:] + lows[0], tops[1][half:] + lows[1]
        )
    back_top = back_top.astype(BF16)
    back_low = back_low.astype(BF16)
    values_grad[...] = weighted_grad[...] * steps + spread_heads(d_skip[...]) * grad_scanned[...]
    values_grad.send()
    step_grad[...] = head_sums(weighted_grad[...] * values)
    scaled = (grad_scanned[...] * spread_heads(jnp.exp(run[...]))).astype(BF16)
    from_state = dot(scaled, state[...], 1, 1)
    maps[0:half, STATE:] = dot(back_top, in_map) + from_state[0:half]
    maps[half:, STATE:] = dot(back_low, in_map[half:]) + from_state[half:]
    in_grad = dot(back_top, out_map[0:half], 0, 0)
    maps[0:half, 0:STATE] = in_grad[0:half]
    maps[half:, 0:STATE] = in_grad[half:] + dot(back_low, out_map[half:], 0, 0)
    run_grad[0:half, :] = carried_grad[0:half, :] + rows_top - columns[0:half]
    run_grad[half:, :] = carried_grad[half:, :] + rows_low - columns[half:] - columns_low


def last_kernel(
    blocks, place, state_grad, edge, run, mixed, step, state, run_grad, step_local, a_log, conv_w,
    values_local, maps, raw_b, hidden, small, cls, own,
    keep, send, rim, back_raw_o, step_grad_o, conv_sums, sums, full, padded, raw,
):
    length = mixed.shape[0]
    taps = conv_w.shape[0]
    width = HEADS * HDIM
    total = run[0:1, :]
    tail = spread_heads(jnp.exp(total - run[...]))
    values = mixed[:, :width].astype(F32)
    in_map = mixed[:, width : width + STATE]
    incoming = state_grad[...]
    reached = dot(in_map, incoming) * tail
    steps = spread_heads(step[:, 0:LANES])
    weighted = values * steps
    ended = head_sums(reached * weighted)
    in_grad = dot((weighted * tail).astype(BF16), incoming, 1, 1)
    product = jnp.sum(incoming.astype(F32) * state[...].astype(F32), axis=0, keepdims=True)
    total_grad = jnp.exp(total) * head_sums(jnp.broadcast_to(product, (8, width)))[0:1]
    row, column = iota((length, length), 0), iota((length, length), 1)
    decay_grad = (
        finer((column <= row).astype(BF16), run_grad[...], 3)
        + finer((column > row).astype(BF16), ended, 3)
        + total_grad
    )
    rate = jnp.exp(widened(a_log[...]))
    step_grad = step_local[...] + head_sums(reached * values) - rate * decay_grad
    before = step[:, LANES:]
    step_grad = jnp.where(
        iota((length, LANES), 1) < HEADS, step_grad / (1.0 + jnp.exp(-before)), 0.0
    )
    step_grad_b = step_grad.astype(BF16)
    step_grad_o[...] = step_grad_b
    raw[...] = raw_b[...].astype(F32)
    padded[0:HALO, :] = jnp.zeros((HALO, padded.shape[1]), F32)
    padded[HALO + length :, :] = jnp.zeros((HALO, padded.shape[1]), F32)
    inner = convolved(raw, conv_w, length)
    gate = 1.0 / (1.0 + jnp.exp(-inner))
    slope = gate * (1.0 + inner * (1.0 - gate))
    middle = slice(HALO, HALO + length)
    padded[middle, 0:width] = (values_local[...] + reached * steps) * slope[:, 0:width]
    padded[middle, width : width + STATE] = (maps[:, 0:STATE] + in_grad) * slope[
        :, width : width + STATE
    ]
    padded[middle, width + STATE :] = maps[:, STATE:] * slope[:, width + STATE :]
    rim[...] = padded[length : length + HALO, :]
    rim.send()
    back_raw = jnp.zeros((length + HALO, padded.shape[1]), F32)
    for tap in range(taps):
        back_raw = back_raw + conv_w[tap : tap + 1, :] * padded[pl.ds(HALO - tap, length + HALO), :]
    back_raw_o[...] = back_raw[0:length]
    back_raw_o.send()
    full[...] = dot(hidden[...], back_raw[0:length].astype(BF16), 0, 0) + dot(
        edge[...], back_raw[length:].astype(BF16), 0, 0
    )
    halves(full, keep, send, place[0] % 2, blocks)
    keep.send()
    send.send()
    back_conv = padded[middle, :]
    for tap in range(taps):
        conv_sums[tap : tap + 1, :] = jnp.sum(
            back_conv * raw[pl.ds(tap, length), :], axis=0, keepdims=True
        )
    dt_grad = dot(step_grad_b, hidden[...], 0, 0)
    sums[0:LABELS, :] = dt_grad[0:LABELS]
    sums[LABELS : 2 * LABELS, :] = cls[...]
    base = 2 * LABELS
    sums[base:, :] = jnp.zeros((8, width), F32)
    sums[base : base + 1, :] = small[0:1, :]
    sums[base + 1 : base + 2, 0:LANES] = jnp.sum(step_grad, axis=0, keepdims=True)
    log_decay = -step[:, 0:LANES] * rate
    sums[base + 2 : base + 3, 0:LANES] = jnp.sum(decay_grad * log_decay, axis=0, keepdims=True)
    sums[base + 3 : base + 4, 0:LANES] = head_sums(jnp.broadcast_to(small[1:2, :], (8, width)))[0:1]
    sums[base + 4 : base + 5, 0:LANES] = own[...] - small[2:3, 0:LANES]


def hidden_kernel(rim, back_raw, conv_w, step_grad, w_dt, w_in, out, joined, edge):
    taps = conv_w.shape[0]
    joined[...] = back_raw[...]
    edge[0:HALO, :] = rim[...]
    edge[HALO:, :] = jnp.zeros((HALO, edge.shape[1]), F32)
    head = joined[0:HALO, :]
    for tap in range(taps):
        head = head + conv_w[tap : tap + 1, :] * edge[pl.ds(HALO - tap, HALO), :]
    joined[0:HALO, :] = head
    wide = (iota((LANES, HEADS), 0) == iota((LANES, HEADS), 1)).astype(BF16)
    w_dt_wide = dot(wide, w_dt[...]).astype(BF16)
    out[...] = (
        dot(joined[...].astype(BF16), w_in[...], 1, 1) + dot(step_grad[...], w_dt_wide)
    ).astype(BF16)


def swapped(x, axis="seq"):
    return lax.all_to_all(x, axis, split_axis=0, concat_axis=0, tiled=True)


def pair_kernel(keep, received, both):
    half = keep.shape[0] // 2
    both[0:half, :] = (keep[0:half, :].astype(F32) + received[0:half, :].astype(F32)).astype(BF16)
    both[half:, :] = (keep[half:, :].astype(F32) + received[half:, :].astype(F32)).astype(BF16)


def paired(keep, send, fetch):
    received = partner(send, "seq", 0)
    return call(pair_kernel, [(keep.shape, BF16)], keep, received, fetch=fetch, leave=(0,))[0]


def scattered(both, devices):
    groups = [[i for i in range(devices) if i % 2 == side] for side in (0, 1)]
    parts = lax.all_to_all(
        both, "seq", split_axis=0, concat_axis=0, axis_index_groups=groups, tiled=True
    )
    size = both.shape[0] // (devices // 2)
    return jnp.sum(parts.reshape(devices // 2, size, both.shape[1]).astype(F32), axis=0)


def per_device(
    hidden_in, w_in, w_dt, dt_bias, a_log, conv_w, d_skip, norm_gain, w_out, w_cls,
    teacher_rows, w_teacher, row_dest, row_start, row_len,
):
    devices = lax.axis_size("seq")
    length = hidden_in.shape[0]
    width = HEADS * HDIM
    channels = w_in.shape[1]
    slice_rows = STATE // devices
    row_count = teacher_rows.shape[0]
    place = lax.axis_index("seq").astype(jnp.int32).reshape(1)

    edge = passed_along(hidden_in[:HALO], "seq", -1)
    extra, own = call(
        functools.partial(teacher_kernel, slice_rows),
        [((STATE, LANES), BF16), ((1, LANES), F32)],
        teacher_rows, w_teacher.T, row_dest.reshape(1, row_count),
        row_start.reshape(1, row_count), row_len.reshape(1, row_count),
        fetch=range(5), leave=(1,),
    )
    w_dt_t = w_dt.T
    a_log_row = a_log.reshape(1, HEADS)
    skip_row = d_skip.reshape(1, HEADS)
    message, mixed, raw, step, run, run_t = call(
        front_kernel,
        [
            ((STATE, width + LANES), BF16),
            ((length, channels), BF16),
            ((length + HALO, channels), BF16),
            ((length, 2 * LANES), F32),
            ((length, LANES), F32),
            ((LANES, length), F32),
        ],
        edge, hidden_in, w_dt_t, dt_bias.reshape(1, HEADS), a_log_row, w_in, conv_w, extra,
        scratch=[pltpu.VMEM((length + HALO, channels), F32)], fetch=range(1, 7), leave=(0, 2),
    )
    arrived = swapped(message).reshape(devices, slice_rows, width + LANES)
    (local,) = call(local_kernel, [((length, width), F32)], mixed, step, run, run_t)
    onward, decay = call(
        states_kernel,
        [((devices, slice_rows, width), BF16), ((devices, slice_rows, width), F32)],
        arrived,
        leave=(0,),
        after=[local],
    )
    state = swapped(onward.reshape(STATE, width))
    (target,) = call(target_kernel, [((length, LANES), F32)], arrived)

    back_state, grad_scanned, normed, branch, back_branch, back_logits, carried_grad, small = call(
        middle_kernel,
        [
            ((STATE, width), BF16),
            ((length, width), F32),
            ((length, width), BF16),
            ((length, width), BF16),
            ((length, width), BF16),
            ((length, LANES), F32),
            ((length, LANES), F32),
            ((8, width), F32),
        ],
        state, mixed, run, local, skip_row, norm_gain, w_out, w_cls.T, target,
        fetch=(4, 5, 6, 7), leave=(0, 2, 3, 4, 5, 7),
    )
    back_arrived = swapped(back_state).reshape(devices, slice_rows, width)
    values_local, maps, run_grad, step_local = call(
        local_back_kernel,
        [
            ((length, width), F32),
            ((length, 2 * STATE), F32),
            ((length, LANES), F32),
            ((length, LANES), F32),
        ],
        mixed, step, run, run_t, grad_scanned, skip_row, state, carried_grad,
        scratch=[pltpu.VMEM((length, width), F32)], fetch=(5,),
    )
    (back_onward,) = call(
        state_grads_kernel,
        [((devices, slice_rows, width), BF16)],
        back_arrived, decay,
        leave=(0,), after=[run_grad],
    )
    state_grad = swapped(back_onward.reshape(STATE, width))
    keep_out, send_out, cls = call(
        functools.partial(outward_kernel, devices),
        [((width // 2, width), BF16), ((width // 2, width), BF16), ((LABELS, width), F32)],
        place, normed, back_branch, branch, back_logits,
        scratch=[pltpu.VMEM((width, width), F32)], scalars=1, fetch=range(1, 5), leave=(0, 1, 2), after=[run_grad],
    )
    both_out = paired(keep_out, send_out, (0, 1))
    grad_w_out = scattered(both_out, devices)

    keep_in, send_in, rim, back_raw, step_grad, conv_sums, sums = call(
        functools.partial(last_kernel, devices),
        [
            ((width // 2, channels), BF16),
            ((width // 2, channels), BF16),
            ((HALO, channels), F32),
            ((length, channels), F32),
            ((length, LANES), BF16),
            (conv_w.shape, F32),
            ((2 * LABELS + 8, width), F32),
        ],
        place, state_grad, edge, run, mixed, step, state, run_grad, step_local, a_log_row, conv_w,
        values_local, maps, raw, hidden_in, small, cls, own,
        scratch=[
            pltpu.VMEM((width, channels), F32),
            pltpu.VMEM((length + 2 * HALO, channels), F32),
            pltpu.VMEM((length + HALO, channels), F32),
        ],
        scalars=1, fetch=(9, 10, 13, 14, 15, 16, 17), leave=(1, 2, 3, 4), wait=[both_out],
    )
    grad_w_in = scattered(paired(keep_in, send_in, ()), devices)
    (grad_hidden,) = call(
        hidden_kernel,
        [((length, w_in.shape[0]), BF16)],
        passed_along(rim, "seq", 1), back_raw, conv_w, step_grad, w_dt_t, w_in,
        scratch=[pltpu.VMEM((length, channels), F32), pltpu.VMEM((2 * HALO, channels), F32)],
        fetch=range(1, 6), leave=(0,),
    )
    flat = jnp.concatenate([sums.reshape(-1, LANES), conv_sums.reshape(-1, LANES)], axis=0)
    for bit in range(devices.bit_length() - 1):
        if bit == 2:
            flat, grad_hidden = lax.optimization_barrier((flat, grad_hidden))
        flat = flat + partner(flat, "seq", bit)
    split = sums.size // LANES
    sums = flat[:split].reshape(sums.shape)
    base = 2 * LABELS
    loss = jnp.sum(sums[base + 4, 0:LANES]).reshape(1) / (row_count * devices)
    return (
        grad_hidden,
        grad_w_in,
        grad_w_out,
        flat[split:].reshape(conv_w.shape),
        sums[0:HEADS].T,
        sums[base + 1 : base + 4, 0:HEADS],
        sums[base],
        sums[LABELS : 2 * LABELS].T,
        loss,
    )


def solution(mesh):
    rows = P(("grp", "seq"), None)
    placed = (rows,) + (P(),) * 9 + (rows, P(), rows, P(("grp", "seq")), P(("grp", "seq")))
    part = P("grp", None)
    return jax.shard_map(
        per_device,
        mesh=mesh,
        in_specs=placed,
        out_specs=(rows, rows, rows, part, part, part, P("grp"), part, P("grp")),
        check_vma=False,
    )
```

```python
import functools

import jax
import jax.numpy as jnp
from jax import lax
from jax.experimental import pallas as pl
from jax.experimental.pallas import tpu as pltpu
from jax.sharding import PartitionSpec as P

HEADS = 12
HDIM = 64
STATE = 128
LABELS = 16
LANES = 128
HALO = 8
TAGS = 48
FACTS = 40
EPSILON = 1e-05
FAR = -1e30

F32 = jnp.float32
BF16 = jnp.bfloat16


def partner(x, axis, apart):
    return lax.ppermute(x, axis, [(i, i ^ 1 << apart) for i in range(lax.axis_size(axis))])


def passed_along(x, axis, by):
    length = lax.axis_size(axis)
    pairs = [(i, i + by) for i in range(length) if 0 <= i + by < length]
    return lax.ppermute(x, axis, pairs)


def dot(a, b, left=1, right=0):
    return lax.dot_general(a, b, (((left,), (right,)), ((), ())), preferred_element_type=F32)


def pieces(x, count):
    parts = []
    for _ in range(count):
        part = x.astype(BF16)
        parts.append(part)
        x = x - part.astype(F32)
    return parts


def finer(a, x, count, left=1, right=0):
    return sum(dot(a, part, left, right) for part in pieces(x, count))


def iota(shape, axis):
    return lax.broadcasted_iota(jnp.int32, shape, axis)


def spread_heads(x):
    rows = x.shape[0]
    first = iota((rows, LANES), 1) < HDIM
    return jnp.concatenate(
        [
            jnp.where(
                first,
                jnp.broadcast_to(x[:, 2 * pair : 2 * pair + 1], (rows, LANES)),
                jnp.broadcast_to(x[:, 2 * pair + 1 : 2 * pair + 2], (rows, LANES)),
            )
            for pair in range(HEADS // 2)
        ],
        axis=1,
    )


def head_sums(x):
    width = x.shape[1]
    member = (iota((width, LANES), 0) // HDIM == iota((width, LANES), 1)).astype(BF16)
    return sum(dot(part, member) for part in pieces(x, 2))


class Fetched:
    def __init__(self, ref, copy):
        self.ref, self.copy, self.shape = ref, copy, ref.shape

    def ready(self):
        if self.copy is not None:
            self.copy.wait()
            self.copy = None
        return self.ref

    def __getitem__(self, at):
        return self.ready()[at]


class Result:
    def __init__(self, ref, copy):
        self.ref, self.copy, self.shape, self.sent = ref, copy, ref.shape, False

    def __getitem__(self, at):
        return self.ref[at]

    def __setitem__(self, at, value):
        self.ref[at] = value

    def send(self):
        self.copy.start()
        self.sent = True


class Kept:
    def __init__(self, ref):
        self.ref, self.shape = ref, ref.shape

    def __getitem__(self, at):
        return self.ref[at]

    def __setitem__(self, at, value):
        self.ref[at] = value

    def send(self):
        pass


def call(body, outs, *args, scratch=(), scalars=0, fetch=(), leave=(), after=(), wait=()):
    waits = len(after) + len(wait)
    fetch = sorted(fetch)

    def kernel(*refs):
        refs = list(refs)

        def take(count):
            taken = refs[:count]
            del refs[:count]
            return taken

        inputs = take(len(args))
        take(waits)
        results = take(len(outs))
        places, outputs, extra = take(len(fetch)), take(len(leave)), take(len(scratch))
        arrivals, departures = refs
        for i, (at, place) in enumerate(zip(fetch, places)):
            copy = pltpu.make_async_copy(inputs[at], place, arrivals.at[i])
            copy.start()
            inputs[at] = Fetched(place, copy)
        written = []
        for i, result in enumerate(results):
            if i in leave:
                at = leave.index(i)
                copy = pltpu.make_async_copy(outputs[at], result, departures.at[at])
                written.append(Result(outputs[at], copy))
            else:
                written.append(Kept(result))
        body(*inputs, *written, *extra)
        for at in fetch:
            inputs[at].ready()
        gone = [result for result in written if isinstance(result, Result)]
        for result in gone:
            if not result.sent:
                result.send()
        for result in gone:
            result.copy.wait()

    far, close = pltpu.HBM, pltpu.VMEM
    specs, given = [], []
    for i, arg in enumerate(args):
        if i < scalars:
            specs.append(pl.BlockSpec(memory_space=pltpu.SMEM))
            given.append(arg)
        else:
            space = far if i in fetch else close
            specs.append(pl.BlockSpec(memory_space=space))
            given.append(pltpu.with_memory_space_constraint(arg, space))
    for space, arrays in ((close, after), (far, wait)):
        for arg in arrays:
            specs.append(pl.BlockSpec(memory_space=space))
            given.append(pltpu.with_memory_space_constraint(arg, space))
    return pl.pallas_call(
        kernel,
        out_shape=[(far if i in leave else close)(*out) for i, out in enumerate(outs)],
        in_specs=specs,
        out_specs=[pl.BlockSpec(memory_space=far if i in leave else close) for i in range(len(outs))],
        scratch_shapes=[
            *(pltpu.VMEM(args[i].shape, args[i].dtype) for i in fetch),
            *(pltpu.VMEM(*outs[i]) for i in leave),
            *scratch,
            pltpu.SemaphoreType.DMA((max(len(fetch), 1),)),
            pltpu.SemaphoreType.DMA((max(len(leave), 1),)),
        ],
        compiler_params=pltpu.CompilerParams(vmem_limit_bytes=24 * 1024 * 1024),
    )(*given)


def widened(x):
    place = (iota((HEADS, LANES), 0) == iota((HEADS, LANES), 1)).astype(BF16)
    return sum(dot(part, place) for part in pieces(x, 3))


def teacher_kernel(slice_rows, rows, weights, dest, start, size, extra, own):
    count = rows.shape[0]
    row, lane = iota((count, count), 0), iota((count, count), 1)
    named = dest[...].astype(F32)
    facts = jnp.where(
        row == 0, named, jnp.where(row == 1, start[...].astype(F32), size[...].astype(F32))
    ).T
    spans = facts[:, 2:3]
    slot = jnp.sum(
        jnp.where((facts[:, 0:1] == named) & (row < lane), 1.0, 0.0), axis=0, keepdims=True
    ).astype(jnp.int32)
    logits = dot(rows[...], weights[...], 1, 1)
    top = jnp.max(logits, axis=1, keepdims=True)
    shifted = logits - top
    logp = shifted - jnp.log(jnp.sum(jnp.exp(shifted), axis=1, keepdims=True))
    prob = jnp.exp(logp)
    label, spot = iota((LABELS, LANES), 0), iota((LABELS, LANES), 1)
    total = jnp.zeros((STATE, LANES), F32)
    for group in range(2):
        base = TAGS + group * FACTS
        inside = sum(
            dot(part, (spot == label + base + i * LABELS).astype(BF16))
            for i, part in enumerate(pieces(prob, 2))
        )
        spare = base + 2 * LABELS
        inside = jnp.where(lane == spare, facts[:, 1:2], inside)
        inside = jnp.where(lane == spare + 1, spans, inside)
        inside = jnp.where(lane == spare + 2, 1.0, inside)
        where_to = dest[...] * slice_rows + slot - group * slice_rows
        fits = (slot >= group * slice_rows) & (slot < (group + 1) * slice_rows)
        chosen = (iota((STATE, count), 0) == jnp.where(fits, where_to, -1)).astype(F32)
        total = total + dot(chosen.astype(BF16), inside.astype(BF16))
    extra[...] = total.astype(BF16)
    gained = jnp.sum(prob * logp, axis=1, keepdims=True) * spans
    own[...] = jnp.where(lane[0:1] == 0, jnp.sum(gained, axis=0, keepdims=True), 0.0)


def target_kernel(arrived, target):
    length = target.shape[0]
    width = HEADS * HDIM
    count, rows = arrived.shape[0], arrived.shape[1]
    facts = arrived[:, :, width:].astype(F32).reshape(count * rows, LANES).astype(BF16)
    facts_f = facts.astype(F32)
    position = iota((count * rows, length), 1).astype(F32)
    total = jnp.zeros((length, LANES), F32)
    for group in range(2):
        base = TAGS + group * FACTS
        spare = base + 2 * LABELS
        start = facts_f[:, spare : spare + 1]
        stop = start + facts_f[:, spare + 1 : spare + 2]
        covered = jnp.where((position >= start) & (position < stop), 1.0, 0.0).astype(BF16)
        sums = dot(covered, facts, 0, 0)
        lane = iota(sums.shape, 1)
        high = pltpu.roll(sums, LANES - base, 1)
        low = pltpu.roll(sums, LANES - base - LABELS, 1)
        cover = pltpu.roll(sums, (LABELS - spare - 2) % LANES, 1)
        total = total + jnp.where(lane < LABELS, high + low, jnp.where(lane == LABELS, cover, 0.0))
    target[...] = total


def convolved(raw, conv_w, length):
    conv = conv_w[0:1, :] * raw[0:length, :]
    for tap in range(1, conv_w.shape[0]):
        conv = conv + conv_w[tap : tap + 1, :] * raw[pl.ds(tap, length), :]
    return conv


def front_kernel(
    edge, hidden, w_dt, dt_bias, a_log, w_in, conv_w, extra,
    message, mixed_o, raw_o, step_o, run_o, run_t, raw,
):
    length = hidden.shape[0]
    wide = (iota((LANES, HEADS), 0) == iota((LANES, HEADS), 1)).astype(BF16)
    w_dt_wide = dot(wide, w_dt[...]).astype(BF16)
    before = dot(hidden[...], w_dt_wide, 1, 1) + widened(dt_bias[...])
    step = jnp.maximum(before, 0.0) + jnp.log1p(jnp.exp(-jnp.abs(before)))
    step = jnp.where(iota((length, LANES), 1) < HEADS, step, 0.0)
    log_decay = -step * jnp.exp(widened(a_log[...]))
    later = (iota((length, length), 1) >= iota((length, length), 0)).astype(BF16)
    run = finer(later, log_decay, 3)
    step_o[:, 0:LANES] = step
    step_o[:, LANES:] = before
    run_o[...] = run
    run_t[...] = run.T
    for result in (step_o, run_o, run_t):
        result.send()
    weights = w_in[...]
    raw_o[0:length, :] = dot(hidden[...], weights).astype(BF16)
    raw_o[length:, :] = dot(edge[...], weights).astype(BF16)
    raw_o.send()
    raw[...] = raw_o[...].astype(F32)
    conv = convolved(raw, conv_w, length)
    mixed = (conv / (1.0 + jnp.exp(-conv))).astype(BF16)
    mixed_o[...] = mixed
    mixed_o.send()
    width = HEADS * HDIM
    total = run[0:1, :]
    weighted = mixed[:, :width].astype(F32) * spread_heads(step * jnp.exp(total - run))
    state = dot(mixed[:, width : width + STATE], weighted.astype(BF16), 0, 0)
    message[:, :width] = state.astype(BF16)
    high, middle, low = (part.astype(F32) for part in pieces(total, 3))
    tags = high + pltpu.roll(middle, 16, 1) + pltpu.roll(low, 32, 1)
    message[:, width:] = (extra[...].astype(F32) + tags).astype(BF16)


def decay_blocks(run, run_t, head, half):
    top = run[0:half, head : head + 1] - run_t[head : head + 1, :]
    low = run[half:, head : head + 1] - run_t[head : head + 1, half:]
    top_seen = iota(top.shape, 1) >= iota(top.shape, 0)
    low_seen = iota(low.shape, 1) >= iota(low.shape, 0)
    return jnp.exp(jnp.where(top_seen, top, FAR)), jnp.exp(jnp.where(low_seen, low, FAR))


def local_kernel(mixed, step, run, run_t, local):
    length = mixed.shape[0]
    half = length // 2
    width = HEADS * HDIM
    in_map = mixed[:, width : width + STATE]
    out_map = mixed[:, width + STATE :]
    top_scores = dot(out_map[0:half], in_map, 1, 1)
    low_scores = dot(out_map[half:], in_map[half:], 1, 1)
    weighted = (mixed[:, :width].astype(F32) * spread_heads(step[:, 0:LANES])).astype(BF16)
    first = iota((half, LANES), 1) < HDIM
    for pair in range(HEADS // 2):
        lanes = slice(pair * LANES, (pair + 1) * LANES)
        own = weighted[:, lanes]
        tops, lows = [], []
        for head in (2 * pair, 2 * pair + 1):
            top, low = decay_blocks(run, run_t, head, half)
            tops.append(dot((top * top_scores).astype(BF16), own))
            lows.append(dot((low * low_scores).astype(BF16), own[half:]))
        local[0:half, lanes] = jnp.where(first, tops[0], tops[1])
        local[half:, lanes] = jnp.where(first, lows[0], lows[1])


def states_kernel(arrived, onward, decay):
    count = arrived.shape[0]
    width = HEADS * HDIM
    rows = arrived.shape[1]
    keep = iota((rows, LANES), 1) < HEADS
    state = jnp.zeros((rows, width), F32)
    for source in range(count - 1, -1, -1):
        onward[source] = state.astype(BF16)
        tags = arrived[source, :, width:].astype(F32)
        total = tags + pltpu.roll(tags, LANES - 16, 1) + pltpu.roll(tags, LANES - 32, 1)
        factor = jnp.exp(jnp.where(keep, total, 0.0))
        decay[source] = factor
        state = arrived[source, :, :width].astype(F32) + spread_heads(factor) * state


def state_grads_kernel(arrived, decay, early, onward):
    count, rows, width = arrived.shape
    state = jnp.zeros(arrived.shape[1:], F32)
    for source in range(count):
        onward[source, :, :width] = state.astype(BF16)
        onward[source, :, width:] = early[source * rows : (source + 1) * rows, :].astype(BF16)
        state = arrived[source].astype(F32) + spread_heads(decay[source]) * state


def middle_kernel(
    state, mixed, run, local, d_skip, gains, w_out, w_cls, target,
    back_state, grad_scanned, normed_o, branch_o, back_branch_o, logits_o, run_grad, small,
):
    length = mixed.shape[0]
    width = HEADS * HDIM
    values = mixed[:, :width].astype(F32)
    out_map = mixed[:, width + STATE :]
    reach = spread_heads(jnp.exp(run[...]))
    carried = dot(out_map, state[...]) * reach
    gain = gains[...].reshape(1, width)
    skip = spread_heads(d_skip[...])
    scanned = local[...] + carried + skip * values
    scale = lax.rsqrt(jnp.mean(scanned * scanned, axis=1, keepdims=True) + EPSILON)
    plain = scanned * scale
    normed = (plain * gain).astype(BF16)
    normed_o[...] = normed
    normed_o.send()
    branch = dot(normed, w_out[...]).astype(BF16)
    branch_o[...] = branch
    branch_o.send()
    label = iota((length, LANES), 1) < LABELS
    wide = (iota((LANES, LABELS), 0) == iota((LANES, LABELS), 1)).astype(BF16)
    weights = dot(wide, w_cls[...]).astype(BF16)
    logits = jnp.where(label, dot(branch, weights, 1, 1), FAR)
    shifted = logits - jnp.max(logits, axis=1, keepdims=True)
    raised = jnp.exp(shifted)
    whole = jnp.sum(raised, axis=1, keepdims=True)
    logp = shifted - jnp.log(whole)
    wanted = target[...]
    cover = wanted[:, LABELS : LABELS + 1]
    back_logits = jnp.where(label, cover * (raised / whole) - wanted, 0.0)
    logits_o[...] = back_logits
    logits_o.send()
    lost = jnp.sum(jnp.where(label, wanted * logp, 0.0), axis=0, keepdims=True)
    back_branch = sum(dot(part, weights) for part in pieces(back_logits, 2)).astype(BF16)
    back_branch_o[...] = back_branch
    back_branch_o.send()
    back_normed = dot(back_branch, w_out[...], 1, 1)
    back_plain = back_normed * gain
    along = jnp.mean(back_plain * plain, axis=1, keepdims=True)
    back = scale * (back_plain - plain * along)
    grad_scanned[...] = back
    grad_scanned.send()
    back_state[...] = dot(out_map, (back * reach).astype(BF16), 0, 0).astype(BF16)
    back_state.send()
    run_grad[...] = head_sums(back * carried)
    small[0:1, :] = jnp.sum(back_normed * plain, axis=0, keepdims=True)
    small[1:2, :] = jnp.sum(back * values, axis=0, keepdims=True)
    small[2:3, :] = jnp.zeros((1, width), F32)
    small[2:3, 0:LANES] = lost
    small[3:, :] = jnp.zeros((5, width), F32)


def halves(full, keep, send, odd, blocks):
    size = full.shape[0] // blocks
    for side in (0, 1):

        @pl.when(odd == side)
        def _():
            for block in range(blocks // 2):
                at = slice(block * size, (block + 1) * size)
                mine = (2 * block + side) * size
                other = (2 * block + 1 - side) * size
                keep[at, :] = full[mine : mine + size, :].astype(BF16)
                send[at, :] = full[other : other + size, :].astype(BF16)


def outward_kernel(
    blocks, place, normed, back_branch, branch, back_logits, small, keep, send, early, full
):
    full[...] = dot(normed[...], back_branch[...], 0, 0)
    halves(full, keep, send, place[0] % 2, blocks)
    keep.send()
    send.send()
    parts = pieces(back_logits[...], 2)
    cls = sum(dot(part, branch[...], 0, 0) for part in parts)[0:LABELS]
    count = cls.shape[1] // LANES
    early[count * LABELS :, :] = jnp.zeros((early.shape[0] - count * LABELS, LANES), F32)
    for block in range(count):
        lanes = slice(block * LANES, (block + 1) * LANES)
        early[block * LABELS : (block + 1) * LABELS, :] = cls[:, lanes]
        at = count * LABELS + block
        early[at : at + 1, :] = small[0:1, lanes]


def local_back_kernel(
    mixed, step, run, grad_scanned, d_skip, state, carried_grad,
    values_grad, maps, run_grad, step_grad, weighted_grad,
):
    length = mixed.shape[0]
    half = length // 2
    width = HEADS * HDIM
    in_map = mixed[:, width : width + STATE]
    out_map = mixed[:, width + STATE :]
    top_scores = dot(out_map[0:half], in_map, 1, 1)
    low_scores = dot(out_map[half:], in_map[half:], 1, 1)
    values = mixed[:, :width].astype(F32)
    steps = spread_heads(step[:, 0:LANES])
    weighted = (values * steps).astype(BF16)
    run_t = run[...].T
    lane = iota((length, LANES), 1)
    back_top = jnp.zeros((half, length), F32)
    back_low = jnp.zeros((half, half), F32)
    rows_top = jnp.zeros((half, LANES), F32)
    rows_low = jnp.zeros((half, LANES), F32)
    columns = jnp.zeros((length, LANES), F32)
    columns_low = jnp.zeros((half, LANES), F32)
    for pair in range(HEADS // 2):
        lanes = slice(pair * LANES, (pair + 1) * LANES)
        own = weighted[:, lanes]
        back_f = grad_scanned[:, lanes]
        back = back_f.astype(BF16)
        tops, lows = [], []
        for side in (0, 1):
            head = 2 * pair + side
            top, low = decay_blocks(run, run_t, head, half)
            mine = jnp.where((lane >= HDIM) == (side == 1), back_f, 0.0).astype(BF16)
            mix_top = (top * top_scores).astype(BF16)
            mix_low = (low * low_scores).astype(BF16)
            tops.append(dot(mix_top, back[0:half], 0, 0))
            lows.append(dot(mix_low, back[half:], 0, 0))
            grad_top = top * dot(mine[0:half], own, 1, 1)
            grad_low = low * dot(mine[half:], own[half:], 1, 1)
            back_top = back_top + grad_top
            back_low = back_low + grad_low
            part_top = (grad_top * top_scores).astype(BF16)
            part_low = (grad_low * low_scores).astype(BF16)
            marker = (lane == head).astype(F32).astype(BF16)
            rows_top = rows_top + dot(part_top, marker)
            rows_low = rows_low + dot(part_low, marker[half:])
            columns = columns + dot(part_top, marker[0:half], 0, 0)
            columns_low = columns_low + dot(part_low, marker[half:], 0, 0)
        weighted_grad[0:half, lanes] = jnp.where(lane[0:half] < HDIM, tops[0][0:half], tops[1][0:half])
        weighted_grad[half:, lanes] = jnp.where(
            lane[half:] < HDIM, tops[0][half:] + lows[0], tops[1][half:] + lows[1]
        )
    back_top = back_top.astype(BF16)
    back_low = back_low.astype(BF16)
    values_grad[...] = weighted_grad[...] * steps + spread_heads(d_skip[...]) * grad_scanned[...]
    values_grad.send()
    step_grad[...] = head_sums(weighted_grad[...] * values)
    scaled = (grad_scanned[...] * spread_heads(jnp.exp(run[...]))).astype(BF16)
    from_state = dot(scaled, state[...], 1, 1)
    maps[0:half, STATE:] = dot(back_top, in_map) + from_state[0:half]
    maps[half:, STATE:] = dot(back_low, in_map[half:]) + from_state[half:]
    in_grad = dot(back_top, out_map[0:half], 0, 0)
    maps[0:half, 0:STATE] = in_grad[0:half]
    maps[half:, 0:STATE] = in_grad[half:] + dot(back_low, out_map[half:], 0, 0)
    run_grad[0:half, :] = carried_grad[0:half, :] + rows_top - columns[0:half]
    run_grad[half:, :] = carried_grad[half:, :] + rows_low - columns[half:] - columns_low


def last_kernel(
    blocks, place, state_grad, edge, run, mixed, step, state, run_grad, step_local, a_log, conv_w,
    values_local, maps, raw_b, hidden, small, own,
    keep, send, rim, back_raw_o, step_grad_o, late, full, padded, raw,
):
    length = mixed.shape[0]
    taps = conv_w.shape[0]
    width = HEADS * HDIM
    total = run[0:1, :]
    tail = spread_heads(jnp.exp(total - run[...]))
    values = mixed[:, :width].astype(F32)
    in_map = mixed[:, width : width + STATE]
    incoming = state_grad[:, :width]
    reached = dot(in_map, incoming) * tail
    steps = spread_heads(step[:, 0:LANES])
    weighted = values * steps
    ended = head_sums(reached * weighted)
    in_grad = dot((weighted * tail).astype(BF16), incoming, 1, 1)
    product = jnp.sum(incoming.astype(F32) * state[...].astype(F32), axis=0, keepdims=True)
    total_grad = jnp.exp(total) * head_sums(jnp.broadcast_to(product, (8, width)))[0:1]
    row, column = iota((length, length), 0), iota((length, length), 1)
    decay_grad = (
        finer((column <= row).astype(BF16), run_grad[...], 3)
        + finer((column > row).astype(BF16), ended, 3)
        + total_grad
    )
    rate = jnp.exp(widened(a_log[...]))
    step_grad = step_local[...] + head_sums(reached * values) - rate * decay_grad
    before = step[:, LANES:]
    step_grad = jnp.where(
        iota((length, LANES), 1) < HEADS, step_grad / (1.0 + jnp.exp(-before)), 0.0
    )
    step_grad_b = step_grad.astype(BF16)
    step_grad_o[...] = step_grad_b
    raw[...] = raw_b[...].astype(F32)
    padded[0:HALO, :] = jnp.zeros((HALO, padded.shape[1]), F32)
    padded[HALO + length :, :] = jnp.zeros((HALO, padded.shape[1]), F32)
    inner = convolved(raw, conv_w, length)
    gate = 1.0 / (1.0 + jnp.exp(-inner))
    slope = gate * (1.0 + inner * (1.0 - gate))
    middle = slice(HALO, HALO + length)
    padded[middle, 0:width] = (values_local[...] + reached * steps) * slope[:, 0:width]
    padded[middle, width : width + STATE] = (maps[:, 0:STATE] + in_grad) * slope[
        :, width : width + STATE
    ]
    padded[middle, width + STATE :] = maps[:, STATE:] * slope[:, width + STATE :]
    rim[...] = padded[length : length + HALO, :]
    rim.send()
    back_raw = jnp.zeros((length + HALO, padded.shape[1]), F32)
    for tap in range(taps):
        back_raw = back_raw + conv_w[tap : tap + 1, :] * padded[pl.ds(HALO - tap, length + HALO), :]
    back_raw_o[...] = back_raw[0:length]
    back_raw_o.send()
    full[...] = dot(hidden[...], back_raw[0:length].astype(BF16), 0, 0) + dot(
        edge[...], back_raw[length:].astype(BF16), 0, 0
    )
    halves(full, keep, send, place[0] % 2, blocks)
    keep.send()
    send.send()
    back_conv = padded[middle, :]
    spare = late.shape[0] - taps
    for tap in range(taps):
        late[spare + tap : spare + tap + 1, :] = jnp.sum(
            back_conv * raw[pl.ds(tap, length), :], axis=0, keepdims=True
        )
    late[0:HEADS, 0:width] = dot(step_grad_b, hidden[...], 0, 0)[0:HEADS]
    late[0:HEADS, width:] = jnp.zeros((HEADS, late.shape[1] - width), F32)
    log_decay = -step[:, 0:LANES] * rate
    facts = jnp.sum(step_grad, axis=0, keepdims=True)
    facts = facts + pltpu.roll(jnp.sum(decay_grad * log_decay, axis=0, keepdims=True), 16, 1)
    skips = head_sums(jnp.broadcast_to(small[1:2, :], (8, width)))[0:1]
    lost = jnp.sum(own[...] - small[2:3, 0:LANES], axis=1, keepdims=True)
    lane = iota((1, LANES), 1)
    facts = facts + pltpu.roll(skips, 32, 1) + jnp.where(lane == 48, lost, 0.0)
    late[HEADS - 4 : HEADS - 3, width : width + LANES] = facts
    shares = state_grad[:, width:].astype(F32)
    rows = shares.shape[0] // blocks
    share = sum(shares[source * rows : (source + 1) * rows] for source in range(blocks))
    for side in (0, 1):

        @pl.when(place[0] % 2 == side)
        def _():
            late[0:rows, width + side * LANES : width + (side + 1) * LANES] = share


def hidden_kernel(rim, back_raw, conv_w, step_grad, w_dt, w_in, out, joined, edge):
    taps = conv_w.shape[0]
    joined[...] = back_raw[...]
    edge[0:HALO, :] = rim[...]
    edge[HALO:, :] = jnp.zeros((HALO, edge.shape[1]), F32)
    head = joined[0:HALO, :]
    for tap in range(taps):
        head = head + conv_w[tap : tap + 1, :] * edge[pl.ds(HALO - tap, HALO), :]
    joined[0:HALO, :] = head
    wide = (iota((LANES, HEADS), 0) == iota((LANES, HEADS), 1)).astype(BF16)
    w_dt_wide = dot(wide, w_dt[...]).astype(BF16)
    out[...] = (
        dot(joined[...].astype(BF16), w_in[...], 1, 1) + dot(step_grad[...], w_dt_wide)
    ).astype(BF16)


def swapped(x, axis="seq"):
    return lax.all_to_all(x, axis, split_axis=0, concat_axis=0, tiled=True)


def pair_kernel(keep, received, both):
    half = keep.shape[0] // 2
    both[0:half, :] = (keep[0:half, :].astype(F32) + received[0:half, :].astype(F32)).astype(BF16)
    both[half:, :] = (keep[half:, :].astype(F32) + received[half:, :].astype(F32)).astype(BF16)


def paired(keep, send, fetch):
    received = partner(send, "seq", 0)
    return call(pair_kernel, [(keep.shape, BF16)], keep, received, fetch=fetch, leave=(0,))[0]


def joint_kernel(blocks, keep, received, late, late_received, both):
    size = keep.shape[0] // blocks
    rows, width = late.shape[0], HEADS * HDIM
    sums = late[...] + late_received[...]
    facts = sums[:, width : width + LANES]
    rest = pltpu.roll(facts - facts.astype(BF16).astype(F32), 1, 0)
    row = iota(facts.shape, 0)
    facts = jnp.where(row == HEADS - 3, rest, facts)
    sums = jnp.concatenate([sums[:, :width], facts, sums[:, width + LANES :]], axis=1).astype(BF16)
    for block in range(blocks):
        base, at = block * (size + rows), slice(block * size, (block + 1) * size)
        both[base : base + size, :] = (
            keep[at, :].astype(F32) + received[at, :].astype(F32)
        ).astype(BF16)
        both[base + size : base + size + rows, :] = sums


def joint_sums_kernel(
    share, rows_in_all, parts, grad_w_in, grad_conv, grad_dt_t, grad_heads, gain, cls_t, loss, early
):
    total = parts[0].astype(F32)
    for chip in range(1, parts.shape[0]):
        total = total + parts[chip].astype(F32)
    size, taps, width = grad_w_in.shape[0], grad_conv.shape[0], HEADS * HDIM
    grad_w_in[...] = total[0:size]
    grad_conv[...] = total[size + HEADS : size + HEADS + taps]
    grad_dt_t[...] = total[size : size + HEADS, 0:width]
    at = size + HEADS - 4
    facts = total[at : at + 1, width : width + LANES] + total[at + 1 : at + 2, width : width + LANES]
    for row in range(3):
        moved = pltpu.roll(facts, (LANES - 16 * row) % LANES, 1) if row else facts
        grad_heads[row : row + 1, :] = moved[:, 0:HEADS]
    loss[...] = pltpu.roll(facts, LANES - 48, 1)[:, 0:1] / rows_in_all
    for chip in range(parts.shape[0]):
        for side in (0, 1):
            base = (2 * chip + side) * share
            lanes = slice(width + side * LANES, width + (side + 1) * LANES)
            early[base : base + share, :] = parts[chip][size : size + share, lanes].astype(F32)
    count = width // LANES
    for block in range(count):
        lanes = slice(block * LANES, (block + 1) * LANES)
        cls_t[:, lanes] = early[block * LABELS : (block + 1) * LABELS, :]
        gain[:, lanes] = early[count * LABELS + block : count * LABELS + block + 1, :]


def exchanged(both, devices):
    groups = [[i for i in range(devices) if i % 2 == side] for side in (0, 1)]
    parts = lax.all_to_all(
        both, "seq", split_axis=0, concat_axis=0, axis_index_groups=groups, tiled=True
    )
    return parts.reshape(devices // 2, -1, both.shape[1])


def per_device(
    hidden_in, w_in, w_dt, dt_bias, a_log, conv_w, d_skip, norm_gain, w_out, w_cls,
    teacher_rows, w_teacher, row_dest, row_start, row_len,
):
    devices = lax.axis_size("seq")
    length = hidden_in.shape[0]
    width = HEADS * HDIM
    channels = w_in.shape[1]
    slice_rows = STATE // devices
    row_count = teacher_rows.shape[0]
    place = lax.axis_index("seq").astype(jnp.int32).reshape(1)

    edge = passed_along(hidden_in[:HALO], "seq", -1)
    extra, own = call(
        functools.partial(teacher_kernel, slice_rows),
        [((STATE, LANES), BF16), ((1, LANES), F32)],
        teacher_rows, w_teacher.T, row_dest.reshape(1, row_count),
        row_start.reshape(1, row_count), row_len.reshape(1, row_count),
        fetch=range(5), leave=(1,),
    )
    w_dt_t = w_dt.T
    a_log_row = a_log.reshape(1, HEADS)
    skip_row = d_skip.reshape(1, HEADS)
    message, mixed, raw, step, run, run_t = call(
        front_kernel,
        [
            ((STATE, width + LANES), BF16),
            ((length, channels), BF16),
            ((length + HALO, channels), BF16),
            ((length, 2 * LANES), F32),
            ((length, LANES), F32),
            ((LANES, length), F32),
        ],
        edge, hidden_in, w_dt_t, dt_bias.reshape(1, HEADS), a_log_row, w_in, conv_w, extra,
        scratch=[pltpu.VMEM((length + HALO, channels), F32)], fetch=range(1, 7), leave=(0, 2),
    )
    arrived = swapped(message).reshape(devices, slice_rows, width + LANES)
    (local,) = call(local_kernel, [((length, width), F32)], mixed, step, run, run_t)
    onward, decay = call(
        states_kernel,
        [((devices, slice_rows, width), BF16), ((devices, slice_rows, LANES), F32)],
        arrived,
        leave=(0,),
        after=[local],
    )
    state = swapped(onward.reshape(STATE, width))
    (target,) = call(target_kernel, [((length, LANES), F32)], arrived)

    back_state, grad_scanned, normed, branch, back_branch, back_logits, carried_grad, small = call(
        middle_kernel,
        [
            ((STATE, width), BF16),
            ((length, width), F32),
            ((length, width), BF16),
            ((length, width), BF16),
            ((length, width), BF16),
            ((length, LANES), F32),
            ((length, LANES), F32),
            ((8, width), F32),
        ],
        state, mixed, run, local, skip_row, norm_gain, w_out, w_cls.T, target,
        fetch=(4, 5, 6, 7), leave=(0, 2, 3, 4, 5, 6, 7),
    )
    back_arrived = swapped(back_state).reshape(devices, slice_rows, width)
    values_local, maps, run_grad, step_local = call(
        local_back_kernel,
        [
            ((length, width), F32),
            ((length, 2 * STATE), F32),
            ((length, LANES), F32),
            ((length, LANES), F32),
        ],
        mixed, step, run, grad_scanned, skip_row, state, carried_grad,
        scratch=[pltpu.VMEM((length, width), F32)], fetch=(4, 6), leave=(1, 3),
    )
    keep_out, send_out, early = call(
        functools.partial(outward_kernel, devices),
        [((width // 2, width), BF16), ((width // 2, width), BF16), ((STATE, LANES), F32)],
        place, normed, back_branch, branch, back_logits, small,
        scratch=[pltpu.VMEM((width, width), F32)],
        scalars=1, fetch=range(1, 6), leave=(0, 1), after=[run_grad],
    )
    (back_onward,) = call(
        state_grads_kernel,
        [((devices, slice_rows, width + LANES), BF16)],
        back_arrived, decay, early,
        leave=(0,),
    )
    state_grad = swapped(back_onward.reshape(STATE, width + LANES))
    both_out = paired(keep_out, send_out, (0,))
    grad_w_out = jnp.sum(exchanged(both_out, devices).astype(F32), axis=0)

    keep_in, send_in, rim, back_raw, step_grad, late = call(
        functools.partial(last_kernel, devices),
        [
            ((width // 2, channels), BF16),
            ((width // 2, channels), BF16),
            ((HALO, channels), F32),
            ((length, channels), F32),
            ((length, LANES), BF16),
            ((HEADS + conv_w.shape[0], channels), F32),
        ],
        place, state_grad, edge, run, mixed, step, state, run_grad, step_local, a_log_row, conv_w,
        values_local, maps, raw, hidden_in, small, own,
        scratch=[
            pltpu.VMEM((width, channels), F32),
            pltpu.VMEM((length + 2 * HALO, channels), F32),
            pltpu.VMEM((length + HALO, channels), F32),
        ],
        scalars=1, fetch=(8, 9, 10, 12, 13, 14, 15, 16), leave=(1, 2, 3, 4), wait=[both_out],
    )
    chips = devices // 2
    (both_in,) = call(
        functools.partial(joint_kernel, chips),
        [((width // 2 + chips * late.shape[0], channels), BF16)],
        keep_in, partner(send_in, "seq", 0), late, partner(late, "seq", 0),
        leave=(0,),
    )
    parts = exchanged(both_in, devices)
    (grad_hidden,) = call(
        hidden_kernel,
        [((length, w_in.shape[0]), BF16)],
        passed_along(rim, "seq", 1), back_raw, conv_w, step_grad, w_dt_t, w_in,
        scratch=[pltpu.VMEM((length, channels), F32), pltpu.VMEM((2 * HALO, channels), F32)],
        fetch=range(1, 6), leave=(0,),
    )
    grad_w_in, grad_conv, grad_dt_t, grad_heads, gain, cls_t, loss = call(
        functools.partial(joint_sums_kernel, slice_rows, float(row_count * devices)),
        [
            ((width // devices, channels), F32),
            (conv_w.shape, F32),
            ((HEADS, width), F32),
            ((3, HEADS), F32),
            ((1, width), F32),
            ((LABELS, width), F32),
            ((1, 1), F32),
        ],
        parts,
        scratch=[pltpu.VMEM((STATE, LANES), F32)], leave=range(7),
    )
    return (
        grad_hidden,
        grad_w_in,
        grad_w_out,
        grad_conv,
        grad_dt_t.T,
        grad_heads,
        gain.reshape(width),
        cls_t.T,
        loss.reshape(1),
    )


def solution(mesh):
    rows = P(("grp", "seq"), None)
    placed = (rows,) + (P(),) * 9 + (rows, P(), rows, P(("grp", "seq")), P(("grp", "seq")))
    part = P("grp", None)
    return jax.shard_map(
        per_device,
        mesh=mesh,
        in_specs=placed,
        out_specs=(rows, rows, rows, part, part, part, P("grp"), part, P("grp")),
        check_vma=False,
    )
```

```python
import functools

import jax
import jax.numpy as jnp
from jax import lax
from jax.experimental import pallas as pl
from jax.experimental.pallas import tpu as pltpu
from jax.sharding import PartitionSpec as P

HEADS = 12
HDIM = 64
STATE = 128
LABELS = 16
LANES = 128
HALO = 8
TAGS = 48
FACTS = 40
EPSILON = 1e-05
FAR = -1e30

F32 = jnp.float32
BF16 = jnp.bfloat16


def partner(x, axis, apart):
    return lax.ppermute(x, axis, [(i, i ^ 1 << apart) for i in range(lax.axis_size(axis))])


def passed_along(x, axis, by):
    length = lax.axis_size(axis)
    pairs = [(i, i + by) for i in range(length) if 0 <= i + by < length]
    return lax.ppermute(x, axis, pairs)


def dot(a, b, left=1, right=0):
    return lax.dot_general(a, b, (((left,), (right,)), ((), ())), preferred_element_type=F32)


def pieces(x, count):
    parts = []
    for _ in range(count):
        part = x.astype(BF16)
        parts.append(part)
        x = x - part.astype(F32)
    return parts


def finer(a, x, count, left=1, right=0):
    return sum(dot(a, part, left, right) for part in pieces(x, count))


def iota(shape, axis):
    return lax.broadcasted_iota(jnp.int32, shape, axis)


def spread_heads(x):
    rows = x.shape[0]
    first = iota((rows, LANES), 1) < HDIM
    return jnp.concatenate(
        [
            jnp.where(
                first,
                jnp.broadcast_to(x[:, 2 * pair : 2 * pair + 1], (rows, LANES)),
                jnp.broadcast_to(x[:, 2 * pair + 1 : 2 * pair + 2], (rows, LANES)),
            )
            for pair in range(HEADS // 2)
        ],
        axis=1,
    )


def head_sums(x):
    width = x.shape[1]
    member = (iota((width, LANES), 0) // HDIM == iota((width, LANES), 1)).astype(BF16)
    return sum(dot(part, member) for part in pieces(x, 2))


class Fetched:
    def __init__(self, ref, copy):
        self.ref, self.copy, self.shape = ref, copy, ref.shape

    def ready(self):
        if self.copy is not None:
            self.copy.wait()
            self.copy = None
        return self.ref

    def __getitem__(self, at):
        return self.ready()[at]


class Result:
    def __init__(self, ref, copy):
        self.ref, self.copy, self.shape, self.sent = ref, copy, ref.shape, False

    def __getitem__(self, at):
        return self.ref[at]

    def __setitem__(self, at, value):
        self.ref[at] = value

    def send(self):
        self.copy.start()
        self.sent = True


class Kept:
    def __init__(self, ref):
        self.ref, self.shape = ref, ref.shape

    def __getitem__(self, at):
        return self.ref[at]

    def __setitem__(self, at, value):
        self.ref[at] = value

    def send(self):
        pass


def call(body, outs, *args, scratch=(), scalars=0, fetch=(), leave=(), after=(), wait=()):
    waits = len(after) + len(wait)
    fetch = sorted(fetch)

    def kernel(*refs):
        refs = list(refs)

        def take(count):
            taken = refs[:count]
            del refs[:count]
            return taken

        inputs = take(len(args))
        take(waits)
        results = take(len(outs))
        places, outputs, extra = take(len(fetch)), take(len(leave)), take(len(scratch))
        arrivals, departures = refs
        for i, (at, place) in enumerate(zip(fetch, places)):
            copy = pltpu.make_async_copy(inputs[at], place, arrivals.at[i])
            copy.start()
            inputs[at] = Fetched(place, copy)
        written = []
        for i, result in enumerate(results):
            if i in leave:
                at = leave.index(i)
                copy = pltpu.make_async_copy(outputs[at], result, departures.at[at])
                written.append(Result(outputs[at], copy))
            else:
                written.append(Kept(result))
        body(*inputs, *written, *extra)
        for at in fetch:
            inputs[at].ready()
        gone = [result for result in written if isinstance(result, Result)]
        for result in gone:
            if not result.sent:
                result.send()
        for result in gone:
            result.copy.wait()

    far, close = pltpu.HBM, pltpu.VMEM
    specs, given = [], []
    for i, arg in enumerate(args):
        if i < scalars:
            specs.append(pl.BlockSpec(memory_space=pltpu.SMEM))
            given.append(arg)
        else:
            space = far if i in fetch else close
            specs.append(pl.BlockSpec(memory_space=space))
            given.append(pltpu.with_memory_space_constraint(arg, space))
    for space, arrays in ((close, after), (far, wait)):
        for arg in arrays:
            specs.append(pl.BlockSpec(memory_space=space))
            given.append(pltpu.with_memory_space_constraint(arg, space))
    return pl.pallas_call(
        kernel,
        out_shape=[(far if i in leave else close)(*out) for i, out in enumerate(outs)],
        in_specs=specs,
        out_specs=[pl.BlockSpec(memory_space=far if i in leave else close) for i in range(len(outs))],
        scratch_shapes=[
            *(pltpu.VMEM(args[i].shape, args[i].dtype) for i in fetch),
            *(pltpu.VMEM(*outs[i]) for i in leave),
            *scratch,
            pltpu.SemaphoreType.DMA((max(len(fetch), 1),)),
            pltpu.SemaphoreType.DMA((max(len(leave), 1),)),
        ],
        compiler_params=pltpu.CompilerParams(vmem_limit_bytes=24 * 1024 * 1024),
    )(*given)


def widened(x):
    place = (iota((HEADS, LANES), 0) == iota((HEADS, LANES), 1)).astype(BF16)
    return sum(dot(part, place) for part in pieces(x, 3))


def teacher_kernel(slice_rows, rows, weights, dest, start, size, extra, own):
    count = rows.shape[0]
    row, lane = iota((count, count), 0), iota((count, count), 1)
    named = dest[...].astype(F32)
    facts = jnp.where(
        row == 0, named, jnp.where(row == 1, start[...].astype(F32), size[...].astype(F32))
    ).T
    spans = facts[:, 2:3]
    slot = jnp.sum(
        jnp.where((facts[:, 0:1] == named) & (row < lane), 1.0, 0.0), axis=0, keepdims=True
    ).astype(jnp.int32)
    logits = dot(rows[...], weights[...], 1, 1)
    top = jnp.max(logits, axis=1, keepdims=True)
    shifted = logits - top
    logp = shifted - jnp.log(jnp.sum(jnp.exp(shifted), axis=1, keepdims=True))
    prob = jnp.exp(logp)
    label, spot = iota((LABELS, LANES), 0), iota((LABELS, LANES), 1)
    total = jnp.zeros((STATE, LANES), F32)
    for group in range(2):
        base = TAGS + group * FACTS
        inside = sum(
            dot(part, (spot == label + base + i * LABELS).astype(BF16))
            for i, part in enumerate(pieces(prob, 2))
        )
        spare = base + 2 * LABELS
        inside = jnp.where(lane == spare, facts[:, 1:2], inside)
        inside = jnp.where(lane == spare + 1, spans, inside)
        inside = jnp.where(lane == spare + 2, 1.0, inside)
        where_to = dest[...] * slice_rows + slot - group * slice_rows
        fits = (slot >= group * slice_rows) & (slot < (group + 1) * slice_rows)
        chosen = (iota((STATE, count), 0) == jnp.where(fits, where_to, -1)).astype(F32)
        total = total + dot(chosen.astype(BF16), inside.astype(BF16))
    extra[...] = total.astype(BF16)
    gained = jnp.sum(prob * logp, axis=1, keepdims=True) * spans
    own[...] = jnp.where(lane[0:1] == 0, jnp.sum(gained, axis=0, keepdims=True), 0.0)


def target_kernel(arrived, w_cls, w_out, target, joined_high, joined_low):
    length = target.shape[0]
    width = HEADS * HDIM
    count, rows = arrived.shape[0], arrived.shape[1]
    facts = arrived[:, :, width:].astype(F32).reshape(count * rows, LANES).astype(BF16)
    facts_f = facts.astype(F32)
    position = iota((count * rows, length), 1).astype(F32)
    total = jnp.zeros((length, LANES), F32)
    for group in range(2):
        base = TAGS + group * FACTS
        spare = base + 2 * LABELS
        start = facts_f[:, spare : spare + 1]
        stop = start + facts_f[:, spare + 1 : spare + 2]
        covered = jnp.where((position >= start) & (position < stop), 1.0, 0.0).astype(BF16)
        sums = dot(covered, facts, 0, 0)
        lane = iota(sums.shape, 1)
        high = pltpu.roll(sums, LANES - base, 1)
        low = pltpu.roll(sums, LANES - base - LABELS, 1)
        cover = pltpu.roll(sums, (LABELS - spare - 2) % LANES, 1)
        total = total + jnp.where(lane < LABELS, high + low, jnp.where(lane == LABELS, cover, 0.0))
    target[...] = total
    place = (iota((LANES, LABELS), 0) == iota((LANES, LABELS), 1)).astype(BF16)
    joined = dot(dot(place, w_cls[...]).astype(BF16), w_out[...], 1, 1)
    joined_high[...], joined_low[...] = pieces(joined, 2)


def convolved(raw, conv_w, length):
    conv = conv_w[0:1, :] * raw[0:length, :]
    for tap in range(1, conv_w.shape[0]):
        conv = conv + conv_w[tap : tap + 1, :] * raw[pl.ds(tap, length), :]
    return conv


def front_kernel(
    edge, hidden, w_dt, dt_bias, a_log, w_in, conv_w, extra,
    message, mixed_o, raw_o, step_o, run_o, run_t, raw,
):
    length = hidden.shape[0]
    wide = (iota((LANES, HEADS), 0) == iota((LANES, HEADS), 1)).astype(BF16)
    w_dt_wide = dot(wide, w_dt[...]).astype(BF16)
    before = dot(hidden[...], w_dt_wide, 1, 1) + widened(dt_bias[...])
    step = jnp.maximum(before, 0.0) + jnp.log1p(jnp.exp(-jnp.abs(before)))
    step = jnp.where(iota((length, LANES), 1) < HEADS, step, 0.0)
    log_decay = -step * jnp.exp(widened(a_log[...]))
    later = (iota((length, length), 1) >= iota((length, length), 0)).astype(BF16)
    run = finer(later, log_decay, 3)
    step_o[:, 0:LANES] = step
    step_o[:, LANES:] = before
    run_o[...] = run
    run_t[...] = run.T
    for result in (step_o, run_o, run_t):
        result.send()
    weights = w_in[...]
    raw_o[0:length, :] = dot(hidden[...], weights).astype(BF16)
    raw_o[length:, :] = dot(edge[...], weights).astype(BF16)
    raw_o.send()
    raw[...] = raw_o[...].astype(F32)
    conv = convolved(raw, conv_w, length)
    mixed = (conv / (1.0 + jnp.exp(-conv))).astype(BF16)
    mixed_o[...] = mixed
    mixed_o.send()
    width = HEADS * HDIM
    total = run[0:1, :]
    weighted = mixed[:, :width].astype(F32) * spread_heads(step * jnp.exp(total - run))
    state = dot(mixed[:, width : width + STATE], weighted.astype(BF16), 0, 0)
    message[:, :width] = state.astype(BF16)
    high, middle, low = (part.astype(F32) for part in pieces(total, 3))
    tags = high + pltpu.roll(middle, 16, 1) + pltpu.roll(low, 32, 1)
    message[:, width:] = (extra[...].astype(F32) + tags).astype(BF16)


def decay_blocks(run, run_t, head, half):
    top = run[0:half, head : head + 1] - run_t[head : head + 1, :]
    low = run[half:, head : head + 1] - run_t[head : head + 1, half:]
    top_seen = iota(top.shape, 1) >= iota(top.shape, 0)
    low_seen = iota(low.shape, 1) >= iota(low.shape, 0)
    return jnp.exp(jnp.where(top_seen, top, FAR)), jnp.exp(jnp.where(low_seen, low, FAR))


def local_kernel(mixed, step, run, run_t, local):
    length = mixed.shape[0]
    half = length // 2
    width = HEADS * HDIM
    in_map = mixed[:, width : width + STATE]
    out_map = mixed[:, width + STATE :]
    top_scores = dot(out_map[0:half], in_map, 1, 1)
    low_scores = dot(out_map[half:], in_map[half:], 1, 1)
    weighted = (mixed[:, :width].astype(F32) * spread_heads(step[:, 0:LANES])).astype(BF16)
    first = iota((half, LANES), 1) < HDIM
    for pair in range(HEADS // 2):
        lanes = slice(pair * LANES, (pair + 1) * LANES)
        own = weighted[:, lanes]
        tops, lows = [], []
        for head in (2 * pair, 2 * pair + 1):
            top, low = decay_blocks(run, run_t, head, half)
            tops.append(dot((top * top_scores).astype(BF16), own))
            lows.append(dot((low * low_scores).astype(BF16), own[half:]))
        local[0:half, lanes] = jnp.where(first, tops[0], tops[1])
        local[half:, lanes] = jnp.where(first, lows[0], lows[1])


def states_kernel(arrived, onward, decay):
    count = arrived.shape[0]
    width = HEADS * HDIM
    rows = arrived.shape[1]
    keep = iota((rows, LANES), 1) < HEADS
    state = jnp.zeros((rows, width), F32)
    for source in range(count - 1, -1, -1):
        onward[source] = state.astype(BF16)
        tags = arrived[source, :, width:].astype(F32)
        total = tags + pltpu.roll(tags, LANES - 16, 1) + pltpu.roll(tags, LANES - 32, 1)
        factor = jnp.exp(jnp.where(keep, total, 0.0))
        decay[source] = factor
        state = arrived[source, :, :width].astype(F32) + spread_heads(factor) * state


def state_grads_kernel(arrived, decay, early, onward):
    count, rows, width = arrived.shape
    state = jnp.zeros(arrived.shape[1:], F32)
    for source in range(count):
        onward[source, :, :width] = state.astype(BF16)
        onward[source, :, width:] = early[source * rows : (source + 1) * rows, :].astype(BF16)
        state = arrived[source].astype(F32) + spread_heads(decay[source]) * state


def middle_kernel(
    state, mixed, run, local, d_skip, gains, high, low, target,
    back_state, grad_scanned, normed_o, logits_o, run_grad, small,
):
    length = mixed.shape[0]
    width = HEADS * HDIM
    values = mixed[:, :width].astype(F32)
    out_map = mixed[:, width + STATE :]
    reach = spread_heads(jnp.exp(run[...]))
    carried = dot(out_map, state[...]) * reach
    gain = gains[...].reshape(1, width)
    skip = spread_heads(d_skip[...])
    scanned = local[...] + carried + skip * values
    scale = lax.rsqrt(jnp.mean(scanned * scanned, axis=1, keepdims=True) + EPSILON)
    plain = scanned * scale
    normed = (plain * gain).astype(BF16)
    normed_o[...] = normed
    normed_o.send()
    label = iota((length, LANES), 1) < LABELS
    logits = jnp.where(label, dot(normed, high[...], 1, 1) + dot(normed, low[...], 1, 1), FAR)
    shifted = logits - jnp.max(logits, axis=1, keepdims=True)
    raised = jnp.exp(shifted)
    whole = jnp.sum(raised, axis=1, keepdims=True)
    logp = shifted - jnp.log(whole)
    wanted = target[...]
    cover = wanted[:, LABELS : LABELS + 1]
    back_logits = jnp.where(label, cover * (raised / whole) - wanted, 0.0)
    logits_o[...] = back_logits
    logits_o.send()
    lost = jnp.sum(jnp.where(label, wanted * logp, 0.0), axis=0, keepdims=True)
    back_high, back_low = pieces(back_logits, 2)
    back_normed = dot(back_high, high[...]) + dot(back_low, high[...]) + dot(back_high, low[...])
    back_plain = back_normed * gain
    along = jnp.mean(back_plain * plain, axis=1, keepdims=True)
    back = scale * (back_plain - plain * along)
    grad_scanned[...] = back
    back_state[...] = dot(out_map, (back * reach).astype(BF16), 0, 0).astype(BF16)
    back_state.send()
    small[0:1, :] = jnp.sum(back_normed * plain, axis=0, keepdims=True)
    small[1:2, :] = jnp.sum(back * values, axis=0, keepdims=True)
    small[2:3, :] = jnp.zeros((1, width), F32)
    small[2:3, 0:LANES] = lost
    small[3:, :] = jnp.zeros((5, width), F32)
    small.send()
    run_grad[...] = head_sums(back * carried)


def halves(full, keep, send, odd, blocks):
    size = full.shape[0] // blocks
    for side in (0, 1):

        @pl.when(odd == side)
        def _():
            for block in range(blocks // 2):
                at = slice(block * size, (block + 1) * size)
                mine = (2 * block + side) * size
                other = (2 * block + 1 - side) * size
                keep[at, :] = full[mine : mine + size, :].astype(BF16)
                send[at, :] = full[other : other + size, :].astype(BF16)


def local_back_kernel(
    mixed, step, run, grad_scanned, d_skip, state, carried_grad, normed, back_logits, small,
    values_grad, maps, run_grad, step_grad, early, weighted_grad,
):
    length = mixed.shape[0]
    half = length // 2
    width = HEADS * HDIM
    in_map = mixed[:, width : width + STATE]
    out_map = mixed[:, width + STATE :]
    top_scores = dot(out_map[0:half], in_map, 1, 1)
    low_scores = dot(out_map[half:], in_map[half:], 1, 1)
    values = mixed[:, :width].astype(F32)
    steps = spread_heads(step[:, 0:LANES])
    weighted = (values * steps).astype(BF16)
    run_t = run[...].T
    lane = iota((length, LANES), 1)
    back_top = jnp.zeros((half, length), F32)
    back_low = jnp.zeros((half, half), F32)
    rows_top = jnp.zeros((half, LANES), F32)
    rows_low = jnp.zeros((half, LANES), F32)
    columns = jnp.zeros((length, LANES), F32)
    columns_low = jnp.zeros((half, LANES), F32)
    for pair in range(HEADS // 2):
        lanes = slice(pair * LANES, (pair + 1) * LANES)
        own = weighted[:, lanes]
        back_f = grad_scanned[:, lanes]
        back = back_f.astype(BF16)
        tops, lows = [], []
        for side in (0, 1):
            head = 2 * pair + side
            top, low = decay_blocks(run, run_t, head, half)
            mine = jnp.where((lane >= HDIM) == (side == 1), back_f, 0.0).astype(BF16)
            mix_top = (top * top_scores).astype(BF16)
            mix_low = (low * low_scores).astype(BF16)
            tops.append(dot(mix_top, back[0:half], 0, 0))
            lows.append(dot(mix_low, back[half:], 0, 0))
            grad_top = top * dot(mine[0:half], own, 1, 1)
            grad_low = low * dot(mine[half:], own[half:], 1, 1)
            back_top = back_top + grad_top
            back_low = back_low + grad_low
            part_top = (grad_top * top_scores).astype(BF16)
            part_low = (grad_low * low_scores).astype(BF16)
            marker = (lane == head).astype(F32).astype(BF16)
            rows_top = rows_top + dot(part_top, marker)
            rows_low = rows_low + dot(part_low, marker[half:])
            columns = columns + dot(part_top, marker[0:half], 0, 0)
            columns_low = columns_low + dot(part_low, marker[half:], 0, 0)
        weighted_grad[0:half, lanes] = jnp.where(lane[0:half] < HDIM, tops[0][0:half], tops[1][0:half])
        weighted_grad[half:, lanes] = jnp.where(
            lane[half:] < HDIM, tops[0][half:] + lows[0], tops[1][half:] + lows[1]
        )
    back_top = back_top.astype(BF16)
    back_low = back_low.astype(BF16)
    values_grad[...] = weighted_grad[...] * steps + spread_heads(d_skip[...]) * grad_scanned[...]
    values_grad.send()
    step_grad[...] = head_sums(weighted_grad[...] * values)
    scaled = (grad_scanned[...] * spread_heads(jnp.exp(run[...]))).astype(BF16)
    from_state = dot(scaled, state[...], 1, 1)
    maps[0:half, STATE:] = dot(back_top, in_map) + from_state[0:half]
    maps[half:, STATE:] = dot(back_low, in_map[half:]) + from_state[half:]
    in_grad = dot(back_top, out_map[0:half], 0, 0)
    maps[0:half, 0:STATE] = in_grad[0:half]
    maps[half:, 0:STATE] = in_grad[half:] + dot(back_low, out_map[half:], 0, 0)
    run_grad[0:half, :] = carried_grad[0:half, :] + rows_top - columns[0:half]
    run_grad[half:, :] = carried_grad[half:, :] + rows_low - columns[half:] - columns_low
    product = sum(dot(part, normed[...], 0, 0) for part in pieces(back_logits[...], 2))[0:LABELS]
    count = width // LANES
    early[count * LABELS :, :] = jnp.zeros((early.shape[0] - count * LABELS, LANES), F32)
    for block in range(count):
        lanes = slice(block * LANES, (block + 1) * LANES)
        early[block * LABELS : (block + 1) * LABELS, :] = product[:, lanes]
        at = count * LABELS + block
        early[at : at + 1, :] = small[0:1, lanes]


def last_kernel(
    blocks, place, state_grad, edge, run, mixed, step, state, run_grad, step_local, a_log, conv_w,
    values_local, maps, raw_b, hidden, small, own,
    keep, send, rim, back_raw_o, step_grad_o, late, full, padded, raw,
):
    length = mixed.shape[0]
    taps = conv_w.shape[0]
    width = HEADS * HDIM
    total = run[0:1, :]
    tail = spread_heads(jnp.exp(total - run[...]))
    values = mixed[:, :width].astype(F32)
    in_map = mixed[:, width : width + STATE]
    incoming = state_grad[:, :width]
    reached = dot(in_map, incoming) * tail
    steps = spread_heads(step[:, 0:LANES])
    weighted = values * steps
    reaching = head_sums(reached * values)
    ended = reaching * step[:, 0:LANES]
    in_grad = dot((weighted * tail).astype(BF16), incoming, 1, 1)
    product = jnp.sum(incoming.astype(F32) * state[...].astype(F32), axis=0, keepdims=True)
    total_grad = jnp.exp(total) * head_sums(jnp.broadcast_to(product, (8, width)))[0:1]
    row, column = iota((length, length), 0), iota((length, length), 1)
    decay_grad = (
        finer((column <= row).astype(BF16), run_grad[...], 3)
        + finer((column > row).astype(BF16), ended, 3)
        + total_grad
    )
    rate = jnp.exp(widened(a_log[...]))
    step_grad = step_local[...] + reaching - rate * decay_grad
    before = step[:, LANES:]
    step_grad = jnp.where(
        iota((length, LANES), 1) < HEADS, step_grad / (1.0 + jnp.exp(-before)), 0.0
    )
    step_grad_b = step_grad.astype(BF16)
    step_grad_o[...] = step_grad_b
    raw[...] = raw_b[...].astype(F32)
    padded[0:HALO, :] = jnp.zeros((HALO, padded.shape[1]), F32)
    padded[HALO + length :, :] = jnp.zeros((HALO, padded.shape[1]), F32)
    inner = convolved(raw, conv_w, length)
    gate = 1.0 / (1.0 + jnp.exp(-inner))
    slope = gate * (1.0 + inner * (1.0 - gate))
    middle = slice(HALO, HALO + length)
    padded[middle, 0:width] = (values_local[...] + reached * steps) * slope[:, 0:width]
    padded[middle, width : width + STATE] = (maps[:, 0:STATE] + in_grad) * slope[
        :, width : width + STATE
    ]
    padded[middle, width + STATE :] = maps[:, STATE:] * slope[:, width + STATE :]
    rim[...] = padded[length : length + HALO, :]
    rim.send()
    back_raw = jnp.zeros((length + HALO, padded.shape[1]), F32)
    for tap in range(taps):
        back_raw = back_raw + conv_w[tap : tap + 1, :] * padded[pl.ds(HALO - tap, length + HALO), :]
    back_raw_o[...] = back_raw[0:length]
    back_raw_o.send()
    full[...] = dot(hidden[...], back_raw[0:length].astype(BF16), 0, 0) + dot(
        edge[...], back_raw[length:].astype(BF16), 0, 0
    )
    halves(full, keep, send, place[0] % 2, blocks)
    keep.send()
    send.send()
    back_conv = padded[middle, :]
    spare = late.shape[0] - taps
    for tap in range(taps):
        late[spare + tap : spare + tap + 1, :] = jnp.sum(
            back_conv * raw[pl.ds(tap, length), :], axis=0, keepdims=True
        )
    late[0:HEADS, 0:width] = dot(step_grad_b, hidden[...], 0, 0)[0:HEADS]
    late[0:HEADS, width:] = jnp.zeros((HEADS, late.shape[1] - width), F32)
    log_decay = -step[:, 0:LANES] * rate
    facts = jnp.sum(step_grad, axis=0, keepdims=True)
    facts = facts + pltpu.roll(jnp.sum(decay_grad * log_decay, axis=0, keepdims=True), 16, 1)
    skips = head_sums(jnp.broadcast_to(small[1:2, :], (8, width)))[0:1]
    lost = jnp.sum(own[...] - small[2:3, 0:LANES], axis=1, keepdims=True)
    lane = iota((1, LANES), 1)
    facts = facts + pltpu.roll(skips, 32, 1) + jnp.where(lane == 48, lost, 0.0)
    late[HEADS - 4 : HEADS - 3, width : width + LANES] = facts
    shares = state_grad[:, width:].astype(F32)
    rows = shares.shape[0] // blocks
    share = sum(shares[source * rows : (source + 1) * rows] for source in range(blocks))
    for side in (0, 1):

        @pl.when(place[0] % 2 == side)
        def _():
            late[0:rows, width + side * LANES : width + (side + 1) * LANES] = share


def hidden_kernel(rim, back_raw, conv_w, step_grad, w_dt, w_in, out, joined, edge):
    taps = conv_w.shape[0]
    joined[...] = back_raw[...]
    edge[0:HALO, :] = rim[...]
    edge[HALO:, :] = jnp.zeros((HALO, edge.shape[1]), F32)
    head = joined[0:HALO, :]
    for tap in range(taps):
        head = head + conv_w[tap : tap + 1, :] * edge[pl.ds(HALO - tap, HALO), :]
    joined[0:HALO, :] = head
    wide = (iota((LANES, HEADS), 0) == iota((LANES, HEADS), 1)).astype(BF16)
    w_dt_wide = dot(wide, w_dt[...]).astype(BF16)
    out[...] = (
        dot(joined[...].astype(BF16), w_in[...], 1, 1) + dot(step_grad[...], w_dt_wide)
    ).astype(BF16)


def swapped(x, axis="seq"):
    return lax.all_to_all(x, axis, split_axis=0, concat_axis=0, tiled=True)


def joint_kernel(blocks, keep, received, late, late_received, both):
    size = keep.shape[0] // blocks
    rows, width = late.shape[0], HEADS * HDIM
    sums = late[...] + late_received[...]
    facts = sums[:, width : width + LANES]
    rest = pltpu.roll(facts - facts.astype(BF16).astype(F32), 1, 0)
    row = iota(facts.shape, 0)
    facts = jnp.where(row == HEADS - 3, rest, facts)
    sums = jnp.concatenate([sums[:, :width], facts, sums[:, width + LANES :]], axis=1).astype(BF16)
    for block in range(blocks):
        base, at = block * (size + rows), slice(block * size, (block + 1) * size)
        both[base : base + size, :] = (
            keep[at, :].astype(F32) + received[at, :].astype(F32)
        ).astype(BF16)
        both[base + size : base + size + rows, :] = sums


def joint_sums_kernel(
    share, rows_in_all, place, parts, w_out, w_cls,
    grad_w_in, grad_conv, grad_dt_t, grad_heads, gain, cls_t, loss, grad_w_out, early, product,
):
    total = parts[0].astype(F32)
    for chip in range(1, parts.shape[0]):
        total = total + parts[chip].astype(F32)
    size, taps, width = grad_w_in.shape[0], grad_conv.shape[0], HEADS * HDIM
    grad_w_in[...] = total[0:size]
    grad_conv[...] = total[size + HEADS : size + HEADS + taps]
    grad_dt_t[...] = total[size : size + HEADS, 0:width]
    at = size + HEADS - 4
    facts = total[at : at + 1, width : width + LANES] + total[at + 1 : at + 2, width : width + LANES]
    for row in range(3):
        moved = pltpu.roll(facts, (LANES - 16 * row) % LANES, 1) if row else facts
        grad_heads[row : row + 1, :] = moved[:, 0:HEADS]
    loss[...] = pltpu.roll(facts, LANES - 48, 1)[:, 0:1] / rows_in_all
    for chip in range(parts.shape[0]):
        for side in (0, 1):
            base = (2 * chip + side) * share
            lanes = slice(width + side * LANES, width + (side + 1) * LANES)
            early[base : base + share, :] = parts[chip][size : size + share, lanes].astype(F32)
    count = width // LANES
    for block in range(count):
        lanes = slice(block * LANES, (block + 1) * LANES)
        product[:, lanes] = early[block * LABELS : (block + 1) * LABELS, :].astype(BF16)
        gain[lanes] = early[count * LABELS + block, :]
    cls_t[...] = dot(product[...], w_out[...])
    own = (iota((size, width), 1) == iota((size, width), 0) + place[0] * size).astype(F32)
    rows = dot(own.astype(BF16), product[...], 1, 1).astype(BF16)
    grad_w_out[...] = dot(rows, w_cls[...])


def exchanged(both, devices):
    groups = [[i for i in range(devices) if i % 2 == side] for side in (0, 1)]
    parts = lax.all_to_all(
        both, "seq", split_axis=0, concat_axis=0, axis_index_groups=groups, tiled=True
    )
    return parts.reshape(devices // 2, -1, both.shape[1])


def per_device(
    hidden_in, w_in, w_dt, dt_bias, a_log, conv_w, d_skip, norm_gain, w_out, w_cls,
    teacher_rows, w_teacher, row_dest, row_start, row_len,
):
    devices = lax.axis_size("seq")
    length = hidden_in.shape[0]
    width = HEADS * HDIM
    channels = w_in.shape[1]
    slice_rows = STATE // devices
    row_count = teacher_rows.shape[0]
    place = lax.axis_index("seq").astype(jnp.int32).reshape(1)

    edge = passed_along(hidden_in[:HALO], "seq", -1)
    extra, own = call(
        functools.partial(teacher_kernel, slice_rows),
        [((STATE, LANES), BF16), ((1, LANES), F32)],
        teacher_rows, w_teacher.T, row_dest.reshape(1, row_count),
        row_start.reshape(1, row_count), row_len.reshape(1, row_count),
        fetch=range(5), leave=(1,),
    )
    w_dt_t = w_dt.T
    a_log_row = a_log.reshape(1, HEADS)
    skip_row = d_skip.reshape(1, HEADS)
    message, mixed, raw, step, run, run_t = call(
        front_kernel,
        [
            ((STATE, width + LANES), BF16),
            ((length, channels), BF16),
            ((length + HALO, channels), BF16),
            ((length, 2 * LANES), F32),
            ((length, LANES), F32),
            ((LANES, length), F32),
        ],
        edge, hidden_in, w_dt_t, dt_bias.reshape(1, HEADS), a_log_row, w_in, conv_w, extra,
        scratch=[pltpu.VMEM((length + HALO, channels), F32)], fetch=range(1, 7), leave=(0, 2),
    )
    arrived = swapped(message).reshape(devices, slice_rows, width + LANES)
    (local,) = call(local_kernel, [((length, width), F32)], mixed, step, run, run_t)
    onward, decay = call(
        states_kernel,
        [((devices, slice_rows, width), BF16), ((devices, slice_rows, LANES), F32)],
        arrived,
        leave=(0,),
        after=[local],
    )
    state = swapped(onward.reshape(STATE, width))
    target, labels_high, labels_low = call(
        target_kernel,
        [((length, LANES), F32), ((LANES, width), BF16), ((LANES, width), BF16)],
        arrived, w_cls.T, w_out,
        fetch=(1, 2),
    )

    back_state, grad_scanned, normed, back_logits, carried_grad, small = call(
        middle_kernel,
        [
            ((STATE, width), BF16),
            ((length, width), F32),
            ((length, width), BF16),
            ((length, LANES), F32),
            ((length, LANES), F32),
            ((8, width), F32),
        ],
        state, mixed, run, local, skip_row, norm_gain, labels_high, labels_low, target,
        fetch=(4, 5), leave=(0, 2, 3, 5),
    )
    back_arrived = swapped(back_state).reshape(devices, slice_rows, width)
    values_local, maps, run_grad, step_local, early = call(
        local_back_kernel,
        [
            ((length, width), F32),
            ((length, 2 * STATE), F32),
            ((length, LANES), F32),
            ((length, LANES), F32),
            ((STATE, LANES), F32),
        ],
        mixed, step, run, grad_scanned, skip_row, state, carried_grad, normed, back_logits, small,
        scratch=[pltpu.VMEM((length, width), F32)], fetch=(4, 7, 8, 9), leave=(1, 3),
    )
    (back_onward,) = call(
        state_grads_kernel,
        [((devices, slice_rows, width + LANES), BF16)],
        back_arrived, decay, early,
        leave=(0,),
    )
    state_grad = swapped(back_onward.reshape(STATE, width + LANES))

    keep_in, send_in, rim, back_raw, step_grad, late = call(
        functools.partial(last_kernel, devices),
        [
            ((width // 2, channels), BF16),
            ((width // 2, channels), BF16),
            ((HALO, channels), F32),
            ((length, channels), F32),
            ((length, LANES), BF16),
            ((HEADS + conv_w.shape[0], channels), F32),
        ],
        place, state_grad, edge, run, mixed, step, state, run_grad, step_local, a_log_row, conv_w,
        values_local, maps, raw, hidden_in, small, own,
        scratch=[
            pltpu.VMEM((width, channels), F32),
            pltpu.VMEM((length + 2 * HALO, channels), F32),
            pltpu.VMEM((length + HALO, channels), F32),
        ],
        scalars=1, fetch=(8, 9, 10, 12, 13, 14, 15, 16), leave=(1, 2, 3, 4),
    )
    chips = devices // 2
    (both_in,) = call(
        functools.partial(joint_kernel, chips),
        [((width // 2 + chips * late.shape[0], channels), BF16)],
        keep_in, partner(send_in, "seq", 0), late, partner(late, "seq", 0),
        leave=(0,),
    )
    parts = exchanged(both_in, devices)
    (grad_hidden,) = call(
        hidden_kernel,
        [((length, w_in.shape[0]), BF16)],
        passed_along(rim, "seq", 1), back_raw, conv_w, step_grad, w_dt_t, w_in,
        scratch=[pltpu.VMEM((length, channels), F32), pltpu.VMEM((2 * HALO, channels), F32)],
        fetch=range(1, 6), leave=(0,),
    )
    grad_w_in, grad_conv, grad_dt_t, grad_heads, gain, cls_t, loss, grad_w_out = call(
        functools.partial(joint_sums_kernel, slice_rows, float(row_count * devices)),
        [
            ((width // devices, channels), F32),
            (conv_w.shape, F32),
            ((HEADS, width), F32),
            ((3, HEADS), F32),
            ((width,), F32),
            ((LABELS, width), F32),
            ((1, 1), F32),
            ((width // devices, width), F32),
        ],
        place, parts, w_out, w_cls.T,
        scratch=[pltpu.VMEM((STATE, LANES), F32), pltpu.VMEM((LABELS, width), BF16)],
        scalars=1, leave=range(8),
    )
    return (
        grad_hidden,
        grad_w_in,
        grad_w_out,
        grad_conv,
        grad_dt_t.T,
        grad_heads,
        gain,
        cls_t.T,
        loss.reshape(1),
    )


def solution(mesh):
    rows = P(("grp", "seq"), None)
    placed = (rows,) + (P(),) * 9 + (rows, P(), rows, P(("grp", "seq")), P(("grp", "seq")))
    part = P("grp", None)
    return jax.shard_map(
        per_device,
        mesh=mesh,
        in_specs=placed,
        out_specs=(rows, rows, rows, part, part, part, P("grp"), part, P("grp")),
        check_vma=False,
    )
```

```python
import functools

import jax
import jax.numpy as jnp
from jax import lax
from jax.experimental import pallas as pl
from jax.experimental.pallas import tpu as pltpu
from jax.sharding import PartitionSpec as P

HEADS = 12
HDIM = 64
STATE = 128
LABELS = 16
LANES = 128
HALO = 8
TAGS = 48
FACTS = 40
EPSILON = 1e-05
FAR = -1e30

F32 = jnp.float32
BF16 = jnp.bfloat16


def partner(x, axis, apart):
    return lax.ppermute(x, axis, [(i, i ^ 1 << apart) for i in range(lax.axis_size(axis))])


def passed_along(x, axis, by):
    length = lax.axis_size(axis)
    pairs = [(i, i + by) for i in range(length) if 0 <= i + by < length]
    return lax.ppermute(x, axis, pairs)


def dot(a, b, left=1, right=0):
    return lax.dot_general(a, b, (((left,), (right,)), ((), ())), preferred_element_type=F32)


def pieces(x, count):
    parts = []
    for _ in range(count):
        part = x.astype(BF16)
        parts.append(part)
        x = x - part.astype(F32)
    return parts


def finer(a, x, count, left=1, right=0):
    return sum(dot(a, part, left, right) for part in pieces(x, count))


def iota(shape, axis):
    return lax.broadcasted_iota(jnp.int32, shape, axis)


def spread_heads(x):
    rows = x.shape[0]
    first = iota((rows, LANES), 1) < HDIM
    return jnp.concatenate(
        [
            jnp.where(
                first,
                jnp.broadcast_to(x[:, 2 * pair : 2 * pair + 1], (rows, LANES)),
                jnp.broadcast_to(x[:, 2 * pair + 1 : 2 * pair + 2], (rows, LANES)),
            )
            for pair in range(HEADS // 2)
        ],
        axis=1,
    )


def head_sums(x):
    width = x.shape[1]
    member = (iota((width, LANES), 0) // HDIM == iota((width, LANES), 1)).astype(BF16)
    return sum(dot(part, member) for part in pieces(x, 2))


class Fetched:
    def __init__(self, ref, copy):
        self.ref, self.copy, self.shape = ref, copy, ref.shape

    def ready(self):
        if self.copy is not None:
            self.copy.wait()
            self.copy = None
        return self.ref

    def __getitem__(self, at):
        return self.ready()[at]


class Result:
    def __init__(self, ref, copy):
        self.ref, self.copy, self.shape, self.sent = ref, copy, ref.shape, False

    def __getitem__(self, at):
        return self.ref[at]

    def __setitem__(self, at, value):
        self.ref[at] = value

    def send(self):
        self.copy.start()
        self.sent = True


class Kept:
    def __init__(self, ref):
        self.ref, self.shape = ref, ref.shape

    def __getitem__(self, at):
        return self.ref[at]

    def __setitem__(self, at, value):
        self.ref[at] = value

    def send(self):
        pass


def call(body, outs, *args, scratch=(), scalars=0, fetch=(), leave=(), after=(), wait=(), into=()):
    waits = len(after) + len(wait)
    fetch = sorted(fetch)

    def kernel(*refs):
        refs = list(refs)

        def take(count):
            taken = refs[:count]
            del refs[:count]
            return taken

        inputs = take(len(args))
        take(waits)
        results = take(len(outs))
        places, outputs, extra = take(len(fetch) - len(into)), take(len(leave)), take(len(scratch))
        places = places + results[len(results) - len(into) :]
        arrivals, departures = refs
        for i, (at, place) in enumerate(zip(fetch, places)):
            copy = pltpu.make_async_copy(inputs[at], place, arrivals.at[i])
            copy.start()
            inputs[at] = Fetched(place, copy)
        written = []
        for i, result in enumerate(results):
            if i in leave:
                at = leave.index(i)
                copy = pltpu.make_async_copy(outputs[at], result, departures.at[at])
                written.append(Result(outputs[at], copy))
            else:
                written.append(Kept(result))
        body(*inputs, *written, *extra)
        for at in fetch:
            inputs[at].ready()
        gone = [result for result in written if isinstance(result, Result)]
        for result in gone:
            if not result.sent:
                result.send()
        for result in gone:
            result.copy.wait()

    far, close = pltpu.HBM, pltpu.VMEM
    specs, given = [], []
    for i, arg in enumerate(args):
        if i < scalars:
            specs.append(pl.BlockSpec(memory_space=pltpu.SMEM))
            given.append(arg)
        else:
            space = far if i in fetch else close
            specs.append(pl.BlockSpec(memory_space=space))
            given.append(pltpu.with_memory_space_constraint(arg, space))
    for space, arrays in ((close, after), (far, wait)):
        for arg in arrays:
            specs.append(pl.BlockSpec(memory_space=space))
            given.append(pltpu.with_memory_space_constraint(arg, space))
    return pl.pallas_call(
        kernel,
        out_shape=[(far if i in leave else close)(*out) for i, out in enumerate(outs)],
        in_specs=specs,
        out_specs=[pl.BlockSpec(memory_space=far if i in leave else close) for i in range(len(outs))],
        scratch_shapes=[
            *(pltpu.VMEM(args[i].shape, args[i].dtype) for i in fetch[: len(fetch) - len(into)]),
            *(pltpu.VMEM(*outs[i]) for i in leave),
            *scratch,
            pltpu.SemaphoreType.DMA((max(len(fetch), 1),)),
            pltpu.SemaphoreType.DMA((max(len(leave), 1),)),
        ],
        compiler_params=pltpu.CompilerParams(vmem_limit_bytes=24 * 1024 * 1024),
    )(*given)


def widened(x):
    place = (iota((HEADS, LANES), 0) == iota((HEADS, LANES), 1)).astype(BF16)
    return sum(dot(part, place) for part in pieces(x, 3))


def teacher_kernel(slice_rows, rows, weights, dest, start, size, hidden, w_in, extra, own, *brought):
    count = rows.shape[0]
    row, lane = iota((count, count), 0), iota((count, count), 1)
    named = dest[...].astype(F32)
    facts = jnp.where(
        row == 0, named, jnp.where(row == 1, start[...].astype(F32), size[...].astype(F32))
    ).T
    spans = facts[:, 2:3]
    slot = jnp.sum(
        jnp.where((facts[:, 0:1] == named) & (row < lane), 1.0, 0.0), axis=0, keepdims=True
    ).astype(jnp.int32)
    logits = dot(rows[...], weights[...], 1, 1)
    top = jnp.max(logits, axis=1, keepdims=True)
    shifted = logits - top
    logp = shifted - jnp.log(jnp.sum(jnp.exp(shifted), axis=1, keepdims=True))
    prob = jnp.exp(logp)
    label, spot = iota((LABELS, LANES), 0), iota((LABELS, LANES), 1)
    total = jnp.zeros((STATE, LANES), F32)
    for group in range(2):
        base = TAGS + group * FACTS
        inside = sum(
            dot(part, (spot == label + base + i * LABELS).astype(BF16))
            for i, part in enumerate(pieces(prob, 2))
        )
        spare = base + 2 * LABELS
        inside = jnp.where(lane == spare, facts[:, 1:2], inside)
        inside = jnp.where(lane == spare + 1, spans, inside)
        inside = jnp.where(lane == spare + 2, 1.0, inside)
        where_to = dest[...] * slice_rows + slot - group * slice_rows
        fits = (slot >= group * slice_rows) & (slot < (group + 1) * slice_rows)
        chosen = (iota((STATE, count), 0) == jnp.where(fits, where_to, -1)).astype(F32)
        total = total + dot(chosen.astype(BF16), inside.astype(BF16))
    extra[...] = total.astype(BF16)
    gained = jnp.sum(prob * logp, axis=1, keepdims=True) * spans
    own[...] = jnp.where(lane[0:1] == 0, jnp.sum(gained, axis=0, keepdims=True), 0.0)


def target_kernel(arrived, w_cls, w_out, target, joined_high, joined_low):
    length = target.shape[0]
    width = HEADS * HDIM
    count, rows = arrived.shape[0], arrived.shape[1]
    facts = arrived[:, :, width:].astype(F32).reshape(count * rows, LANES).astype(BF16)
    facts_f = facts.astype(F32)
    position = iota((count * rows, length), 1).astype(F32)
    total = jnp.zeros((length, LANES), F32)
    for group in range(2):
        base = TAGS + group * FACTS
        spare = base + 2 * LABELS
        start = facts_f[:, spare : spare + 1]
        stop = start + facts_f[:, spare + 1 : spare + 2]
        covered = jnp.where((position >= start) & (position < stop), 1.0, 0.0).astype(BF16)
        sums = dot(covered, facts, 0, 0)
        lane = iota(sums.shape, 1)
        high = pltpu.roll(sums, LANES - base, 1)
        low = pltpu.roll(sums, LANES - base - LABELS, 1)
        cover = pltpu.roll(sums, (LABELS - spare - 2) % LANES, 1)
        total = total + jnp.where(lane < LABELS, high + low, jnp.where(lane == LABELS, cover, 0.0))
    target[...] = total
    place = (iota((LANES, LABELS), 0) == iota((LANES, LABELS), 1)).astype(BF16)
    joined = dot(dot(place, w_cls[...]).astype(BF16), w_out[...], 1, 1)
    joined_high[...], joined_low[...] = pieces(joined, 2)


def convolved(raw, conv_w, length):
    conv = conv_w[0:1, :] * raw[0:length, :]
    for tap in range(1, conv_w.shape[0]):
        conv = conv + conv_w[tap : tap + 1, :] * raw[pl.ds(tap, length), :]
    return conv


def front_kernel(
    edge, hidden, w_dt, dt_bias, a_log, w_in, conv_w, extra,
    message, mixed_o, raw_o, step_o, run_o, run_t, raw,
):
    length = hidden.shape[0]
    weights = w_in[...]
    raw_o[0:length, :] = dot(hidden[...], weights).astype(BF16)
    raw_o[length:, :] = dot(edge[...], weights).astype(BF16)
    raw_o.send()
    wide = (iota((LANES, HEADS), 0) == iota((LANES, HEADS), 1)).astype(BF16)
    w_dt_wide = dot(wide, w_dt[...]).astype(BF16)
    before = dot(hidden[...], w_dt_wide, 1, 1) + widened(dt_bias[...])
    step = jnp.maximum(before, 0.0) + jnp.log1p(jnp.exp(-jnp.abs(before)))
    step = jnp.where(iota((length, LANES), 1) < HEADS, step, 0.0)
    log_decay = -step * jnp.exp(widened(a_log[...]))
    later = (iota((length, length), 1) >= iota((length, length), 0)).astype(BF16)
    run = finer(later, log_decay, 3)
    step_o[:, 0:LANES] = step
    step_o[:, LANES:] = before
    run_o[...] = run
    run_t[...] = run.T
    for result in (step_o, run_o, run_t):
        result.send()
    raw[...] = raw_o[...].astype(F32)
    conv = convolved(raw, conv_w, length)
    mixed = (conv / (1.0 + jnp.exp(-conv))).astype(BF16)
    mixed_o[...] = mixed
    mixed_o.send()
    width = HEADS * HDIM
    total = run[0:1, :]
    weighted = mixed[:, :width].astype(F32) * spread_heads(step * jnp.exp(total - run))
    state = dot(mixed[:, width : width + STATE], weighted.astype(BF16), 0, 0)
    message[:, :width] = state.astype(BF16)
    high, middle, low = (part.astype(F32) for part in pieces(total, 3))
    tags = high + pltpu.roll(middle, 16, 1) + pltpu.roll(low, 32, 1)
    message[:, width:] = (extra[...].astype(F32) + tags).astype(BF16)


def decay_blocks(run, run_t, head, half):
    top = run[0:half, head : head + 1] - run_t[head : head + 1, :]
    low = run[half:, head : head + 1] - run_t[head : head + 1, half:]
    top_seen = iota(top.shape, 1) >= iota(top.shape, 0)
    low_seen = iota(low.shape, 1) >= iota(low.shape, 0)
    return jnp.exp(jnp.where(top_seen, top, FAR)), jnp.exp(jnp.where(low_seen, low, FAR))


def local_kernel(
    mixed, step, run, run_t, d_skip, raw_b, conv_w, hidden,
    local, slope, tail_values, tail_steps, tail_weighted, hidden_t, raw,
):
    length = mixed.shape[0]
    half = length // 2
    width = HEADS * HDIM
    in_map = mixed[:, width : width + STATE]
    out_map = mixed[:, width + STATE :]
    top_scores = dot(out_map[0:half], in_map, 1, 1)
    low_scores = dot(out_map[half:], in_map[half:], 1, 1)
    weighted = (mixed[:, :width].astype(F32) * spread_heads(step[:, 0:LANES])).astype(BF16)
    first = iota((half, LANES), 1) < HDIM
    for pair in range(HEADS // 2):
        lanes = slice(pair * LANES, (pair + 1) * LANES)
        own = weighted[:, lanes]
        tops, lows = [], []
        for head in (2 * pair, 2 * pair + 1):
            top, low = decay_blocks(run, run_t, head, half)
            tops.append(dot((top * top_scores).astype(BF16), own))
            lows.append(dot((low * low_scores).astype(BF16), own[half:]))
        local[0:half, lanes] = jnp.where(first, tops[0], tops[1])
        local[half:, lanes] = jnp.where(first, lows[0], lows[1])
    local[...] = local[...] + spread_heads(d_skip[...]) * mixed[:, :width].astype(F32)
    hidden_t[...] = hidden[...].astype(F32).T.astype(BF16)
    hidden_t.send()
    tail = spread_heads(jnp.exp(run[0:1, :] - run[...]))
    steps = spread_heads(step[:, 0:LANES])
    reaching = tail * mixed[:, :width].astype(F32)
    tail_values[...] = reaching
    tail_values.send()
    tail_steps[...] = tail * steps
    tail_steps.send()
    tail_weighted[...] = (reaching * steps).astype(BF16)
    tail_weighted.send()
    raw[...] = raw_b[...].astype(F32)
    inner = convolved(raw, conv_w, length)
    gate = 1.0 / (1.0 + jnp.exp(-inner))
    slope[...] = gate * (1.0 + inner * (1.0 - gate))


def states_kernel(arrived, onward, decay):
    count = arrived.shape[0]
    width = HEADS * HDIM
    rows = arrived.shape[1]
    keep = iota((rows, LANES), 1) < HEADS
    state = jnp.zeros((rows, width), F32)
    for source in range(count - 1, -1, -1):
        onward[source] = state.astype(BF16)
        tags = arrived[source, :, width:].astype(F32)
        total = tags + pltpu.roll(tags, LANES - 16, 1) + pltpu.roll(tags, LANES - 32, 1)
        factor = jnp.exp(jnp.where(keep, total, 0.0))
        decay[source] = factor
        state = arrived[source, :, :width].astype(F32) + spread_heads(factor) * state


def state_grads_kernel(arrived, decay, early, onward):
    count, rows, width = arrived.shape
    state = jnp.zeros(arrived.shape[1:], F32)
    for source in range(count):
        onward[source, :, :width] = state.astype(BF16)
        onward[source, :, width:] = early[source * rows : (source + 1) * rows, :].astype(BF16)
        state = arrived[source].astype(F32) + spread_heads(decay[source]) * state


def middle_kernel(
    state, mixed, run, local, gains, high, low, target,
    back_state, grad_scanned, normed_o, logits_o, run_grad, small,
):
    length = mixed.shape[0]
    width = HEADS * HDIM
    values = mixed[:, :width].astype(F32)
    out_map = mixed[:, width + STATE :]
    reach = spread_heads(jnp.exp(run[...]))
    carried = dot(out_map, state[...]) * reach
    scanned = local[...] + carried
    scale = lax.rsqrt(jnp.mean(scanned * scanned, axis=1, keepdims=True) + EPSILON)
    plain = scanned * scale
    gain = gains[...].reshape(1, width)
    normed = (plain * gain).astype(BF16)
    normed_o[...] = normed
    normed_o.send()
    label = iota((length, LANES), 1) < LABELS
    logits = jnp.where(label, dot(normed, high[...], 1, 1) + dot(normed, low[...], 1, 1), FAR)
    shifted = logits - jnp.max(logits, axis=1, keepdims=True)
    raised = jnp.exp(shifted)
    whole = jnp.sum(raised, axis=1, keepdims=True)
    logp = shifted - jnp.log(whole)
    wanted = target[...]
    cover = wanted[:, LABELS : LABELS + 1]
    back_logits = jnp.where(label, cover * (raised / whole) - wanted, 0.0)
    logits_o[...] = back_logits
    logits_o.send()
    lost = jnp.sum(jnp.where(label, wanted * logp, 0.0), axis=0, keepdims=True)
    back_high, back_low = pieces(back_logits, 2)
    back_normed = dot(back_high, high[...]) + dot(back_low, high[...]) + dot(back_high, low[...])
    back_plain = back_normed * gain
    along = jnp.mean(back_plain * plain, axis=1, keepdims=True)
    back = scale * (back_plain - plain * along)
    grad_scanned[...] = back
    back_state[...] = dot(out_map, (back * reach).astype(BF16), 0, 0).astype(BF16)
    back_state.send()
    small[0:1, :] = jnp.sum(back_normed * plain, axis=0, keepdims=True)
    small[1:2, :] = jnp.sum(back * values, axis=0, keepdims=True)
    small[2:3, :] = jnp.zeros((1, width), F32)
    small[2:3, 0:LANES] = lost
    small[3:, :] = jnp.zeros((5, width), F32)
    small.send()
    run_grad[...] = head_sums(back * carried)


def halves(full, keep, send, odd, blocks):
    size = full.shape[0] // blocks
    for side in (0, 1):

        @pl.when(odd == side)
        def _():
            for block in range(blocks // 2):
                at = slice(block * size, (block + 1) * size)
                mine = (2 * block + side) * size
                other = (2 * block + 1 - side) * size
                keep[at, :] = full[mine : mine + size, :].astype(BF16)
                send[at, :] = full[other : other + size, :].astype(BF16)


def local_back_kernel(
    mixed, step, run, grad_scanned, d_skip, state, carried_grad, normed, back_logits, small,
    values_grad, maps, run_grad, step_grad, early, weighted_grad,
):
    length = mixed.shape[0]
    half = length // 2
    width = HEADS * HDIM
    in_map = mixed[:, width : width + STATE]
    out_map = mixed[:, width + STATE :]
    top_scores = dot(out_map[0:half], in_map, 1, 1)
    low_scores = dot(out_map[half:], in_map[half:], 1, 1)
    values = mixed[:, :width].astype(F32)
    steps = spread_heads(step[:, 0:LANES])
    weighted = (values * steps).astype(BF16)
    run_t = run[...].T
    lane = iota((length, LANES), 1)
    back_top = jnp.zeros((half, length), F32)
    back_low = jnp.zeros((half, half), F32)
    rows_top = jnp.zeros((half, LANES), F32)
    rows_low = jnp.zeros((half, LANES), F32)
    columns = jnp.zeros((length, LANES), F32)
    columns_low = jnp.zeros((half, LANES), F32)
    for pair in range(HEADS // 2):
        lanes = slice(pair * LANES, (pair + 1) * LANES)
        own = weighted[:, lanes]
        back_f = grad_scanned[:, lanes]
        back = back_f.astype(BF16)
        tops, lows = [], []
        for side in (0, 1):
            head = 2 * pair + side
            top, low = decay_blocks(run, run_t, head, half)
            mine = jnp.where((lane >= HDIM) == (side == 1), back_f, 0.0).astype(BF16)
            mix_top = (top * top_scores).astype(BF16)
            mix_low = (low * low_scores).astype(BF16)
            tops.append(dot(mix_top, back[0:half], 0, 0))
            lows.append(dot(mix_low, back[half:], 0, 0))
            grad_top = top * dot(mine[0:half], own, 1, 1)
            grad_low = low * dot(mine[half:], own[half:], 1, 1)
            back_top = back_top + grad_top
            back_low = back_low + grad_low
            part_top = (grad_top * top_scores).astype(BF16)
            part_low = (grad_low * low_scores).astype(BF16)
            marker = (lane == head).astype(F32).astype(BF16)
            rows_top = rows_top + dot(part_top, marker)
            rows_low = rows_low + dot(part_low, marker[half:])
            columns = columns + dot(part_top, marker[0:half], 0, 0)
            columns_low = columns_low + dot(part_low, marker[half:], 0, 0)
        weighted_grad[0:half, lanes] = jnp.where(lane[0:half] < HDIM, tops[0][0:half], tops[1][0:half])
        weighted_grad[half:, lanes] = jnp.where(
            lane[half:] < HDIM, tops[0][half:] + lows[0], tops[1][half:] + lows[1]
        )
    back_top = back_top.astype(BF16)
    back_low = back_low.astype(BF16)
    values_grad[...] = weighted_grad[...] * steps + spread_heads(d_skip[...]) * grad_scanned[...]
    values_grad.send()
    step_grad[...] = head_sums(weighted_grad[...] * values)
    scaled = (grad_scanned[...] * spread_heads(jnp.exp(run[...]))).astype(BF16)
    from_state = dot(scaled, state[...], 1, 1)
    maps[0:half, STATE:] = dot(back_top, in_map) + from_state[0:half]
    maps[half:, STATE:] = dot(back_low, in_map[half:]) + from_state[half:]
    in_grad = dot(back_top, out_map[0:half], 0, 0)
    maps[0:half, 0:STATE] = in_grad[0:half]
    maps[half:, 0:STATE] = in_grad[half:] + dot(back_low, out_map[half:], 0, 0)
    run_grad[0:half, :] = carried_grad[0:half, :] + rows_top - columns[0:half]
    run_grad[half:, :] = carried_grad[half:, :] + rows_low - columns[half:] - columns_low
    product = sum(dot(part, normed[...], 0, 0) for part in pieces(back_logits[...], 2))[0:LABELS]
    count = width // LANES
    early[count * LABELS :, :] = jnp.zeros((early.shape[0] - count * LABELS, LANES), F32)
    for block in range(count):
        lanes = slice(block * LANES, (block + 1) * LANES)
        early[block * LABELS : (block + 1) * LABELS, :] = product[:, lanes]
        at = count * LABELS + block
        early[at : at + 1, :] = small[0:1, lanes]


def last_kernel(
    blocks, place, state_grad, edge, run, mixed, step, state, run_grad,
    tail_values, tail_weighted, step_local, a_log, conv_w, tail_steps, values_local, maps, slope, hidden_t,
    raw_b, small, own,
    keep, send, rim, back_raw_o, step_grad_o, late, full, padded, raw,
):
    length = mixed.shape[0]
    taps = conv_w.shape[0]
    width = HEADS * HDIM
    total = run[0:1, :]
    in_map = mixed[:, width : width + STATE]
    incoming = state_grad[:, :width]
    reached = dot(in_map, incoming)
    product = jnp.sum(incoming.astype(F32) * state[...].astype(F32), axis=0, keepdims=True)
    total_grad = jnp.exp(total) * head_sums(jnp.broadcast_to(product, (8, width)))[0:1]
    row, column = iota((length, length), 0), iota((length, length), 1)
    decay_grad = finer((column <= row).astype(BF16), run_grad[...], 3) + total_grad
    padded[0:HALO, :] = jnp.zeros((HALO, padded.shape[1]), F32)
    padded[HALO + length :, :] = jnp.zeros((HALO, padded.shape[1]), F32)
    reaching = head_sums(reached * tail_values[...])
    ended = reaching * step[:, 0:LANES]
    in_grad = dot(tail_weighted[...], incoming, 1, 1)
    decay_grad = decay_grad + finer((column > row).astype(BF16), ended, 3)
    rate = jnp.exp(widened(a_log[...]))
    step_grad = step_local[...] + reaching - rate * decay_grad
    before = step[:, LANES:]
    step_grad = jnp.where(
        iota((length, LANES), 1) < HEADS, step_grad / (1.0 + jnp.exp(-before)), 0.0
    )
    step_grad_b = step_grad.astype(BF16)
    step_grad_o[...] = step_grad_b
    middle = slice(HALO, HALO + length)
    padded[middle, 0:width] = (values_local[...] + reached * tail_steps[...]) * slope[:, 0:width]
    padded[middle, width : width + STATE] = (maps[:, 0:STATE] + in_grad) * slope[
        :, width : width + STATE
    ]
    padded[middle, width + STATE :] = maps[:, STATE:] * slope[:, width + STATE :]
    rim[...] = padded[length : length + HALO, :]
    rim.send()
    back_raw = jnp.zeros((length + HALO, padded.shape[1]), F32)
    for tap in range(taps):
        back_raw = back_raw + conv_w[tap : tap + 1, :] * padded[pl.ds(HALO - tap, length + HALO), :]
    back_raw_o[...] = back_raw[0:length]
    full[...] = dot(hidden_t[...], back_raw[0:length].astype(BF16)) + dot(
        edge[...], back_raw[length:].astype(BF16), 0, 0
    )
    halves(full, keep, send, place[0] % 2, blocks)
    send.send()
    back_raw_o.send()
    back_conv = padded[middle, :]
    raw[...] = raw_b[...].astype(F32)
    spare = late.shape[0] - taps
    for tap in range(taps):
        late[spare + tap : spare + tap + 1, :] = jnp.sum(
            back_conv * raw[pl.ds(tap, length), :], axis=0, keepdims=True
        )
    late[0:HEADS, 0:width] = dot(step_grad_b, hidden_t[...], 0, 1)[0:HEADS]
    late[0:HEADS, width:] = jnp.zeros((HEADS, late.shape[1] - width), F32)
    log_decay = -step[:, 0:LANES] * rate
    facts = jnp.sum(step_grad, axis=0, keepdims=True)
    facts = facts + pltpu.roll(jnp.sum(decay_grad * log_decay, axis=0, keepdims=True), 16, 1)
    skips = head_sums(jnp.broadcast_to(small[1:2, :], (8, width)))[0:1]
    lost = jnp.sum(own[...] - small[2:3, 0:LANES], axis=1, keepdims=True)
    lane = iota((1, LANES), 1)
    facts = facts + pltpu.roll(skips, 32, 1) + jnp.where(lane == 48, lost, 0.0)
    late[HEADS - 4 : HEADS - 3, width : width + LANES] = facts
    shares = state_grad[:, width:].astype(F32)
    rows = shares.shape[0] // blocks
    share = sum(shares[source * rows : (source + 1) * rows] for source in range(blocks))
    for side in (0, 1):

        @pl.when(place[0] % 2 == side)
        def _():
            late[0:rows, width + side * LANES : width + (side + 1) * LANES] = share


def hidden_kernel(rim, back_raw, conv_w, step_grad, w_dt, w_in, out, joined, edge):
    taps = conv_w.shape[0]
    joined[...] = back_raw[...]
    edge[0:HALO, :] = rim[...]
    edge[HALO:, :] = jnp.zeros((HALO, edge.shape[1]), F32)
    head = joined[0:HALO, :]
    for tap in range(taps):
        head = head + conv_w[tap : tap + 1, :] * edge[pl.ds(HALO - tap, HALO), :]
    joined[0:HALO, :] = head
    wide = (iota((LANES, HEADS), 0) == iota((LANES, HEADS), 1)).astype(BF16)
    w_dt_wide = dot(wide, w_dt[...]).astype(BF16)
    out[...] = (
        dot(joined[...].astype(BF16), w_in[...], 1, 1) + dot(step_grad[...], w_dt_wide)
    ).astype(BF16)


def swapped(x, axis="seq"):
    return lax.all_to_all(x, axis, split_axis=0, concat_axis=0, tiled=True)


def joint_kernel(blocks, keep, received, late, late_received, both):
    size = keep.shape[0] // blocks
    rows, width = late.shape[0], HEADS * HDIM
    sums = late[...] + late_received[...]
    facts = sums[:, width : width + LANES]
    rest = pltpu.roll(facts - facts.astype(BF16).astype(F32), 1, 0)
    row = iota(facts.shape, 0)
    facts = jnp.where(row == HEADS - 3, rest, facts)
    sums = jnp.concatenate([sums[:, :width], facts, sums[:, width + LANES :]], axis=1).astype(BF16)
    for block in range(blocks):
        base, at = block * (size + rows), slice(block * size, (block + 1) * size)
        both[base : base + size, :] = (
            keep[at, :].astype(F32) + received[at, :].astype(F32)
        ).astype(BF16)
        both[base + size : base + size + rows, :] = sums


def joint_sums_kernel(
    share, rows_in_all, place, parts, w_out, w_cls,
    grad_w_in, grad_conv, grad_dt_t, grad_heads, gain, cls_t, loss, grad_w_out, early, product,
):
    total = parts[0].astype(F32)
    for chip in range(1, parts.shape[0]):
        total = total + parts[chip].astype(F32)
    size, taps, width = grad_w_in.shape[0], grad_conv.shape[0], HEADS * HDIM
    grad_w_in[...] = total[0:size]
    grad_conv[...] = total[size + HEADS : size + HEADS + taps]
    grad_dt_t[...] = total[size : size + HEADS, 0:width]
    at = size + HEADS - 4
    facts = total[at : at + 1, width : width + LANES] + total[at + 1 : at + 2, width : width + LANES]
    for row in range(3):
        moved = pltpu.roll(facts, (LANES - 16 * row) % LANES, 1) if row else facts
        grad_heads[row : row + 1, :] = moved[:, 0:HEADS]
    loss[...] = pltpu.roll(facts, LANES - 48, 1)[:, 0:1] / rows_in_all
    for chip in range(parts.shape[0]):
        for side in (0, 1):
            base = (2 * chip + side) * share
            lanes = slice(width + side * LANES, width + (side + 1) * LANES)
            early[base : base + share, :] = parts[chip][size : size + share, lanes].astype(F32)
    count = width // LANES
    for block in range(count):
        lanes = slice(block * LANES, (block + 1) * LANES)
        product[:, lanes] = early[block * LABELS : (block + 1) * LABELS, :].astype(BF16)
        gain[lanes] = early[count * LABELS + block, :]
    cls_t[...] = dot(product[...], w_out[...])
    own = (iota((size, width), 1) == iota((size, width), 0) + place[0] * size).astype(F32)
    rows = dot(own.astype(BF16), product[...], 1, 1).astype(BF16)
    grad_w_out[...] = dot(rows, w_cls[...])


def exchanged(both, devices):
    groups = [[i for i in range(devices) if i % 2 == side] for side in (0, 1)]
    parts = lax.all_to_all(
        both, "seq", split_axis=0, concat_axis=0, axis_index_groups=groups, tiled=True
    )
    return parts.reshape(devices // 2, -1, both.shape[1])


def per_device(
    hidden_in, w_in, w_dt, dt_bias, a_log, conv_w, d_skip, norm_gain, w_out, w_cls,
    teacher_rows, w_teacher, row_dest, row_start, row_len,
):
    devices = lax.axis_size("seq")
    length = hidden_in.shape[0]
    width = HEADS * HDIM
    channels = w_in.shape[1]
    slice_rows = STATE // devices
    row_count = teacher_rows.shape[0]
    place = lax.axis_index("seq").astype(jnp.int32).reshape(1)

    edge = passed_along(hidden_in[:HALO], "seq", -1)
    extra, own, hidden_near, w_in_near = call(
        functools.partial(teacher_kernel, slice_rows),
        [
            ((STATE, LANES), BF16),
            ((1, LANES), F32),
            (hidden_in.shape, BF16),
            (w_in.shape, BF16),
        ],
        teacher_rows, w_teacher.T, row_dest.reshape(1, row_count),
        row_start.reshape(1, row_count), row_len.reshape(1, row_count), hidden_in, w_in,
        fetch=range(7), leave=(1,), into=(5, 6),
    )
    w_dt_t = w_dt.T
    a_log_row = a_log.reshape(1, HEADS)
    skip_row = d_skip.reshape(1, HEADS)
    message, mixed, raw, step, run, run_t = call(
        front_kernel,
        [
            ((STATE, width + LANES), BF16),
            ((length, channels), BF16),
            ((length + HALO, channels), BF16),
            ((length, 2 * LANES), F32),
            ((length, LANES), F32),
            ((LANES, length), F32),
        ],
        edge, hidden_near, w_dt_t, dt_bias.reshape(1, HEADS), a_log_row, w_in_near, conv_w, extra,
        scratch=[pltpu.VMEM((length + HALO, channels), F32)], fetch=(2, 3, 4, 6), leave=(0, 2),
    )
    arrived = swapped(message).reshape(devices, slice_rows, width + LANES)
    local, slope, tail_values, tail_steps, tail_weighted, hidden_t = call(
        local_kernel,
        [
            ((length, width), F32),
            ((length, channels), F32),
            ((length, width), F32),
            ((length, width), F32),
            ((length, width), BF16),
            ((hidden_in.shape[1], length), BF16),
        ],
        mixed, step, run, run_t, skip_row, raw, conv_w, hidden_in,
        scratch=[pltpu.VMEM((length + HALO, channels), F32)],
        fetch=(4, 5, 6, 7), leave=(1, 2, 3, 4, 5),
    )
    onward, decay = call(
        states_kernel,
        [((devices, slice_rows, width), BF16), ((devices, slice_rows, LANES), F32)],
        arrived,
        leave=(0,),
        after=[local],
    )
    state = swapped(onward.reshape(STATE, width))
    target, labels_high, labels_low = call(
        target_kernel,
        [((length, LANES), F32), ((LANES, width), BF16), ((LANES, width), BF16)],
        arrived, w_cls.T, w_out,
        fetch=(1, 2), leave=(0,),
    )

    back_state, grad_scanned, normed, back_logits, carried_grad, small = call(
        middle_kernel,
        [
            ((STATE, width), BF16),
            ((length, width), F32),
            ((length, width), BF16),
            ((length, LANES), F32),
            ((length, LANES), F32),
            ((8, width), F32),
        ],
        state, mixed, run, local, norm_gain, labels_high, labels_low, target,
        fetch=(4, 7), leave=(0, 2, 3, 5),
    )
    back_arrived = swapped(back_state).reshape(devices, slice_rows, width)
    values_local, maps, run_grad, step_local, early = call(
        local_back_kernel,
        [
            ((length, width), F32),
            ((length, 2 * STATE), F32),
            ((length, LANES), F32),
            ((length, LANES), F32),
            ((STATE, LANES), F32),
        ],
        mixed, step, run, grad_scanned, skip_row, state, carried_grad, normed, back_logits, small,
        scratch=[pltpu.VMEM((length, width), F32)], fetch=(4, 7, 8, 9), leave=(1, 3),
    )
    (back_onward,) = call(
        state_grads_kernel,
        [((devices, slice_rows, width + LANES), BF16)],
        back_arrived, decay, early,
        leave=(0,),
    )
    state_grad = swapped(back_onward.reshape(STATE, width + LANES))

    keep_in, send_in, rim, back_raw, step_grad, late = call(
        functools.partial(last_kernel, devices),
        [
            ((width // 2, channels), BF16),
            ((width // 2, channels), BF16),
            ((HALO, channels), F32),
            ((length, channels), F32),
            ((length, LANES), BF16),
            ((HEADS + conv_w.shape[0], channels), F32),
        ],
        place, state_grad, edge, run, mixed, step, state, run_grad,
        tail_values, tail_weighted, step_local, a_log_row, conv_w, tail_steps, values_local, maps, slope,
        hidden_t, raw, small, own,
        scratch=[
            pltpu.VMEM((width, channels), F32),
            pltpu.VMEM((length + 2 * HALO, channels), F32),
            pltpu.VMEM((length + HALO, channels), F32),
        ],
        scalars=1, fetch=(8, 9, 10, 11, 12, 13, 15, 16, 17, 18, 19, 20), leave=(1, 2, 3, 4),
    )
    chips = devices // 2
    (both_in,) = call(
        functools.partial(joint_kernel, chips),
        [((width // 2 + chips * late.shape[0], channels), BF16)],
        keep_in, partner(send_in, "seq", 0), late, partner(late, "seq", 0),
        leave=(0,),
    )
    parts = exchanged(both_in, devices)
    (grad_hidden,) = call(
        hidden_kernel,
        [((length, w_in.shape[0]), BF16)],
        passed_along(rim, "seq", 1), back_raw, conv_w, step_grad, w_dt_t, w_in,
        scratch=[pltpu.VMEM((length, channels), F32), pltpu.VMEM((2 * HALO, channels), F32)],
        fetch=range(1, 6), leave=(0,),
    )
    grad_w_in, grad_conv, grad_dt_t, grad_heads, gain, cls_t, loss, grad_w_out = call(
        functools.partial(joint_sums_kernel, slice_rows, float(row_count * devices)),
        [
            ((width // devices, channels), F32),
            (conv_w.shape, F32),
            ((HEADS, width), F32),
            ((3, HEADS), F32),
            ((width,), F32),
            ((LABELS, width), F32),
            ((1, 1), F32),
            ((width // devices, width), F32),
        ],
        place, parts, w_out, w_cls.T,
        scratch=[pltpu.VMEM((STATE, LANES), F32), pltpu.VMEM((LABELS, width), BF16)],
        scalars=1, leave=range(8),
    )
    return (
        grad_hidden,
        grad_w_in,
        grad_w_out,
        grad_conv,
        grad_dt_t.T,
        grad_heads,
        gain,
        cls_t.T,
        loss.reshape(1),
    )


def solution(mesh):
    rows = P(("grp", "seq"), None)
    placed = (rows,) + (P(),) * 9 + (rows, P(), rows, P(("grp", "seq")), P(("grp", "seq")))
    part = P("grp", None)
    return jax.shard_map(
        per_device,
        mesh=mesh,
        in_specs=placed,
        out_specs=(rows, rows, rows, part, part, part, P("grp"), part, P("grp")),
        check_vma=False,
    )
```

```python
import functools

import jax
import jax.numpy as jnp
from jax import lax
from jax.experimental import pallas as pl
from jax.experimental.pallas import tpu as pltpu
from jax.sharding import PartitionSpec as P

HEADS = 12
HDIM = 64
STATE = 128
LABELS = 16
LANES = 128
HALO = 8
CHUNK = 64
TAGS = 48
FACTS = 40
EPSILON = 1e-05
FAR = -1e30

F32 = jnp.float32
BF16 = jnp.bfloat16


def partner(x, axis, apart):
    return lax.ppermute(x, axis, [(i, i ^ 1 << apart) for i in range(lax.axis_size(axis))])


def passed_along(x, axis, by):
    length = lax.axis_size(axis)
    pairs = [(i, i + by) for i in range(length) if 0 <= i + by < length]
    return lax.ppermute(x, axis, pairs)


def dot(a, b, left=1, right=0):
    return lax.dot_general(a, b, (((left,), (right,)), ((), ())), preferred_element_type=F32)


def pieces(x, count):
    parts = []
    for _ in range(count):
        part = x.astype(BF16)
        parts.append(part)
        x = x - part.astype(F32)
    return parts


def finer(a, x, count, left=1, right=0):
    return sum(dot(a, part, left, right) for part in pieces(x, count))


def iota(shape, axis):
    return lax.broadcasted_iota(jnp.int32, shape, axis)


def spread_heads(x):
    rows = x.shape[0]
    first = iota((rows, LANES), 1) < HDIM
    return jnp.concatenate(
        [
            jnp.where(
                first,
                jnp.broadcast_to(x[:, 2 * pair : 2 * pair + 1], (rows, LANES)),
                jnp.broadcast_to(x[:, 2 * pair + 1 : 2 * pair + 2], (rows, LANES)),
            )
            for pair in range(HEADS // 2)
        ],
        axis=1,
    )


def head_sums(x):
    width = x.shape[1]
    member = (iota((width, LANES), 0) // HDIM == iota((width, LANES), 1)).astype(BF16)
    return sum(dot(part, member) for part in pieces(x, 2))


class Fetched:
    def __init__(self, ref, copy):
        self.ref, self.copy, self.shape = ref, copy, ref.shape

    def ready(self):
        if self.copy is not None:
            self.copy.wait()
            self.copy = None
        return self.ref

    def __getitem__(self, at):
        return self.ready()[at]


class Result:
    def __init__(self, ref, copy):
        self.ref, self.copy, self.shape, self.sent = ref, copy, ref.shape, False

    def __getitem__(self, at):
        return self.ref[at]

    def __setitem__(self, at, value):
        self.ref[at] = value

    def send(self):
        self.copy.start()
        self.sent = True


class Kept:
    def __init__(self, ref):
        self.ref, self.shape = ref, ref.shape

    def __getitem__(self, at):
        return self.ref[at]

    def __setitem__(self, at, value):
        self.ref[at] = value

    def send(self):
        pass


def call(body, outs, *args, scratch=(), scalars=0, fetch=(), leave=(), after=(), wait=(), into=()):
    waits = len(after) + len(wait)
    fetch = sorted(fetch)

    def kernel(*refs):
        refs = list(refs)

        def take(count):
            taken = refs[:count]
            del refs[:count]
            return taken

        inputs = take(len(args))
        take(waits)
        results = take(len(outs))
        places, outputs, extra = take(len(fetch) - len(into)), take(len(leave)), take(len(scratch))
        places = places + results[len(results) - len(into) :]
        arrivals, departures = refs
        for i, (at, place) in enumerate(zip(fetch, places)):
            copy = pltpu.make_async_copy(inputs[at], place, arrivals.at[i])
            copy.start()
            inputs[at] = Fetched(place, copy)
        written = []
        for i, result in enumerate(results):
            if i in leave:
                at = leave.index(i)
                copy = pltpu.make_async_copy(outputs[at], result, departures.at[at])
                written.append(Result(outputs[at], copy))
            else:
                written.append(Kept(result))
        body(*inputs, *written, *extra)
        for at in fetch:
            inputs[at].ready()
        gone = [result for result in written if isinstance(result, Result)]
        for result in gone:
            if not result.sent:
                result.send()
        for result in gone:
            result.copy.wait()

    far, close = pltpu.HBM, pltpu.VMEM
    specs, given = [], []
    for i, arg in enumerate(args):
        if i < scalars:
            specs.append(pl.BlockSpec(memory_space=pltpu.SMEM))
            given.append(arg)
        else:
            space = far if i in fetch else close
            specs.append(pl.BlockSpec(memory_space=space))
            given.append(pltpu.with_memory_space_constraint(arg, space))
    for space, arrays in ((close, after), (far, wait)):
        for arg in arrays:
            specs.append(pl.BlockSpec(memory_space=space))
            given.append(pltpu.with_memory_space_constraint(arg, space))
    return pl.pallas_call(
        kernel,
        out_shape=[(far if i in leave else close)(*out) for i, out in enumerate(outs)],
        in_specs=specs,
        out_specs=[pl.BlockSpec(memory_space=far if i in leave else close) for i in range(len(outs))],
        scratch_shapes=[
            *(pltpu.VMEM(args[i].shape, args[i].dtype) for i in fetch[: len(fetch) - len(into)]),
            *(pltpu.VMEM(*outs[i]) for i in leave),
            *scratch,
            pltpu.SemaphoreType.DMA((max(len(fetch), 1),)),
            pltpu.SemaphoreType.DMA((max(len(leave), 1),)),
        ],
        compiler_params=pltpu.CompilerParams(vmem_limit_bytes=24 * 1024 * 1024),
    )(*given)


def widened(x):
    place = (iota((HEADS, LANES), 0) == iota((HEADS, LANES), 1)).astype(BF16)
    return sum(dot(part, place) for part in pieces(x, 3))


def teacher_kernel(slice_rows, rows, weights, dest, start, size, hidden, w_in, extra, own, *brought):
    count = rows.shape[0]
    row, lane = iota((count, count), 0), iota((count, count), 1)
    named = dest[...].astype(F32)
    facts = jnp.where(
        row == 0, named, jnp.where(row == 1, start[...].astype(F32), size[...].astype(F32))
    ).T
    spans = facts[:, 2:3]
    slot = jnp.sum(
        jnp.where((facts[:, 0:1] == named) & (row < lane), 1.0, 0.0), axis=0, keepdims=True
    ).astype(jnp.int32)
    logits = dot(rows[...], weights[...], 1, 1)
    top = jnp.max(logits, axis=1, keepdims=True)
    shifted = logits - top
    logp = shifted - jnp.log(jnp.sum(jnp.exp(shifted), axis=1, keepdims=True))
    prob = jnp.exp(logp)
    label, spot = iota((LABELS, LANES), 0), iota((LABELS, LANES), 1)
    total = jnp.zeros((STATE, LANES), F32)
    for group in range(2):
        base = TAGS + group * FACTS
        inside = sum(
            dot(part, (spot == label + base + i * LABELS).astype(BF16))
            for i, part in enumerate(pieces(prob, 2))
        )
        spare = base + 2 * LABELS
        inside = jnp.where(lane == spare, facts[:, 1:2], inside)
        inside = jnp.where(lane == spare + 1, spans, inside)
        inside = jnp.where(lane == spare + 2, 1.0, inside)
        where_to = dest[...] * slice_rows + slot - group * slice_rows
        fits = (slot >= group * slice_rows) & (slot < (group + 1) * slice_rows)
        chosen = (iota((STATE, count), 0) == jnp.where(fits, where_to, -1)).astype(F32)
        total = total + dot(chosen.astype(BF16), inside.astype(BF16))
    extra[...] = total.astype(BF16)
    gained = jnp.sum(prob * logp, axis=1, keepdims=True) * spans
    own[...] = jnp.where(lane[0:1] == 0, jnp.sum(gained, axis=0, keepdims=True), 0.0)


def target_kernel(arrived, w_cls, w_out, target, joined_high, joined_low):
    length = target.shape[0]
    width = HEADS * HDIM
    count, rows = arrived.shape[0], arrived.shape[1]
    facts = arrived[:, :, width:].astype(F32).reshape(count * rows, LANES).astype(BF16)
    facts_f = facts.astype(F32)
    position = iota((count * rows, length), 1).astype(F32)
    total = jnp.zeros((length, LANES), F32)
    for group in range(2):
        base = TAGS + group * FACTS
        spare = base + 2 * LABELS
        start = facts_f[:, spare : spare + 1]
        stop = start + facts_f[:, spare + 1 : spare + 2]
        covered = jnp.where((position >= start) & (position < stop), 1.0, 0.0).astype(BF16)
        sums = dot(covered, facts, 0, 0)
        lane = iota(sums.shape, 1)
        high = pltpu.roll(sums, LANES - base, 1)
        low = pltpu.roll(sums, LANES - base - LABELS, 1)
        cover = pltpu.roll(sums, (LABELS - spare - 2) % LANES, 1)
        total = total + jnp.where(lane < LABELS, high + low, jnp.where(lane == LABELS, cover, 0.0))
    target[...] = total
    place = (iota((LANES, LABELS), 0) == iota((LANES, LABELS), 1)).astype(BF16)
    joined = dot(dot(place, w_cls[...]).astype(BF16), w_out[...], 1, 1)
    joined_high[...], joined_low[...] = pieces(joined, 2)


def convolved(raw, conv_w, length):
    conv = conv_w[0:1, :] * raw[0:length, :]
    for tap in range(1, conv_w.shape[0]):
        conv = conv + conv_w[tap : tap + 1, :] * raw[pl.ds(tap, length), :]
    return conv


def front_kernel(
    edge, hidden, w_dt, dt_bias, a_log, w_in, conv_w, extra,
    message, mixed_o, raw_o, step_o, run_o, run_t, raw,
):
    length = hidden.shape[0]
    weights = w_in[...]
    raw_o[0:length, :] = dot(hidden[...], weights).astype(BF16)
    raw_o[length:, :] = dot(edge[...], weights).astype(BF16)
    raw_o.send()
    wide = (iota((LANES, HEADS), 0) == iota((LANES, HEADS), 1)).astype(BF16)
    w_dt_wide = dot(wide, w_dt[...]).astype(BF16)
    before = dot(hidden[...], w_dt_wide, 1, 1) + widened(dt_bias[...])
    step = jnp.maximum(before, 0.0) + jnp.log1p(jnp.exp(-jnp.abs(before)))
    step = jnp.where(iota((length, LANES), 1) < HEADS, step, 0.0)
    log_decay = -step * jnp.exp(widened(a_log[...]))
    later = (iota((length, length), 1) >= iota((length, length), 0)).astype(BF16)
    run = finer(later, log_decay, 3)
    step_o[:, 0:LANES] = step
    step_o[:, LANES:] = before
    run_o[...] = run
    run_t[...] = run.T
    for result in (step_o, run_o, run_t):
        result.send()
    raw[...] = raw_o[...].astype(F32)
    conv = convolved(raw, conv_w, length)
    mixed = (conv / (1.0 + jnp.exp(-conv))).astype(BF16)
    mixed_o[...] = mixed
    mixed_o.send()
    width = HEADS * HDIM
    total = run[0:1, :]
    weighted = mixed[:, :width].astype(F32) * spread_heads(step * jnp.exp(total - run))
    state = dot(mixed[:, width : width + STATE], weighted.astype(BF16), 0, 0)
    message[:, :width] = state.astype(BF16)
    high, middle, low = (part.astype(F32) for part in pieces(total, 3))
    tags = high + pltpu.roll(middle, 16, 1) + pltpu.roll(low, 32, 1)
    message[:, width:] = (extra[...].astype(F32) + tags).astype(BF16)


def decay_blocks(run, run_t, head, half):
    top = run[0:half, head : head + 1] - run_t[head : head + 1, :]
    low = run[half:, head : head + 1] - run_t[head : head + 1, half:]
    top_seen = iota(top.shape, 1) >= iota(top.shape, 0)
    low_seen = iota(low.shape, 1) >= iota(low.shape, 0)
    return jnp.exp(jnp.where(top_seen, top, FAR)), jnp.exp(jnp.where(low_seen, low, FAR))


def local_kernel(
    blocks, place, mixed, step, run, run_t, edge, d_skip, raw_b, conv_w, hidden,
    local, slope, tail_values, tail_steps, tail_weighted, keep_t, send_t, raw, turned,
):
    length = mixed.shape[0]
    half = length // 2
    width = HEADS * HDIM
    in_map = mixed[:, width : width + STATE]
    out_map = mixed[:, width + STATE :]
    top_scores = dot(out_map[0:half], in_map, 1, 1)
    low_scores = dot(out_map[half:], in_map[half:], 1, 1)
    weighted = (mixed[:, :width].astype(F32) * spread_heads(step[:, 0:LANES])).astype(BF16)
    first = iota((half, LANES), 1) < HDIM
    for pair in range(HEADS // 2):
        lanes = slice(pair * LANES, (pair + 1) * LANES)
        own = weighted[:, lanes]
        tops, lows = [], []
        for head in (2 * pair, 2 * pair + 1):
            top, low = decay_blocks(run, run_t, head, half)
            tops.append(dot((top * top_scores).astype(BF16), own))
            lows.append(dot((low * low_scores).astype(BF16), own[half:]))
        local[0:half, lanes] = jnp.where(first, tops[0], tops[1])
        local[half:, lanes] = jnp.where(first, lows[0], lows[1])
    local[...] = local[...] + spread_heads(d_skip[...]) * mixed[:, :width].astype(F32)
    turned[:, 0:length] = hidden[...].astype(F32).T
    rest = jnp.zeros((LANES - HALO, turned.shape[0]), F32)
    turned[:, length:] = jnp.concatenate([edge[...].astype(F32), rest], axis=0).T
    halves(turned, keep_t, send_t, place[0] % 2, blocks)
    keep_t.send()
    send_t.send()
    tail = spread_heads(jnp.exp(run[0:1, :] - run[...]))
    steps = spread_heads(step[:, 0:LANES])
    reaching = tail * mixed[:, :width].astype(F32)
    tail_values[...] = reaching
    tail_values.send()
    tail_steps[...] = tail * steps
    tail_steps.send()
    tail_weighted[...] = (reaching * steps).astype(BF16)
    tail_weighted.send()
    raw[...] = raw_b[...].astype(F32)
    inner = convolved(raw, conv_w, length)
    gate = 1.0 / (1.0 + jnp.exp(-inner))
    slope[...] = gate * (1.0 + inner * (1.0 - gate))


def states_kernel(arrived, onward, decay):
    count = arrived.shape[0]
    width = HEADS * HDIM
    rows = arrived.shape[1]
    keep = iota((rows, LANES), 1) < HEADS
    state = jnp.zeros((rows, width), F32)
    for source in range(count - 1, -1, -1):
        onward[source] = state.astype(BF16)
        tags = arrived[source, :, width:].astype(F32)
        total = tags + pltpu.roll(tags, LANES - 16, 1) + pltpu.roll(tags, LANES - 32, 1)
        factor = jnp.exp(jnp.where(keep, total, 0.0))
        decay[source] = factor
        state = arrived[source, :, :width].astype(F32) + spread_heads(factor) * state


def state_grads_kernel(arrived, decay, early, onward):
    count, rows, width = arrived.shape
    state = jnp.zeros(arrived.shape[1:], F32)
    for source in range(count):
        onward[source, :, :width] = state.astype(BF16)
        onward[source, :, width:] = early[source * rows : (source + 1) * rows, :].astype(BF16)
        state = arrived[source].astype(F32) + spread_heads(decay[source]) * state


def middle_kernel(
    state, mixed, run, local, gains, high, low, target,
    back_state, grad_scanned, normed_o, logits_o, run_grad, small,
):
    length = mixed.shape[0]
    width = HEADS * HDIM
    values = mixed[:, :width].astype(F32)
    out_map = mixed[:, width + STATE :]
    reach = spread_heads(jnp.exp(run[...]))
    carried = dot(out_map, state[...]) * reach
    scanned = local[...] + carried
    scale = lax.rsqrt(jnp.mean(scanned * scanned, axis=1, keepdims=True) + EPSILON)
    plain = scanned * scale
    gain = gains[...].reshape(1, width)
    normed = (plain * gain).astype(BF16)
    normed_o[...] = normed
    normed_o.send()
    label = iota((length, LANES), 1) < LABELS
    logits = jnp.where(label, dot(normed, high[...], 1, 1) + dot(normed, low[...], 1, 1), FAR)
    shifted = logits - jnp.max(logits, axis=1, keepdims=True)
    raised = jnp.exp(shifted)
    whole = jnp.sum(raised, axis=1, keepdims=True)
    logp = shifted - jnp.log(whole)
    wanted = target[...]
    cover = wanted[:, LABELS : LABELS + 1]
    back_logits = jnp.where(label, cover * (raised / whole) - wanted, 0.0)
    logits_o[...] = back_logits
    logits_o.send()
    lost = jnp.sum(jnp.where(label, wanted * logp, 0.0), axis=0, keepdims=True)
    back_high, back_low = pieces(back_logits, 2)
    back_normed = dot(back_high, high[...]) + dot(back_low, high[...]) + dot(back_high, low[...])
    back_plain = back_normed * gain
    along = jnp.mean(back_plain * plain, axis=1, keepdims=True)
    back = scale * (back_plain - plain * along)
    grad_scanned[...] = back
    back_state[...] = dot(out_map, (back * reach).astype(BF16), 0, 0).astype(BF16)
    back_state.send()
    small[0:1, :] = jnp.sum(back_normed * plain, axis=0, keepdims=True)
    small[1:2, :] = jnp.sum(back * values, axis=0, keepdims=True)
    small[2:3, :] = jnp.zeros((1, width), F32)
    small[2:3, 0:LANES] = lost
    small[3:, :] = jnp.zeros((5, width), F32)
    small.send()
    run_grad[...] = head_sums(back * carried)


def halves(full, keep, send, odd, blocks):
    size = full.shape[0] // blocks
    for side in (0, 1):

        @pl.when(odd == side)
        def _():
            for block in range(blocks // 2):
                at = slice(block * size, (block + 1) * size)
                mine = (2 * block + side) * size
                other = (2 * block + 1 - side) * size
                keep[at, :] = full[mine : mine + size, :].astype(BF16)
                send[at, :] = full[other : other + size, :].astype(BF16)


def local_back_kernel(
    mixed, step, run, grad_scanned, d_skip, state, carried_grad, normed, back_logits, small,
    values_grad, maps, run_grad, step_grad, early, weighted_grad,
):
    length = mixed.shape[0]
    half = length // 2
    width = HEADS * HDIM
    in_map = mixed[:, width : width + STATE]
    out_map = mixed[:, width + STATE :]
    top_scores = dot(out_map[0:half], in_map, 1, 1)
    low_scores = dot(out_map[half:], in_map[half:], 1, 1)
    values = mixed[:, :width].astype(F32)
    steps = spread_heads(step[:, 0:LANES])
    weighted = (values * steps).astype(BF16)
    run_t = run[...].T
    lane = iota((length, LANES), 1)
    back_top = jnp.zeros((half, length), F32)
    back_low = jnp.zeros((half, half), F32)
    rows_top = jnp.zeros((half, LANES), F32)
    rows_low = jnp.zeros((half, LANES), F32)
    columns = jnp.zeros((length, LANES), F32)
    columns_low = jnp.zeros((half, LANES), F32)
    for pair in range(HEADS // 2):
        lanes = slice(pair * LANES, (pair + 1) * LANES)
        own = weighted[:, lanes]
        back_f = grad_scanned[:, lanes]
        back = back_f.astype(BF16)
        tops, lows = [], []
        for side in (0, 1):
            head = 2 * pair + side
            top, low = decay_blocks(run, run_t, head, half)
            mine = jnp.where((lane >= HDIM) == (side == 1), back_f, 0.0).astype(BF16)
            mix_top = (top * top_scores).astype(BF16)
            mix_low = (low * low_scores).astype(BF16)
            tops.append(dot(mix_top, back[0:half], 0, 0))
            lows.append(dot(mix_low, back[half:], 0, 0))
            grad_top = top * dot(mine[0:half], own, 1, 1)
            grad_low = low * dot(mine[half:], own[half:], 1, 1)
            back_top = back_top + grad_top
            back_low = back_low + grad_low
            part_top = (grad_top * top_scores).astype(BF16)
            part_low = (grad_low * low_scores).astype(BF16)
            marker = (lane == head).astype(F32).astype(BF16)
            rows_top = rows_top + dot(part_top, marker)
            rows_low = rows_low + dot(part_low, marker[half:])
            columns = columns + dot(part_top, marker[0:half], 0, 0)
            columns_low = columns_low + dot(part_low, marker[half:], 0, 0)
        weighted_grad[0:half, lanes] = jnp.where(lane[0:half] < HDIM, tops[0][0:half], tops[1][0:half])
        weighted_grad[half:, lanes] = jnp.where(
            lane[half:] < HDIM, tops[0][half:] + lows[0], tops[1][half:] + lows[1]
        )
    back_top = back_top.astype(BF16)
    back_low = back_low.astype(BF16)
    values_grad[...] = weighted_grad[...] * steps + spread_heads(d_skip[...]) * grad_scanned[...]
    values_grad.send()
    step_grad[...] = head_sums(weighted_grad[...] * values)
    scaled = (grad_scanned[...] * spread_heads(jnp.exp(run[...]))).astype(BF16)
    from_state = dot(scaled, state[...], 1, 1)
    maps[0:half, STATE:] = dot(back_top, in_map) + from_state[0:half]
    maps[half:, STATE:] = dot(back_low, in_map[half:]) + from_state[half:]
    in_grad = dot(back_top, out_map[0:half], 0, 0)
    maps[0:half, 0:STATE] = in_grad[0:half]
    maps[half:, 0:STATE] = in_grad[half:] + dot(back_low, out_map[half:], 0, 0)
    run_grad[0:half, :] = carried_grad[0:half, :] + rows_top - columns[0:half]
    run_grad[half:, :] = carried_grad[half:, :] + rows_low - columns[half:] - columns_low
    product = sum(dot(part, normed[...], 0, 0) for part in pieces(back_logits[...], 2))[0:LABELS]
    count = width // LANES
    early[count * LABELS :, :] = jnp.zeros((early.shape[0] - count * LABELS, LANES), F32)
    for block in range(count):
        lanes = slice(block * LANES, (block + 1) * LANES)
        early[block * LABELS : (block + 1) * LABELS, :] = product[:, lanes]
        at = count * LABELS + block
        early[at : at + 1, :] = small[0:1, lanes]


def last_kernel(
    blocks, place, state_grad, run, mixed, step, state, run_grad,
    tail_values, tail_weighted, step_local, a_log, conv_w, tail_steps, values_local, maps, slope, send_t,
    keep_t, hidden, raw_b, small, own,
    keep, send, rim, back_raw_o, step_grad_o, late, padded, raw, back_raw_b,
):
    length = mixed.shape[0]
    taps = conv_w.shape[0]
    width = HEADS * HDIM
    total = run[0:1, :]
    in_map = mixed[:, width : width + STATE]
    incoming = state_grad[:, :width]
    reached = dot(in_map, incoming)
    product = jnp.sum(incoming.astype(F32) * state[...].astype(F32), axis=0, keepdims=True)
    total_grad = jnp.exp(total) * head_sums(jnp.broadcast_to(product, (8, width)))[0:1]
    row, column = iota((length, length), 0), iota((length, length), 1)
    decay_grad = finer((column <= row).astype(BF16), run_grad[...], 3) + total_grad
    padded[0:HALO, :] = jnp.zeros((HALO, padded.shape[1]), F32)
    padded[HALO + length :, :] = jnp.zeros((HALO, padded.shape[1]), F32)
    reaching = head_sums(reached * tail_values[...])
    ended = reaching * step[:, 0:LANES]
    in_grad = dot(tail_weighted[...], incoming, 1, 1)
    decay_grad = decay_grad + finer((column > row).astype(BF16), ended, 3)
    rate = jnp.exp(widened(a_log[...]))
    step_grad = step_local[...] + reaching - rate * decay_grad
    before = step[:, LANES:]
    step_grad = jnp.where(
        iota((length, LANES), 1) < HEADS, step_grad / (1.0 + jnp.exp(-before)), 0.0
    )
    step_grad_b = step_grad.astype(BF16)
    step_grad_o[...] = step_grad_b
    middle = slice(HALO, HALO + length)
    for at in range(0, length, CHUNK):
        rows, moved = slice(at, at + CHUNK), slice(HALO + at, HALO + at + CHUNK)
        padded[moved, 0:width] = (
            values_local[rows, :] + reached[rows, :] * tail_steps[rows, :]
        ) * slope[rows, 0:width]
        padded[moved, width : width + STATE] = (maps[rows, 0:STATE] + in_grad[rows, :]) * slope[
            rows, width : width + STATE
        ]
        padded[moved, width + STATE :] = maps[rows, STATE:] * slope[rows, width + STATE :]
    rim[...] = padded[length : length + HALO, :]
    rim.send()
    for at in range(0, length + HALO, CHUNK):
        size = min(CHUNK, length + HALO - at)
        part = conv_w[0:1, :] * padded[pl.ds(HALO + at, size), :]
        for tap in range(1, taps):
            part = part + conv_w[tap : tap + 1, :] * padded[pl.ds(HALO + at - tap, size), :]
        if at < length:
            back_raw_o[at : at + size, :] = part
        back_raw_b[at : at + size, :] = part.astype(BF16)
    back_raw_b[length + HALO :, :] = jnp.zeros((LANES - HALO, padded.shape[1]), BF16)
    send[...] = dot(send_t[...], back_raw_b[...]).astype(BF16)
    send.send()
    keep[...] = dot(keep_t[...], back_raw_b[...]).astype(BF16)
    back_raw_o.send()
    raw[...] = raw_b[...].astype(F32)
    spare = late.shape[0] - taps
    conv_sums = [jnp.zeros((1, padded.shape[1]), F32)] * taps
    for at in range(0, length, CHUNK):
        back_conv = padded[HALO + at : HALO + at + CHUNK, :]
        for tap in range(taps):
            conv_sums[tap] = conv_sums[tap] + jnp.sum(
                back_conv * raw[pl.ds(at + tap, CHUNK), :], axis=0, keepdims=True
            )
    for tap in range(taps):
        late[spare + tap : spare + tap + 1, :] = conv_sums[tap]
    late[0:HEADS, 0:width] = dot(step_grad_b, hidden[...], 0, 0)[0:HEADS]
    late[0:HEADS, width:] = jnp.zeros((HEADS, late.shape[1] - width), F32)
    log_decay = -step[:, 0:LANES] * rate
    facts = jnp.sum(step_grad, axis=0, keepdims=True)
    facts = facts + pltpu.roll(jnp.sum(decay_grad * log_decay, axis=0, keepdims=True), 16, 1)
    skips = head_sums(jnp.broadcast_to(small[1:2, :], (8, width)))[0:1]
    lost = jnp.sum(own[...] - small[2:3, 0:LANES], axis=1, keepdims=True)
    lane = iota((1, LANES), 1)
    facts = facts + pltpu.roll(skips, 32, 1) + jnp.where(lane == 48, lost, 0.0)
    late[HEADS - 4 : HEADS - 3, width : width + LANES] = facts
    shares = state_grad[:, width:].astype(F32)
    rows = shares.shape[0] // blocks
    share = sum(shares[source * rows : (source + 1) * rows] for source in range(blocks))
    for side in (0, 1):

        @pl.when(place[0] % 2 == side)
        def _():
            late[0:rows, width + side * LANES : width + (side + 1) * LANES] = share


def hidden_kernel(rim, back_raw, conv_w, step_grad, w_dt, w_in, out, joined, edge):
    taps = conv_w.shape[0]
    joined[...] = back_raw[...]
    edge[0:HALO, :] = rim[...]
    edge[HALO:, :] = jnp.zeros((HALO, edge.shape[1]), F32)
    head = joined[0:HALO, :]
    for tap in range(taps):
        head = head + conv_w[tap : tap + 1, :] * edge[pl.ds(HALO - tap, HALO), :]
    joined[0:HALO, :] = head
    wide = (iota((LANES, HEADS), 0) == iota((LANES, HEADS), 1)).astype(BF16)
    w_dt_wide = dot(wide, w_dt[...]).astype(BF16)
    out[...] = (
        dot(joined[...].astype(BF16), w_in[...], 1, 1) + dot(step_grad[...], w_dt_wide)
    ).astype(BF16)


def swapped(x, axis="seq"):
    return lax.all_to_all(x, axis, split_axis=0, concat_axis=0, tiled=True)


def joint_kernel(blocks, keep, received, late, late_received, both):
    size = keep.shape[0] // blocks
    rows, width = late.shape[0], HEADS * HDIM
    sums = late[...] + late_received[...]
    facts = sums[:, width : width + LANES]
    rest = pltpu.roll(facts - facts.astype(BF16).astype(F32), 1, 0)
    row = iota(facts.shape, 0)
    facts = jnp.where(row == HEADS - 3, rest, facts)
    sums = jnp.concatenate([sums[:, :width], facts, sums[:, width + LANES :]], axis=1).astype(BF16)
    for block in range(blocks):
        base, at = block * (size + rows), slice(block * size, (block + 1) * size)
        both[base : base + size, :] = (
            keep[at, :].astype(F32) + received[at, :].astype(F32)
        ).astype(BF16)
        both[base + size : base + size + rows, :] = sums


def joint_sums_kernel(
    share, rows_in_all, place, parts, w_out, w_cls,
    grad_w_in, grad_conv, grad_dt_t, grad_heads, gain, cls_t, loss, grad_w_out, early, product,
):
    total = parts[0].astype(F32)
    for chip in range(1, parts.shape[0]):
        total = total + parts[chip].astype(F32)
    size, taps, width = grad_w_in.shape[0], grad_conv.shape[0], HEADS * HDIM
    grad_w_in[...] = total[0:size]
    grad_conv[...] = total[size + HEADS : size + HEADS + taps]
    grad_dt_t[...] = total[size : size + HEADS, 0:width]
    at = size + HEADS - 4
    facts = total[at : at + 1, width : width + LANES] + total[at + 1 : at + 2, width : width + LANES]
    for row in range(3):
        moved = pltpu.roll(facts, (LANES - 16 * row) % LANES, 1) if row else facts
        grad_heads[row : row + 1, :] = moved[:, 0:HEADS]
    loss[...] = pltpu.roll(facts, LANES - 48, 1)[:, 0:1] / rows_in_all
    for chip in range(parts.shape[0]):
        for side in (0, 1):
            base = (2 * chip + side) * share
            lanes = slice(width + side * LANES, width + (side + 1) * LANES)
            early[base : base + share, :] = parts[chip][size : size + share, lanes].astype(F32)
    count = width // LANES
    for block in range(count):
        lanes = slice(block * LANES, (block + 1) * LANES)
        product[:, lanes] = early[block * LABELS : (block + 1) * LABELS, :].astype(BF16)
        gain[lanes] = early[count * LABELS + block, :]
    cls_t[...] = dot(product[...], w_out[...])
    own = (iota((size, width), 1) == iota((size, width), 0) + place[0] * size).astype(F32)
    rows = dot(own.astype(BF16), product[...], 1, 1).astype(BF16)
    grad_w_out[...] = dot(rows, w_cls[...])


def exchanged(both, devices):
    groups = [[i for i in range(devices) if i % 2 == side] for side in (0, 1)]
    parts = lax.all_to_all(
        both, "seq", split_axis=0, concat_axis=0, axis_index_groups=groups, tiled=True
    )
    return parts.reshape(devices // 2, -1, both.shape[1])


def per_device(
    hidden_in, w_in, w_dt, dt_bias, a_log, conv_w, d_skip, norm_gain, w_out, w_cls,
    teacher_rows, w_teacher, row_dest, row_start, row_len,
):
    devices = lax.axis_size("seq")
    length = hidden_in.shape[0]
    width = HEADS * HDIM
    channels = w_in.shape[1]
    slice_rows = STATE // devices
    row_count = teacher_rows.shape[0]
    place = lax.axis_index("seq").astype(jnp.int32).reshape(1)

    edge = passed_along(hidden_in[:HALO], "seq", -1)
    extra, own, hidden_near, w_in_near = call(
        functools.partial(teacher_kernel, slice_rows),
        [
            ((STATE, LANES), BF16),
            ((1, LANES), F32),
            (hidden_in.shape, BF16),
            (w_in.shape, BF16),
        ],
        teacher_rows, w_teacher.T, row_dest.reshape(1, row_count),
        row_start.reshape(1, row_count), row_len.reshape(1, row_count), hidden_in, w_in,
        fetch=range(7), leave=(1,), into=(5, 6),
    )
    w_dt_t = w_dt.T
    a_log_row = a_log.reshape(1, HEADS)
    skip_row = d_skip.reshape(1, HEADS)
    message, mixed, raw, step, run, run_t = call(
        front_kernel,
        [
            ((STATE, width + LANES), BF16),
            ((length, channels), BF16),
            ((length + HALO, channels), BF16),
            ((length, 2 * LANES), F32),
            ((length, LANES), F32),
            ((LANES, length), F32),
        ],
        edge, hidden_near, w_dt_t, dt_bias.reshape(1, HEADS), a_log_row, w_in_near, conv_w, extra,
        scratch=[pltpu.VMEM((length + HALO, channels), F32)], fetch=(2, 3, 4, 6), leave=(0, 2),
    )
    arrived = swapped(message).reshape(devices, slice_rows, width + LANES)
    local, slope, tail_values, tail_steps, tail_weighted, keep_t, send_t = call(
        functools.partial(local_kernel, devices),
        [
            ((length, width), F32),
            ((length, channels), F32),
            ((length, width), F32),
            ((length, width), F32),
            ((length, width), BF16),
            ((width // 2, length + LANES), BF16),
            ((width // 2, length + LANES), BF16),
        ],
        place, mixed, step, run, run_t, edge, skip_row, raw, conv_w, hidden_in,
        scratch=[
            pltpu.VMEM((length + HALO, channels), F32),
            pltpu.VMEM((width, length + LANES), F32),
        ],
        scalars=1, fetch=(6, 7, 8, 9), leave=(1, 2, 3, 4, 5, 6),
    )
    onward, decay = call(
        states_kernel,
        [((devices, slice_rows, width), BF16), ((devices, slice_rows, LANES), F32)],
        arrived,
        leave=(0,),
        after=[local],
    )
    state = swapped(onward.reshape(STATE, width))
    target, labels_high, labels_low = call(
        target_kernel,
        [((length, LANES), F32), ((LANES, width), BF16), ((LANES, width), BF16)],
        arrived, w_cls.T, w_out,
        fetch=(1, 2), leave=(0,),
    )

    back_state, grad_scanned, normed, back_logits, carried_grad, small = call(
        middle_kernel,
        [
            ((STATE, width), BF16),
            ((length, width), F32),
            ((length, width), BF16),
            ((length, LANES), F32),
            ((length, LANES), F32),
            ((8, width), F32),
        ],
        state, mixed, run, local, norm_gain, labels_high, labels_low, target,
        fetch=(4, 7), leave=(0, 2, 3, 5),
    )
    back_arrived = swapped(back_state).reshape(devices, slice_rows, width)
    values_local, maps, run_grad, step_local, early = call(
        local_back_kernel,
        [
            ((length, width), F32),
            ((length, 2 * STATE), F32),
            ((length, LANES), F32),
            ((length, LANES), F32),
            ((STATE, LANES), F32),
        ],
        mixed, step, run, grad_scanned, skip_row, state, carried_grad, normed, back_logits, small,
        scratch=[pltpu.VMEM((length, width), F32)], fetch=(4, 7, 8, 9), leave=(1, 3),
    )
    (back_onward,) = call(
        state_grads_kernel,
        [((devices, slice_rows, width + LANES), BF16)],
        back_arrived, decay, early,
        leave=(0,),
    )
    state_grad = swapped(back_onward.reshape(STATE, width + LANES))

    keep_in, send_in, rim, back_raw, step_grad, late = call(
        functools.partial(last_kernel, devices),
        [
            ((width // 2, channels), BF16),
            ((width // 2, channels), BF16),
            ((HALO, channels), F32),
            ((length, channels), F32),
            ((length, LANES), BF16),
            ((HEADS + conv_w.shape[0], channels), F32),
        ],
        place, state_grad, run, mixed, step, state, run_grad,
        tail_values, tail_weighted, step_local, a_log_row, conv_w, tail_steps, values_local, maps, slope,
        send_t, keep_t, hidden_in, raw, small, own,
        scratch=[
            pltpu.VMEM((length + 2 * HALO, channels), F32),
            pltpu.VMEM((length + HALO, channels), F32),
            pltpu.VMEM((length + LANES, channels), BF16),
        ],
        scalars=1, fetch=(7, 8, 9, 10, 11, 12, 14, 15, 16, 17, 18, 19, 20, 21), leave=(1, 2, 3, 4),
    )
    chips = devices // 2
    (both_in,) = call(
        functools.partial(joint_kernel, chips),
        [((width // 2 + chips * late.shape[0], channels), BF16)],
        keep_in, partner(send_in, "seq", 0), late, partner(late, "seq", 0),
        leave=(0,),
    )
    parts = exchanged(both_in, devices)
    (grad_hidden,) = call(
        hidden_kernel,
        [((length, w_in.shape[0]), BF16)],
        passed_along(rim, "seq", 1), back_raw, conv_w, step_grad, w_dt_t, w_in,
        scratch=[pltpu.VMEM((length, channels), F32), pltpu.VMEM((2 * HALO, channels), F32)],
        fetch=range(1, 6), leave=(0,),
    )
    grad_w_in, grad_conv, grad_dt_t, grad_heads, gain, cls_t, loss, grad_w_out = call(
        functools.partial(joint_sums_kernel, slice_rows, float(row_count * devices)),
        [
            ((width // devices, channels), F32),
            (conv_w.shape, F32),
            ((HEADS, width), F32),
            ((3, HEADS), F32),
            ((width,), F32),
            ((LABELS, width), F32),
            ((1, 1), F32),
            ((width // devices, width), F32),
        ],
        place, parts, w_out, w_cls.T,
        scratch=[pltpu.VMEM((STATE, LANES), F32), pltpu.VMEM((LABELS, width), BF16)],
        scalars=1, leave=range(8),
    )
    return (
        grad_hidden,
        grad_w_in,
        grad_w_out,
        grad_conv,
        grad_dt_t.T,
        grad_heads,
        gain,
        cls_t.T,
        loss.reshape(1),
    )


def solution(mesh):
    rows = P(("grp", "seq"), None)
    placed = (rows,) + (P(),) * 9 + (rows, P(), rows, P(("grp", "seq")), P(("grp", "seq")))
    part = P("grp", None)
    return jax.shard_map(
        per_device,
        mesh=mesh,
        in_specs=placed,
        out_specs=(rows, rows, rows, part, part, part, P("grp"), part, P("grp")),
        check_vma=False,
    )
```
